32 devices in a mesh: row: 16 (over z, y, x), col: 2 (over core).
Axes of the slice: x: 2, y: 2, z: 4, core: 2. Of those that a mesh axis runs over, the one named last changes fastest.
Arguments:
- descriptors: bfloat16 [4096, 20480], P('row', 'col')
- block_mask: int32 [32, 160], P('row', 'col'), may hold values 0 or 1
- config_of: int32 [4096], P('row'), may hold values from 0 to 1023, as said below
Outputs:
- gram: float32 [384, 20480], P('row', 'col')
The draws below stay inside these ranges and needn't reach their ends.
Inputs may be any that keep to these rules, and one draw needn't show every extreme that they name: `config_of`: each source device's 256 environments name every owner index of row equally often, 256 // 16 times.
All inputs are finite; a program needn't handle non-finite values. No bound on the sum of `block_mask` on one device may be relied on, other than what follows from the above.
Results may differ from the reference program's by a relative error of at most 0.0024.
Values may be sent and summed in bfloat16 or wider, within the bound.
A program may use at most 64 MiB of HBM per device.

```python
import math
import jax
import jax.numpy as jnp
from jax import lax

COLS = 20480
BLOCK = 128
PW = 384
ROW_DEV = 256
CONF_DEV = 64
ROWS = 4096
N_ROW = 16
N_COL = 2


def draw_config_of(key, part):
    devices = ROWS // ROW_DEV
    base = jnp.repeat(jnp.arange(devices, dtype=jnp.int32), ROW_DEV // devices)
    keys = jax.random.split(jax.random.fold_in(key, 1), devices)
    slabs = jax.vmap(lambda k: jax.random.permutation(k, base))(keys).reshape(ROWS)
    local = jax.random.randint(jax.random.fold_in(key, 2), (ROWS,), 0, CONF_DEV, dtype=jnp.int32)
    return slabs * CONF_DEV + local


def draw_descriptors(key, part):
    k_vals = jax.random.fold_in(key, 11)
    k_cols = jax.random.fold_in(key, 12)
    column = jnp.exp(jax.random.uniform(k_cols, (COLS,), jnp.float32, math.log(0.3), math.log(3.0)))
    values = jax.random.normal(k_vals, (ROWS, COLS), jnp.float32)
    return (values * column[None, :]).astype(jnp.bfloat16)


def set_ends(result, key, least, high):
    longest = result.shape.index(max(result.shape))
    spots = []
    for shift in (0, 1):
        where = [jax.random.randint(jax.random.fold_in(key, axis), (), 0, length) for axis, length in enumerate(result.shape)]
        where[longest] = (where[longest] + shift) % result.shape[longest]
        spots.append(tuple(where))
    return result.at[spots[0]].set(least).at[spots[1]].set(high)


def setup_inputs(seed: int = 0) -> dict:
    arg_keys = jax.random.split(jax.random.key(seed), 4)
    descriptors = draw_descriptors(jax.random.fold_in(arg_keys[3], 71), 0)
    block_mask = set_ends((jax.random.randint(arg_keys[1], (ROWS // BLOCK, COLS // BLOCK), 0, 4) < 3).astype(jnp.int32), jax.random.fold_in(arg_keys[1], 1), 0, 1)
    config_of = draw_config_of(jax.random.fold_in(arg_keys[3], 71), 0)
    return dict(descriptors=descriptors, block_mask=block_mask, config_of=config_of)


def reference(descriptors, block_mask, config_of):
    width = COLS // N_COL
    part = PW // N_COL
    configs = CONF_DEV * N_ROW
    counts = jax.ops.segment_sum(jnp.ones((ROWS,), jnp.float32), config_of, configs)
    row_mask = jnp.repeat(block_mask, BLOCK, axis=0).astype(jnp.bfloat16)

    def center(group):
        span = lax.dynamic_slice_in_dim(descriptors, group * width, width, 1)
        marks = lax.dynamic_slice_in_dim(row_mask, group * (width // BLOCK), width // BLOCK, 1)
        masked = (span.reshape(ROWS, width // BLOCK, BLOCK) * marks[:, :, None]).reshape(ROWS, width)
        sums = jax.ops.segment_sum(masked.astype(jnp.float32), config_of, configs)
        means = sums / jnp.maximum(counts, 1.0)[:, None]
        return (masked.astype(jnp.float32) - means[config_of]).astype(jnp.bfloat16)

    groups = jnp.arange(N_COL, dtype=jnp.int32)
    pieces = lax.map(lambda g: center(g)[:, :part], groups)
    panel = jnp.moveaxis(pieces, 0, 1).reshape(ROWS, PW)

    def gram_group(group):
        return jnp.dot(panel.T, center(group), preferred_element_type=jnp.float32) * (1.0 / ROWS)

    grams = lax.map(gram_group, groups)
    return jnp.moveaxis(grams, 0, 1).reshape(PW, COLS)
```

```python
import functools

import jax
import jax.numpy as jnp
from jax import lax
from jax.experimental import pallas as pl
from jax.experimental.pallas import tpu as pltpu
from jax.sharding import PartitionSpec as P

PW = 384
CONF_DEV = 64
BLOCK = 128
G = 4
SLOT = 16
TILES = 10
AHEAD = (1, 3, 5)
F32 = jnp.float32
BF16 = jnp.bfloat16


def remote(src, dst, send, recv, **where):
    return pltpu.make_async_remote_copy(
        src_ref=src, dst_ref=dst, send_sem=send, recv_sem=recv,
        device_id=where, device_id_type=pl.DeviceIdType.MESH,
    )


def kernel(cfg, crow, marks, x, out,
           pext, perm, asend, arec, bsend, brec, xraw, xm, xin, own, mate,
           acc, rsend, rrec, zsend, from_low, from_high, landed, fin,
           a_s, a_r, b_s, b_r, p_s, p_r, c_s, c_r, e_s, e_r, l_s,
           x_s, x_r, r_s, r_r, lo_s, lo_r, hi_s, hi_r, f_s, f_r):
    n, ncol, rows, width, part, wide, bw, tiles, tw, line, pd, pr, zs, factor = cfg
    quarter = width // 4
    r = lax.axis_index("row")
    c = lax.axis_index("col")
    z = r // G
    q = r % G
    bit = (q % 2, q // 2)
    peer = tuple(r + (1 - 2 * bit[h]) * (1 << h) for h in range(2))

    barrier = pltpu.get_barrier_semaphore()

    @pl.loop(1, n)
    def _(k):
        pl.semaphore_signal(barrier, inc=1, device_id={"row": (r + k) % n}, device_id_type=pl.DeviceIdType.MESH)

    @pl.loop(1, ncol)
    def _(k):
        pl.semaphore_signal(barrier, inc=1, device_id={"col": (c + k) % ncol}, device_id_type=pl.DeviceIdType.MESH)

    panel_copy = pltpu.make_async_copy(x.at[:, :wide], pext, l_s.at[0])
    panel_copy.start()

    def start_of(h, b):
        return h * 2 * quarter + b * quarter

    def load(h, b, i):
        cols = pl.ds(pl.multiple_of(start_of(h, b), BLOCK), quarter)
        return pltpu.make_async_copy(x.at[:, cols], xraw.at[:, cols], l_s.at[i])

    away = [load(h, 1 - bit[h], 2 + h) for h in range(2)]
    kept = [load(h, bit[h], 4 + h) for h in range(2)]
    for copy in away + kept:
        copy.start()

    first = lax.broadcasted_iota(jnp.int32, (rows, rows), 0)
    second = lax.broadcasted_iota(jnp.int32, (rows, rows), 1)
    ids_row = jnp.broadcast_to(crow[...], (rows, rows)).astype(F32)
    ids_col = jnp.sum(jnp.where(first == second, ids_row, 0.0), axis=1, keepdims=True).astype(jnp.int32)
    shift = CONF_DEV.bit_length() - 1
    owner = crow[...] >> shift
    before = ((ids_col >> shift) == owner) & (first < second)
    rank = jnp.sum(jnp.where(before, 1.0, 0.0), axis=0, keepdims=True)
    place = owner.astype(F32) * SLOT + rank
    slots = lax.broadcasted_iota(jnp.int32, (n * SLOT, rows), 0).astype(F32)
    perm[...] = jnp.where(slots == place, 1.0, 0.0).astype(BF16)
    label = ((ids_col & (CONF_DEV - 1)) + 1).astype(F32)
    lane = lax.broadcasted_iota(jnp.int32, (BLOCK, BLOCK), 1)
    panel_copy.wait()
    for b in range(rows // BLOCK):
        span = slice(b * BLOCK, (b + 1) * BLOCK)
        for w in range(wide // BLOCK):
            cols = slice(w * BLOCK, (w + 1) * BLOCK)
            keep = marks[b, w].astype(F32) if w * BLOCK < part else 0.0
            block = pext[span, cols].astype(F32) * jnp.broadcast_to(keep, (BLOCK, BLOCK))
            if (w + 1) * BLOCK > part:
                block = jnp.where(lane + w * BLOCK < part, block, jnp.broadcast_to(label[span], (BLOCK, BLOCK)))
            pext[span, cols] = block.astype(BF16)
    asend[...] = jnp.dot(perm[...], pext[...], preferred_element_type=F32).astype(BF16)

    def mask(h, b, t):
        base = start_of(h, b) + t * tw
        for i in range(rows // BLOCK):
            span = slice(i * BLOCK, (i + 1) * BLOCK)
            for w in range(tw // BLOCK):
                keep = marks[i, base // BLOCK + w].astype(F32)
                cols = pl.ds(pl.multiple_of(base + w * BLOCK, BLOCK), BLOCK)
                xm[h, b, t, span, w * BLOCK:(w + 1) * BLOCK] = (
                    xraw[span, cols] * jnp.broadcast_to(keep, (BLOCK, BLOCK)).astype(BF16))

    def mask_away(low, high):
        @pl.loop(low, high)
        def _(t):
            for h in range(2):
                mask(h, 1 - bit[h], t)

    for copy in away:
        copy.wait()
    mask_away(0, AHEAD[0])
    pl.semaphore_wait(barrier, n - 1 + ncol - 1)

    def slot_rows(k):
        return pl.ds(pl.multiple_of(k * SLOT, SLOT), SLOT)

    def to_owner(k):
        to = (r + k) % n
        return remote(asend.at[slot_rows(to), :], arec.at[slot_rows(r), :], a_s.at[k], a_r.at[r], row=to)

    def from_source(k):
        to = (r + k) % n
        return remote(asend.at[slot_rows(to), :], arec.at[slot_rows(to), :], a_s.at[k], a_r.at[to], row=to)

    def to_source(k):
        to = (r + k) % n
        return remote(bsend.at[slot_rows(to), :], brec.at[slot_rows(r), :], b_s.at[k], b_r.at[r], row=to)

    def from_owner(k):
        to = (r + k) % n
        return remote(bsend.at[slot_rows(to), :], brec.at[slot_rows(to), :], b_s.at[k], b_r.at[to], row=to)

    def x_copy(h, t):
        return remote(xm.at[h, 1 - bit[h], t], xin.at[h, t], x_s.at[h, t], x_r.at[h, t], row=peer[h])

    def start_x(t):
        for h in range(2):
            x_copy(h, t).start()

    def p_copy(h):
        return remote(own.at[h, :, c], mate.at[h, :, c], p_s.at[h], p_r.at[h], row=peer[h])

    def c_send(j):
        to = (c + j) % ncol
        return remote(own.at[:, :, c], own.at[:, :, c], c_s.at[j], c_r.at[c], col=to)

    def c_from(j):
        to = (c + j) % ncol
        return remote(own.at[:, :, c], own.at[:, :, to], c_s.at[j], c_r.at[to], col=to)

    def e_send(h, j):
        to = (c + j) % ncol
        return remote(mate.at[h, :, c], mate.at[h, :, c], e_s.at[h, j], e_r.at[h, c], col=to)

    def e_from(h, j):
        to = (c + j) % ncol
        return remote(mate.at[h, :, c], mate.at[h, :, to], e_s.at[h, j], e_r.at[h, to], col=to)

    own_a = pltpu.make_async_copy(asend.at[slot_rows(r), :], arec.at[slot_rows(r), :], l_s.at[0])
    own_a.start()

    @pl.loop(1, n)
    def _(k):
        to_owner(k).start()

    for t in range(AHEAD[0]):
        start_x(t)
    mask_away(AHEAD[0], tiles)

    own_a.wait()

    @pl.loop(1, n)
    def _(k):
        from_source(k).wait_recv()

    arrived = arec[...]
    label = arrived[:, part:part + 1].astype(F32)
    ids = lax.broadcasted_iota(jnp.int32, (n * SLOT, BLOCK), 1).astype(F32) + 1.0
    member = jnp.where((label == ids) & (ids <= CONF_DEV), 1.0, 0.0).astype(BF16)
    same = lax.dot_general(member, member, (((1,), (1,)), ((), ())), preferred_element_type=F32)
    counts = jnp.maximum(jnp.sum(same, axis=1, keepdims=True), 1.0)
    same = same.astype(BF16)
    means = jnp.dot(same, arrived, preferred_element_type=F32) / counts
    high = (arrived.astype(F32) - means).astype(BF16)
    low = -(jnp.dot(same, high, preferred_element_type=F32) / counts)
    both = [high.astype(F32)[:, :part], low[:, :part]]
    if bw > 2 * part:
        both.append(jnp.zeros((n * SLOT, bw - 2 * part), F32))
    bsend[...] = jnp.concatenate(both, axis=1).astype(BF16)

    own_b = pltpu.make_async_copy(bsend.at[slot_rows(r), :], brec.at[slot_rows(r), :], l_s.at[1])
    own_b.start()

    @pl.loop(1, n)
    def _(k):
        to_source(k).start()

    for t in range(AHEAD[0], AHEAD[1]):
        start_x(t)
    for copy in kept:
        copy.wait()

    @pl.loop(0, tiles)
    def _(t):
        for h in range(2):
            mask(h, bit[h], t)

    own_b.wait()

    @pl.loop(1, n)
    def _(k):
        from_owner(k).wait_recv()

    back = lax.dot_general(brec[...], perm[...], (((0,), (0,)), ((), ())), preferred_element_type=F32)
    for h in range(2):
        for b in range(2):
            for s in range(zs):
                for i in range(2):
                    pieces = []
                    for o in range(2):
                        at = i * part + (s * G + (2 * b + o if h == 0 else 2 * o + b)) * pd
                        pieces.append(back[at:at + pd])
                    if pr > 2 * pd:
                        pieces.append(jnp.zeros((pr - 2 * pd, rows), F32))
                    own[h, b, c, s * pr:(s + 1) * pr, i * rows:(i + 1) * rows] = (
                        jnp.concatenate(pieces, axis=0).astype(BF16))
    for h in range(2):
        p_copy(h).start()

    @pl.loop(1, ncol)
    def _(j):
        c_send(j).start()

    for t in range(AHEAD[1], AHEAD[2]):
        start_x(t)

    for h in range(2):
        p_copy(h).wait_recv()

        @pl.loop(1, ncol)
        def _(j, h=h):
            e_send(h, j).start()

    @pl.loop(1, ncol)
    def _(j):
        c_from(j).wait_recv()
        for h in range(2):
            e_from(h, j).wait_recv()

    def r_copy(h, t):
        return remote(rsend.at[t, h], rrec.at[t, h], r_s.at[h, t], r_r.at[h, t], row=peer[1 - h])

    def multiply(t):
        for h in range(2):
            x_copy(h, t).wait_recv()
            mine = xm[h, bit[h], t]
            theirs = xin[h, t]

            def product(b):
                ours = own[h, b].reshape(line * pr, 2 * rows)
                other = mate[h, b].reshape(line * pr, 2 * rows)
                total = jnp.dot(ours[:, :rows], mine, preferred_element_type=F32)
                total += jnp.dot(ours[:, rows:], mine, preferred_element_type=F32)
                total += jnp.dot(other[:, :rows], theirs, preferred_element_type=F32)
                total += jnp.dot(other[:, rows:], theirs, preferred_element_type=F32)
                return total

            rsend[t, h] = product(1 - bit[1 - h]).astype(BF16)
            r_copy(h, t).start()
            total = product(bit[1 - h])
            for a in range(line):
                acc[t, a, h] = total[a * pr:(a + 1) * pr]

    def reduce(t):
        for h in range(2):
            r_copy(h, t).wait_recv()
            for a in range(line):
                acc[t, a, h] += rrec[t, h, a * pr:(a + 1) * pr].astype(F32)

    def up(t, a):
        return remote(zsend.at[t, a], from_low.at[t, a], lo_s.at[t, a], lo_r.at[t, a], row=(r + G) % n)

    def down(t, a):
        return remote(zsend.at[t, a], from_high.at[t, a], hi_s.at[t, a], hi_r.at[t, a], row=(r + n - G) % n)

    def up_last(t):
        return remote(acc.at[t, line - 1], landed.at[t], lo_s.at[t, line - 1], lo_r.at[t, line - 1], row=(r + G) % n)

    def down_last(t):
        return remote(acc.at[t, 0], landed.at[t], hi_s.at[t, 0], hi_r.at[t, 0], row=(r + n - G) % n)

    def either(pred, yes, no):
        pl.when(pred)(yes)
        pl.when(jnp.logical_not(pred))(no)

    def take_up(t, a):
        def last():
            up_last(t).wait_recv()
            acc[t, a] += landed[t]

        def other():
            up(t, a).wait_recv()
            acc[t, a] += from_low[t, a].astype(F32)

        @pl.when(z > 0)
        def _():
            either(z == line - 1, last, other)

    def take_down(t, a):
        def last():
            down_last(t).wait_recv()
            acc[t, a] += landed[t]

        def other():
            down(t, a).wait_recv()
            acc[t, a] += from_high[t, a].astype(F32)

        @pl.when(z < line - 1)
        def _():
            either(z == 0, last, other)

    def forward(t):
        def go_up(i, carry):
            a = line - 1 - i
            take_up(t, a)

            def other():
                zsend[t, a] = acc[t, a].astype(BF16)
                up(t, a).start()

            either(z == line - 2, lambda: up_last(t).start(), other)
            return carry

        def go_down(a, carry):
            take_down(t, a)

            def other():
                zsend[t, a] = acc[t, a].astype(BF16)
                down(t, a).start()

            either(z == 1, lambda: down_last(t).start(), other)
            return carry

        @pl.when(z < line // 2)
        def _():
            lax.fori_loop(0, line - 1 - z, go_up, 0)

        lax.fori_loop(0, z, go_down, 0)

        @pl.when(z >= line // 2)
        def _():
            lax.fori_loop(0, line - 1 - z, go_up, 0)

    def cols_of(h, b, t):
        return pl.ds(pl.multiple_of(start_of(h, b) + t * tw, BLOCK), tw)

    def f_copy(h, t):
        return remote(fin.at[t, h, 1 - bit[h]], out.at[:, cols_of(h, bit[h], t)],
                      f_s.at[h, t], f_r.at[h, t], row=peer[h])

    def f_from(h, t):
        return remote(fin.at[t, h, 1 - bit[h]], out.at[:, cols_of(h, 1 - bit[h], t)],
                      f_s.at[h, t], f_r.at[h, t], row=peer[h])

    def finish(t):
        take_up(t, z)
        take_down(t, z)
        for h in range(2):
            total = acc[t, z, h] * factor
            for o in range(2):
                fin[t, h, o] = total[o * pd:(o + 1) * pd]
            f_copy(h, t).start()
            out[:, cols_of(h, bit[h], t)] = fin[t, h, bit[h]]

    edge = (z == 0) | (z == line - 1)

    def step(t, carry):
        @pl.when(t < tiles)
        def _():
            multiply(t)

        @pl.when(t + AHEAD[2] < tiles)
        def _():
            start_x(t + AHEAD[2])

        @pl.when((t >= 1) & (t < tiles + 1))
        def _():
            reduce(t - 1)

        @pl.when(edge & (t >= 1) & (t < tiles + 1))
        def _():
            forward(t - 1)

        @pl.when(jnp.logical_not(edge) & (t >= 2) & (t < tiles + 2))
        def _():
            forward(t - 2)

        @pl.when(t >= 3)
        def _():
            finish(t - 3)

        return carry

    lax.fori_loop(0, tiles + 3, step, 0)

    @pl.loop(0, tiles)
    def _(t):
        for h in range(2):
            f_from(h, t).wait_recv()
            f_copy(h, t).wait_send()
            x_copy(h, t).wait_send()
            r_copy(h, t).wait_send()

        def sent_up(a, carry):
            either(z == line - 2, lambda: up_last(t).wait_send(), lambda: up(t, a).wait_send())
            return carry

        def sent_down(a, carry):
            either(z == 1, lambda: down_last(t).wait_send(), lambda: down(t, a).wait_send())
            return carry

        lax.fori_loop(z + 1, line, sent_up, 0)
        lax.fori_loop(0, z, sent_down, 0)

    for h in range(2):
        p_copy(h).wait_send()

    @pl.loop(1, ncol)
    def _(j):
        c_send(j).wait_send()
        for h in range(2):
            e_send(h, j).wait_send()

    @pl.loop(1, n)
    def _(k):
        to_owner(k).wait_send()
        to_source(k).wait_send()


def body(descriptors, block_mask, config_of):
    n, ncol = lax.axis_size("row"), lax.axis_size("col")
    rows, width = descriptors.shape
    part = PW // ncol
    wide = -(-(part + 1) // BLOCK) * BLOCK
    bw = -(-2 * part // BLOCK) * BLOCK
    quarter_blocks = width // BLOCK // 4
    tiles = next(k for k in (TILES, 5, 1) if quarter_blocks % k == 0)
    tw = quarter_blocks // tiles * BLOCK
    line = n // G
    pd = PW // n
    pr = -(-2 * pd // 16) * 16
    zs = line // ncol

    cfg = (n, ncol, rows, width, part, wide, bw, tiles, tw, line, pd, pr, zs, 1.0 / (rows * n))
    vm = pltpu.VMEM
    dma = pltpu.SemaphoreType.DMA
    full = pl.BlockSpec(memory_space=pltpu.VMEM)
    return pl.pallas_call(
        functools.partial(kernel, cfg),
        out_shape=jax.ShapeDtypeStruct((pd, width), F32),
        in_specs=[full, pl.BlockSpec(memory_space=pltpu.SMEM), pl.BlockSpec(memory_space=pl.ANY)],
        out_specs=full,
        scratch_shapes=[
            vm((rows, wide), BF16),
            vm((n * SLOT, rows), BF16),
            vm((n * SLOT, wide), BF16),
            vm((n * SLOT, wide), BF16),
            vm((n * SLOT, bw), BF16),
            vm((n * SLOT, bw), BF16),
            vm((rows, width), BF16),
            vm((2, 2, tiles, rows, tw), BF16),
            vm((2, tiles, rows, tw), BF16),
            vm((2, 2, ncol, zs * pr, 2 * rows), BF16),
            vm((2, 2, ncol, zs * pr, 2 * rows), BF16),
            vm((tiles, line, 2, pr, tw), F32),
            vm((tiles, 2, line * pr, tw), BF16),
            vm((tiles, 2, line * pr, tw), BF16),
            vm((tiles, line, 2, pr, tw), BF16),
            vm((tiles, line, 2, pr, tw), BF16),
            vm((tiles, line, 2, pr, tw), BF16),
            vm((tiles, 2, pr, tw), F32),
            vm((tiles, 2, 2, pd, tw), F32),
            dma((n,)), dma((n,)), dma((n,)), dma((n,)),
            dma((2,)), dma((2,)), dma((ncol,)), dma((ncol,)), dma((2, ncol)), dma((2, ncol)), dma((6,)),
            dma((2, tiles)), dma((2, tiles)), dma((2, tiles)), dma((2, tiles)),
            dma((tiles, line)), dma((tiles, line)), dma((tiles, line)), dma((tiles, line)),
            dma((2, tiles)), dma((2, tiles)),
        ],
        compiler_params=pltpu.CompilerParams(
            collective_id=0, has_side_effects=True, vmem_limit_bytes=56 * 1024 * 1024),
    )(config_of[None, :], block_mask, descriptors)


def solution(mesh):
    in_specs = (P("row", "col"), P("row", "col"), P("row"))
    out_specs = P("row", "col")
    return jax.shard_map(body, mesh=mesh, in_specs=in_specs, out_specs=out_specs, check_vma=False)
```

```python
import functools

import jax
import jax.numpy as jnp
from jax import lax
from jax.experimental import pallas as pl
from jax.experimental.pallas import tpu as pltpu
from jax.sharding import PartitionSpec as P

PW = 384
CONF_DEV = 64
BLOCK = 128
G = 4
SLOT = 16
TILES = 10
AHEAD = (2, 3, 4)
DEFER = 2
LAGS = (1, 2, 3, 3, 5)
F32 = jnp.float32
BF16 = jnp.bfloat16


def remote(src, dst, send, recv, **where):
    return pltpu.make_async_remote_copy(
        src_ref=src, dst_ref=dst, send_sem=send, recv_sem=recv,
        device_id=where, device_id_type=pl.DeviceIdType.MESH,
    )


def kernel(cfg, config_of, block_mask, x, out,
           crow, marks, pext, perm, asend, arec, bsend, brec, xraw, xm, xin, own, mate,
           acc, rsend, rrec, zsend, from_low, from_high, landed, fin,
           a_s, a_r, b_s, b_r, p_s, p_r, c_s, c_r, e_s, e_r, l_s,
           x_s, x_r, r_s, r_r, z_s, lo_r, hi_r, f_s, f_r, g_s):
    n, ncol, rows, width, part, wide, bw, tiles, tw, line, pd, pr, zs, factor = cfg
    quarter = width // 4
    half = line // 2
    r = lax.axis_index("row")
    c = lax.axis_index("col")
    z = r // G
    q = r % G
    near, far = z // half, 1 - z // half
    bit = (q % 2, q // 2)
    peer = tuple(r + (1 - 2 * bit[h]) * (1 << h) for h in range(2))

    barrier = pltpu.get_barrier_semaphore()

    @pl.loop(1, n)
    def _(k):
        pl.semaphore_signal(barrier, inc=1, device_id={"row": (r + k) % n}, device_id_type=pl.DeviceIdType.MESH)

    @pl.loop(1, ncol)
    def _(k):
        pl.semaphore_signal(barrier, inc=1, device_id={"col": (c + k) % ncol}, device_id_type=pl.DeviceIdType.MESH)

    crow_copy = pltpu.make_async_copy(config_of, crow, l_s.at[6])
    marks_copy = pltpu.make_async_copy(block_mask, marks, l_s.at[7])
    crow_copy.start()
    marks_copy.start()
    panel_copy = pltpu.make_async_copy(x.at[:, :wide], pext, l_s.at[0])
    panel_copy.start()

    def start_of(h, b):
        return h * 2 * quarter + b * quarter

    def load(h, b, i):
        cols = pl.ds(pl.multiple_of(start_of(h, b), BLOCK), quarter)
        return pltpu.make_async_copy(x.at[:, cols], xraw.at[:, cols], l_s.at[i])

    away = [load(h, 1 - bit[h], 2 + h) for h in range(2)]
    kept = [load(h, bit[h], 4 + h) for h in range(2)]
    for copy in away + kept:
        copy.start()

    first = lax.broadcasted_iota(jnp.int32, (rows, rows), 0)
    second = lax.broadcasted_iota(jnp.int32, (rows, rows), 1)
    crow_copy.wait()
    ids_row = jnp.broadcast_to(crow[...], (rows, rows)).astype(F32)
    ids_col = jnp.sum(jnp.where(first == second, ids_row, 0.0), axis=1, keepdims=True).astype(jnp.int32)
    shift = CONF_DEV.bit_length() - 1
    owner = crow[...] >> shift
    before = ((ids_col >> shift) == owner) & (first < second)
    rank = jnp.sum(jnp.where(before, 1.0, 0.0), axis=0, keepdims=True)
    place = owner.astype(F32) * SLOT + rank
    slots = lax.broadcasted_iota(jnp.int32, (n * SLOT, rows), 0).astype(F32)
    perm[...] = jnp.where(slots == place, 1.0, 0.0).astype(BF16)
    label = ((ids_col & (CONF_DEV - 1)) + 1).astype(F32)
    lane = lax.broadcasted_iota(jnp.int32, (BLOCK, BLOCK), 1)
    panel_copy.wait()
    marks_copy.wait()
    for b in range(rows // BLOCK):
        span = slice(b * BLOCK, (b + 1) * BLOCK)
        for w in range(wide // BLOCK):
            cols = slice(w * BLOCK, (w + 1) * BLOCK)
            keep = marks[b, w].astype(F32) if w * BLOCK < part else 0.0
            block = pext[span, cols].astype(F32) * jnp.broadcast_to(keep, (BLOCK, BLOCK))
            if (w + 1) * BLOCK > part:
                block = jnp.where(lane + w * BLOCK < part, block, jnp.broadcast_to(label[span], (BLOCK, BLOCK)))
            pext[span, cols] = block.astype(BF16)
    asend[...] = jnp.dot(perm[...], pext[...], preferred_element_type=F32).astype(BF16)

    def mask(h, b, t):
        base = start_of(h, b) + t * tw
        for i in range(rows // BLOCK):
            span = slice(i * BLOCK, (i + 1) * BLOCK)
            for w in range(tw // BLOCK):
                keep = marks[i, base // BLOCK + w].astype(F32)
                cols = pl.ds(pl.multiple_of(base + w * BLOCK, BLOCK), BLOCK)
                xm[h, b, t, span, w * BLOCK:(w + 1) * BLOCK] = (
                    xraw[span, cols] * jnp.broadcast_to(keep, (BLOCK, BLOCK)).astype(BF16))

    def mask_away(low, high):
        @pl.loop(low, high)
        def _(t):
            for h in range(2):
                mask(h, 1 - bit[h], t)

    for copy in away:
        copy.wait()
    mask_away(0, AHEAD[0])
    pl.semaphore_wait(barrier, n - 1 + ncol - 1)

    def slot_rows(k):
        return pl.ds(pl.multiple_of(k * SLOT, SLOT), SLOT)

    def to_owner(k):
        to = (r + k) % n
        return remote(asend.at[slot_rows(to), :], arec.at[slot_rows(r), :], a_s, a_r, row=to)

    others = slice(0, (n - 1) * SLOT)

    def all_a():
        return remote(asend.at[others, :], arec.at[others, :], a_s, a_r, row=(r + 1) % n)

    def to_source(k):
        to = (r + k) % n
        return remote(bsend.at[slot_rows(to), :], brec.at[slot_rows(r), :], b_s, b_r, row=to)

    def all_b():
        return remote(bsend.at[others, :], brec.at[others, :], b_s, b_r, row=(r + 1) % n)

    def x_copy(h, t):
        return remote(xm.at[h, 1 - bit[h], t], xin.at[t, h], x_s.at[h], x_r.at[t], row=peer[h])

    def x_both(t):
        return remote(xin.at[t], xin.at[t], x_s.at[0], x_r.at[t], row=peer[0])

    def x_all(h):
        return remote(xm.at[h, 1 - bit[h]], xm.at[h, 1 - bit[h]], x_s.at[h], x_r.at[0], row=peer[h])

    def start_x(t):
        for h in range(2):
            x_copy(h, t).start()

    def p_copy(h):
        return remote(own.at[h, :, c], mate.at[h, :, c], p_s.at[h], p_r.at[h], row=peer[h])

    def c_send(j):
        to = (c + j) % ncol
        return remote(own.at[:, :, c], own.at[:, :, c], c_s.at[j], c_r.at[c], col=to)

    def c_from(j):
        to = (c + j) % ncol
        return remote(own.at[:, :, c], own.at[:, :, to], c_s.at[j], c_r.at[to], col=to)

    def e_send(h, j):
        to = (c + j) % ncol
        return remote(mate.at[h, :, c], mate.at[h, :, c], e_s.at[h, j], e_r.at[h, c], col=to)

    def e_from(h, j):
        to = (c + j) % ncol
        return remote(mate.at[h, :, c], mate.at[h, :, to], e_s.at[h, j], e_r.at[h, to], col=to)

    own_a = pltpu.make_async_copy(asend.at[slot_rows(r), :], arec.at[slot_rows(r), :], l_s.at[0])
    own_a.start()

    @pl.loop(1, n)
    def _(k):
        to_owner(k).start()

    for t in range(AHEAD[0]):
        start_x(t)
    mask_away(AHEAD[0], tiles)

    own_a.wait()
    all_a().wait_recv()

    arrived = arec[...]
    label = arrived[:, part:part + 1].astype(F32)
    ids = lax.broadcasted_iota(jnp.int32, (n * SLOT, BLOCK), 1).astype(F32) + 1.0
    member = jnp.where((label == ids) & (ids <= CONF_DEV), 1.0, 0.0).astype(BF16)
    same = lax.dot_general(member, member, (((1,), (1,)), ((), ())), preferred_element_type=F32)
    counts = jnp.maximum(jnp.sum(same, axis=1, keepdims=True), 1.0)
    same = same.astype(BF16)
    means = jnp.dot(same, arrived, preferred_element_type=F32) / counts
    high = (arrived.astype(F32) - means).astype(BF16)
    low = -(jnp.dot(same, high, preferred_element_type=F32) / counts)
    both = [high.astype(F32)[:, :part], low[:, :part]]
    if bw > 2 * part:
        both.append(jnp.zeros((n * SLOT, bw - 2 * part), F32))
    bsend[...] = jnp.concatenate(both, axis=1).astype(BF16)

    own_b = pltpu.make_async_copy(bsend.at[slot_rows(r), :], brec.at[slot_rows(r), :], l_s.at[1])
    own_b.start()

    @pl.loop(1, n)
    def _(k):
        to_source(k).start()

    for t in range(AHEAD[0], AHEAD[1]):
        start_x(t)
    for copy in kept:
        copy.wait()

    @pl.loop(0, tiles)
    def _(t):
        for h in range(2):
            mask(h, bit[h], t)

    own_b.wait()
    all_b().wait_recv()

    back = lax.dot_general(brec[...], perm[...], (((0,), (0,)), ((), ())), preferred_element_type=F32)
    for h in range(2):
        for b in range(2):
            for s in range(zs):
                for i in range(2):
                    pieces = []
                    for o in range(2):
                        at = i * part + (s * G + (2 * b + o if h == 0 else 2 * o + b)) * pd
                        pieces.append(back[at:at + pd])
                    if pr > 2 * pd:
                        pieces.append(jnp.zeros((pr - 2 * pd, rows), F32))
                    own[h, b, c, s * pr:(s + 1) * pr, i * rows:(i + 1) * rows] = (
                        jnp.concatenate(pieces, axis=0).astype(BF16))
    for h in range(2):
        p_copy(h).start()

    @pl.loop(1, ncol)
    def _(j):
        c_send(j).start()

    for t in range(AHEAD[1], AHEAD[2]):
        start_x(t)

    for h in range(2):
        p_copy(h).wait_recv()

        @pl.loop(1, ncol)
        def _(j, h=h):
            e_send(h, j).start()

    @pl.loop(1, ncol)
    def _(j):
        c_from(j).wait_recv()
        for h in range(2):
            e_from(h, j).wait_recv()

    def r_copy(h, t, k):
        return remote(rsend.at[t, k, h], rrec.at[t, k, h], r_s, r_r.at[t, k], row=peer[1 - h])

    def r_both(t, k):
        return remote(rrec.at[t, k], rrec.at[t, k], r_s, r_r.at[t, k], row=peer[0])

    def r_all():
        return remote(rsend, rrec, r_s, r_r.at[0, 0], row=peer[0])

    def start_r(t, k):
        for h in range(2):
            r_copy(h, t, k).start()

    def multiply(t):
        x_both(t).wait_recv()

        def product(h, b):
            ours = own[h, b].reshape(line * pr, 2 * rows)
            other = mate[h, b].reshape(line * pr, 2 * rows)
            mine = xm[h, bit[h], t]
            theirs = xin[t, h]
            total = jnp.dot(ours[:, :rows], mine, preferred_element_type=F32)
            total += jnp.dot(ours[:, rows:], mine, preferred_element_type=F32)
            total += jnp.dot(other[:, :rows], theirs, preferred_element_type=F32)
            total += jnp.dot(other[:, rows:], theirs, preferred_element_type=F32)
            return total

        for h in range(2):
            total = product(h, 1 - bit[1 - h]).astype(BF16)
            for k in range(2):
                rsend[t, k, h] = total[k * half * pr:(k + 1) * half * pr]
            r_copy(h, t, far).start()
        for h in range(2):
            total = product(h, bit[1 - h])
            for a in range(line):
                acc[t, a, h] = total[a * pr:(a + 1) * pr]

    def reduce(t, k):
        r_both(t, k).wait_recv()
        for h in range(2):
            for i in range(half):
                acc[t, k * half + i, h] += rrec[t, k, h, i * pr:(i + 1) * pr].astype(F32)

    def up(t, a):
        return remote(zsend.at[t, a], from_low.at[t, a], z_s.at[a], lo_r.at[t, a], row=(r + G) % n)

    def down(t, a):
        return remote(zsend.at[t, a], from_high.at[t, a], z_s.at[a], hi_r.at[t, a], row=(r + n - G) % n)

    def up_last(t):
        return remote(acc.at[t, line - 1], landed.at[t], z_s.at[line - 1], lo_r.at[t, line - 1], row=(r + G) % n)

    def down_last(t):
        return remote(acc.at[t, 0], landed.at[t], z_s.at[0], hi_r.at[t, 0], row=(r + n - G) % n)

    def either(pred, yes, no):
        pl.when(pred)(yes)
        pl.when(jnp.logical_not(pred))(no)

    def take_up(t, a):
        def last():
            up_last(t).wait_recv()
            acc[t, a] += landed[t]

        def other():
            up(t, a).wait_recv()
            acc[t, a] += from_low[t, a].astype(F32)

        @pl.when(z > 0)
        def _():
            either(z == line - 1, last, other)

    def take_down(t, a):
        def last():
            down_last(t).wait_recv()
            acc[t, a] += landed[t]

        def other():
            down(t, a).wait_recv()
            acc[t, a] += from_high[t, a].astype(F32)

        @pl.when(z < line - 1)
        def _():
            either(z == 0, last, other)

    def go_up(t, a):
        take_up(t, a)

        def other():
            zsend[t, a] = acc[t, a].astype(BF16)
            up(t, a).start()

        either(z == line - 2, lambda: up_last(t).start(), other)

    def go_down(t, a):
        take_down(t, a)

        def other():
            zsend[t, a] = acc[t, a].astype(BF16)
            down(t, a).start()

        either(z == 1, lambda: down_last(t).start(), other)

    def forward_far(t):
        @pl.loop(0, half)
        def _(i):
            either(z < half, lambda: go_up(t, line - 1 - i), lambda: go_down(t, i))

    def forward_near(t):
        last = (near + 1) * half - 1

        @pl.loop(0, last - z)
        def _(i):
            go_up(t, last - i)

        @pl.loop(near * half, z)
        def _(a):
            go_down(t, a)

    def cols_of(h, b, t):
        return pl.ds(pl.multiple_of(start_of(h, b) + t * tw, BLOCK), tw)

    def f_copy(h, t):
        return remote(fin.at[t, h, 1 - bit[h]], out.at[:, cols_of(h, bit[h], t)],
                      f_s.at[h], f_r.at[h], row=peer[h])

    def f_own(h, t):
        return pltpu.make_async_copy(fin.at[t, h, bit[h]], out.at[:, cols_of(h, bit[h], t)], g_s.at[h])

    def f_all(h, b):
        area = out.at[:, pl.ds(pl.multiple_of(start_of(h, b), BLOCK), quarter)]
        return remote(area, area, f_s.at[h], f_r.at[h], row=peer[h])

    def g_all(h):
        area = out.at[:, pl.ds(pl.multiple_of(start_of(h, bit[h]), BLOCK), quarter)]
        return pltpu.make_async_copy(area, area, g_s.at[h])

    def finish(t):
        take_up(t, z)
        take_down(t, z)
        for h in range(2):
            total = acc[t, z, h] * factor
            for o in range(2):
                fin[t, h, o] = total[o * pd:(o + 1) * pd]
            f_copy(h, t).start()
            f_own(h, t).start()

    edge = (z == 0) | (z == line - 1)

    def at(step, lag, act, also=True):
        t = step - lag

        @pl.when((t >= 0) & (t < tiles) & also)
        def _():
            act(t)

    def step(t, carry):
        at(t, 0, multiply)

        @pl.when(t + AHEAD[2] < tiles)
        def _():
            start_x(t + AHEAD[2])

        @pl.when((t >= DEFER) & (t < tiles))
        def _():
            start_r(t - DEFER, near)

        @pl.when(t == tiles - 1)
        def _():
            for k in range(tiles - DEFER, tiles):
                start_r(k, near)

        at(t, LAGS[0], lambda k: reduce(k, far))
        at(t, LAGS[0], forward_far, edge)
        at(t, LAGS[1], forward_far, jnp.logical_not(edge))
        at(t, LAGS[2], lambda k: reduce(k, near))
        at(t, LAGS[3], forward_near)
        at(t, LAGS[4], finish)
        return carry

    lax.fori_loop(0, tiles + LAGS[4], step, 0)

    for h in range(2):
        f_all(h, 1 - bit[h]).wait_recv()
        f_all(h, bit[h]).wait_send()
        g_all(h).wait()
        x_all(h).wait_send()
        p_copy(h).wait_send()
    r_all().wait_send()

    @pl.loop(0, line)
    def _(a):
        last = ((z == line - 2) & (a == line - 1)) | ((z == 1) & (a == 0))

        @pl.when(last)
        def _():
            remote(acc.at[:, a], acc.at[:, a], z_s.at[a], lo_r.at[0, 0], row=peer[0]).wait_send()

        @pl.when(jnp.logical_not(last) & (a != z))
        def _():
            remote(zsend.at[:, a], zsend.at[:, a], z_s.at[a], lo_r.at[0, 0], row=peer[0]).wait_send()

    @pl.loop(1, ncol)
    def _(j):
        c_send(j).wait_send()
        for h in range(2):
            e_send(h, j).wait_send()

    all_a().wait_send()
    all_b().wait_send()


def body(descriptors, block_mask, config_of):
    n, ncol = lax.axis_size("row"), lax.axis_size("col")
    rows, width = descriptors.shape
    part = PW // ncol
    wide = -(-(part + 1) // BLOCK) * BLOCK
    bw = -(-2 * part // BLOCK) * BLOCK
    quarter_blocks = width // BLOCK // 4
    tiles = next(k for k in (TILES, 5, 1) if quarter_blocks % k == 0)
    tw = quarter_blocks // tiles * BLOCK
    line = n // G
    pd = PW // n
    pr = -(-2 * pd // 16) * 16
    zs = line // ncol

    cfg = (n, ncol, rows, width, part, wide, bw, tiles, tw, line, pd, pr, zs, 1.0 / (rows * n))
    vm = pltpu.VMEM
    dma = pltpu.SemaphoreType.DMA
    hbm = pl.BlockSpec(memory_space=pl.ANY)
    return pl.pallas_call(
        functools.partial(kernel, cfg),
        out_shape=jax.ShapeDtypeStruct((pd, width), F32),
        in_specs=[hbm, hbm, hbm],
        out_specs=hbm,
        scratch_shapes=[
            vm((1, rows), jnp.int32),
            pltpu.SMEM(block_mask.shape, jnp.int32),
            vm((rows, wide), BF16),
            vm((n * SLOT, rows), BF16),
            vm((n * SLOT, wide), BF16),
            vm((n * SLOT, wide), BF16),
            vm((n * SLOT, bw), BF16),
            vm((n * SLOT, bw), BF16),
            vm((rows, width), BF16),
            vm((2, 2, tiles, rows, tw), BF16),
            vm((tiles, 2, rows, tw), BF16),
            vm((2, 2, ncol, zs * pr, 2 * rows), BF16),
            vm((2, 2, ncol, zs * pr, 2 * rows), BF16),
            vm((tiles, line, 2, pr, tw), F32),
            vm((tiles, 2, 2, line // 2 * pr, tw), BF16),
            vm((tiles, 2, 2, line // 2 * pr, tw), BF16),
            vm((tiles, line, 2, pr, tw), BF16),
            vm((tiles, line, 2, pr, tw), BF16),
            vm((tiles, line, 2, pr, tw), BF16),
            vm((tiles, 2, pr, tw), F32),
            vm((tiles, 2, 2, pd, tw), F32),
            dma, dma, dma, dma,
            dma((2,)), dma((2,)), dma((ncol,)), dma((ncol,)), dma((2, ncol)), dma((2, ncol)), dma((8,)),
            dma((2,)), dma((tiles,)), dma, dma((tiles, 2)), dma((line,)), dma((tiles, line)), dma((tiles, line)),
            dma((2,)), dma((2,)), dma((2,)),
        ],
        compiler_params=pltpu.CompilerParams(
            collective_id=0, has_side_effects=True, vmem_limit_bytes=56 * 1024 * 1024),
    )(config_of[None, :], block_mask, descriptors)


def solution(mesh):
    in_specs = (P("row", "col"), P("row", "col"), P("row"))
    out_specs = P("row", "col")
    return jax.shard_map(body, mesh=mesh, in_specs=in_specs, out_specs=out_specs, check_vma=False)
```

```python
import functools

import jax
import jax.numpy as jnp
from jax import lax
from jax.experimental import pallas as pl
from jax.experimental.pallas import tpu as pltpu
from jax.sharding import PartitionSpec as P

PW = 384
CONF_DEV = 64
BLOCK = 128
G = 4
SLOT = 16
TILES = 8
AHEAD = (3, 4, 5)
DEFER = 3
LAGS = (1, 3, 4, 4, 7)
PAIR_AHEAD = (0, 0, 0)
PAIR_LAGS = (2, 3, 4, 6)
F32 = jnp.float32
BF16 = jnp.bfloat16


def remote(src, dst, send, recv, **where):
    return pltpu.make_async_remote_copy(
        src_ref=src, dst_ref=dst, send_sem=send, recv_sem=recv,
        device_id=where, device_id_type=pl.DeviceIdType.MESH,
    )


def kernel(cfg, config_of, block_mask, x, out,
           crow, marks, pext, perm, asend, arec, bsend, brec, xraw, xm, xin, own, mate,
           xz, zin, zfull, z1s, z1r, z2s, z2r, z3s, z3r, fz,
           acc, rsend, rrec, zsend, from_low, from_high, landed, fin,
           a_s, a_r, b_s, b_r, p_s, p_r, c_s, c_r, e_s, e_r, l_s,
           x_s, x_r, r_s, r_r, z_s, lo_r, hi_r, f_s, f_r, g_s,
           zx_s, zx_r, z1_s, z1_r, z2_s, z2_r, z3_s, z3_r, fz_s, fz_r, gz_s):
    n, ncol, rows, width, part, wide, bw, tiles, tw, line, pd, pr, zs, quarter, groups, factor = cfg
    side = (width - 4 * quarter) // 2
    pairs = line // 2
    half = line // 2
    r = lax.axis_index("row")
    c = lax.axis_index("col")
    z = r // G
    q = r % G
    near, far = z // half, 1 - z // half
    pair, odd = z // 2, z % 2
    bit = (q % 2, q // 2)
    peer = tuple(r + (1 - 2 * bit[h]) * (1 << h) for h in range(2)) + (r + (1 - 2 * odd) * G,)

    barrier = pltpu.get_barrier_semaphore()

    @pl.loop(1, n)
    def _(k):
        pl.semaphore_signal(barrier, inc=1, device_id={"row": (r + k) % n}, device_id_type=pl.DeviceIdType.MESH)

    @pl.loop(1, ncol)
    def _(k):
        pl.semaphore_signal(barrier, inc=1, device_id={"col": (c + k) % ncol}, device_id_type=pl.DeviceIdType.MESH)

    crow_copy = pltpu.make_async_copy(config_of, crow, l_s.at[6])
    marks_copy = pltpu.make_async_copy(block_mask, marks, l_s.at[7])
    crow_copy.start()
    marks_copy.start()
    panel_copy = pltpu.make_async_copy(x.at[:, :wide], pext, l_s.at[0])
    panel_copy.start()

    def start_of(h, b):
        return h * 2 * quarter + b * quarter

    def load(h, b, i):
        cols = pl.ds(pl.multiple_of(start_of(h, b), BLOCK), quarter)
        return pltpu.make_async_copy(x.at[:, cols], xraw.at[:, cols], l_s.at[i])

    away = [load(h, 1 - bit[h], 2 + h) for h in range(2)]
    kept = [load(h, bit[h], 4 + h) for h in range(2)]
    rest = pltpu.make_async_copy(x.at[:, 4 * quarter:], xraw.at[:, 4 * quarter:], l_s.at[8])
    for copy in away + [rest] + kept:
        copy.start()

    first = lax.broadcasted_iota(jnp.int32, (rows, rows), 0)
    second = lax.broadcasted_iota(jnp.int32, (rows, rows), 1)
    crow_copy.wait()
    ids_row = jnp.broadcast_to(crow[...], (rows, rows)).astype(F32)
    ids_col = jnp.sum(jnp.where(first == second, ids_row, 0.0), axis=1, keepdims=True).astype(jnp.int32)
    shift = CONF_DEV.bit_length() - 1
    owner = crow[...] >> shift
    before = ((ids_col >> shift) == owner) & (first < second)
    rank = jnp.sum(jnp.where(before, 1.0, 0.0), axis=0, keepdims=True)
    place = owner.astype(F32) * SLOT + rank
    slots = lax.broadcasted_iota(jnp.int32, (n * SLOT, rows), 0).astype(F32)
    perm[...] = jnp.where(slots == place, 1.0, 0.0).astype(BF16)
    label = ((ids_col & (CONF_DEV - 1)) + 1).astype(F32)
    lane = lax.broadcasted_iota(jnp.int32, (BLOCK, BLOCK), 1)
    panel_copy.wait()
    marks_copy.wait()
    for b in range(rows // BLOCK):
        span = slice(b * BLOCK, (b + 1) * BLOCK)
        for w in range(wide // BLOCK):
            cols = slice(w * BLOCK, (w + 1) * BLOCK)
            keep = marks[b, w].astype(F32) if w * BLOCK < part else 0.0
            block = pext[span, cols].astype(F32) * jnp.broadcast_to(keep, (BLOCK, BLOCK))
            if (w + 1) * BLOCK > part:
                block = jnp.where(lane + w * BLOCK < part, block, jnp.broadcast_to(label[span], (BLOCK, BLOCK)))
            pext[span, cols] = block.astype(BF16)
    asend[...] = jnp.dot(perm[...], pext[...], preferred_element_type=F32).astype(BF16)

    def mask_to(dst, base):
        for i in range(rows // BLOCK):
            span = slice(i * BLOCK, (i + 1) * BLOCK)
            for w in range(tw // BLOCK):
                keep = marks[i, base // BLOCK + w].astype(F32)
                cols = pl.ds(pl.multiple_of(base + w * BLOCK, BLOCK), BLOCK)
                dst[span, w * BLOCK:(w + 1) * BLOCK] = (
                    xraw[span, cols] * jnp.broadcast_to(keep, (BLOCK, BLOCK)).astype(BF16))

    def mask(h, b, t):
        mask_to(xm.at[h, b, t], start_of(h, b) + t * tw)

    def pair_start(b, u):
        return 4 * quarter + b * side + u * 2 * tw

    def mask_pair(b, u):
        for g in range(2):
            mask_to(xz.at[b, u, g], pair_start(b, u) + g * tw)

    def mask_away(low, high):
        @pl.loop(low, high)
        def _(t):
            for h in range(2):
                mask(h, 1 - bit[h], t)

    for copy in away:
        copy.wait()
    mask_away(0, AHEAD[0])
    pl.semaphore_wait(barrier, n - 1 + ncol - 1)

    def slot_rows(k):
        return pl.ds(pl.multiple_of(k * SLOT, SLOT), SLOT)

    def to_owner(k):
        to = (r + k) % n
        return remote(asend.at[slot_rows(to), :], arec.at[slot_rows(r), :], a_s, a_r, row=to)

    others = slice(0, (n - 1) * SLOT)

    def all_a():
        return remote(asend.at[others, :], arec.at[others, :], a_s, a_r, row=(r + 1) % n)

    def to_source(k):
        to = (r + k) % n
        return remote(bsend.at[slot_rows(to), :], brec.at[slot_rows(r), :], b_s, b_r, row=to)

    def all_b():
        return remote(bsend.at[others, :], brec.at[others, :], b_s, b_r, row=(r + 1) % n)

    def x_copy(h, t):
        return remote(xm.at[h, 1 - bit[h], t], xin.at[t, h], x_s.at[h], x_r.at[t], row=peer[h])

    def x_both(t):
        return remote(xin.at[t], xin.at[t], x_s.at[0], x_r.at[t], row=peer[0])

    def x_all(h):
        return remote(xm.at[h, 1 - bit[h]], xm.at[h, 1 - bit[h]], x_s.at[h], x_r.at[0], row=peer[h])

    def start_x(t):
        for h in range(2):
            x_copy(h, t).start()

    def zx_copy(u):
        return remote(xz.at[1 - odd, u], zin.at[u], zx_s, zx_r.at[u], row=peer[2])

    def p_copy(h):
        return remote(own.at[h, :, c], mate.at[h, :, c], p_s.at[h], p_r.at[h], row=peer[h])

    def c_send(j):
        to = (c + j) % ncol
        return remote(own.at[:, :, c], own.at[:, :, c], c_s.at[j], c_r.at[c], col=to)

    def c_from(j):
        to = (c + j) % ncol
        return remote(own.at[:, :, c], own.at[:, :, to], c_s.at[j], c_r.at[to], col=to)

    def e_send(h, j):
        to = (c + j) % ncol
        return remote(mate.at[h, :, c], mate.at[h, :, c], e_s.at[h, j], e_r.at[h, c], col=to)

    def e_from(h, j):
        to = (c + j) % ncol
        return remote(mate.at[h, :, c], mate.at[h, :, to], e_s.at[h, j], e_r.at[h, to], col=to)

    own_a = pltpu.make_async_copy(asend.at[slot_rows(r), :], arec.at[slot_rows(r), :], l_s.at[0])
    own_a.start()

    @pl.loop(1, n)
    def _(k):
        to_owner(k).start()

    for t in range(AHEAD[0]):
        start_x(t)
    rest.wait()
    for u in range(groups):
        mask_pair(1 - odd, u)
    for u in range(min(PAIR_AHEAD[0], groups)):
        zx_copy(u).start()
    mask_away(AHEAD[0], tiles)

    own_a.wait()
    all_a().wait_recv()

    arrived = arec[...]
    label = arrived[:, part:part + 1].astype(F32)
    ids = lax.broadcasted_iota(jnp.int32, (n * SLOT, BLOCK), 1).astype(F32) + 1.0
    member = jnp.where((label == ids) & (ids <= CONF_DEV), 1.0, 0.0).astype(BF16)
    same = lax.dot_general(member, member, (((1,), (1,)), ((), ())), preferred_element_type=F32)
    counts = jnp.maximum(jnp.sum(same, axis=1, keepdims=True), 1.0)
    same = same.astype(BF16)
    means = jnp.dot(same, arrived, preferred_element_type=F32) / counts
    high = (arrived.astype(F32) - means).astype(BF16)
    low = -(jnp.dot(same, high, preferred_element_type=F32) / counts)
    both = [high.astype(F32)[:, :part], low[:, :part]]
    if bw > 2 * part:
        both.append(jnp.zeros((n * SLOT, bw - 2 * part), F32))
    bsend[...] = jnp.concatenate(both, axis=1).astype(BF16)

    own_b = pltpu.make_async_copy(bsend.at[slot_rows(r), :], brec.at[slot_rows(r), :], l_s.at[1])
    own_b.start()

    @pl.loop(1, n)
    def _(k):
        to_source(k).start()

    for t in range(AHEAD[0], AHEAD[1]):
        start_x(t)
    for u in range(min(PAIR_AHEAD[0], groups), min(PAIR_AHEAD[1], groups)):
        zx_copy(u).start()
    for u in range(groups):
        mask_pair(odd, u)
    for copy in kept:
        copy.wait()

    @pl.loop(0, tiles)
    def _(t):
        for h in range(2):
            mask(h, bit[h], t)

    own_b.wait()
    all_b().wait_recv()

    back = lax.dot_general(brec[...], perm[...], (((0,), (0,)), ((), ())), preferred_element_type=F32)
    for h in range(3):
        for b in range(2):
            for s in range(zs):
                for i in range(2):
                    pieces = []
                    for o in range(2):
                        if h == 2:
                            at = i * part + ((s // 2 * 2 + o) * G + 2 * (s % 2) + b) * pd
                        else:
                            at = i * part + (s * G + (2 * b + o if h == 0 else 2 * o + b)) * pd
                        pieces.append(back[at:at + pd])
                    if pr > 2 * pd:
                        pieces.append(jnp.zeros((pr - 2 * pd, rows), F32))
                    own[h, b, c, s * pr:(s + 1) * pr, i * rows:(i + 1) * rows] = (
                        jnp.concatenate(pieces, axis=0).astype(BF16))
    for h in range(3):
        p_copy(h).start()

    @pl.loop(1, ncol)
    def _(j):
        c_send(j).start()

    for t in range(AHEAD[1], AHEAD[2]):
        start_x(t)
    for u in range(min(PAIR_AHEAD[1], groups), min(PAIR_AHEAD[2], groups)):
        zx_copy(u).start()

    for h in range(3):
        p_copy(h).wait_recv()

        @pl.loop(1, ncol)
        def _(j, h=h):
            e_send(h, j).start()

    @pl.loop(1, ncol)
    def _(j):
        c_from(j).wait_recv()
        for h in range(3):
            e_from(h, j).wait_recv()

    def r_copy(h, t, k):
        return remote(rsend.at[t, k, h], rrec.at[t, k, h], r_s, r_r.at[t, k], row=peer[1 - h])

    def r_both(t, k):
        return remote(rrec.at[t, k], rrec.at[t, k], r_s, r_r.at[t, k], row=peer[0])

    def r_all():
        return remote(rsend, rrec, r_s, r_r.at[0, 0], row=peer[0])

    def start_r(t, k):
        for h in range(2):
            r_copy(h, t, k).start()

    def product(h, b, mine, theirs):
        ours = own[h, b].reshape(line * pr, 2 * rows)
        other = mate[h, b].reshape(line * pr, 2 * rows)
        total = jnp.dot(ours[:, :rows], mine, preferred_element_type=F32)
        total += jnp.dot(ours[:, rows:], mine, preferred_element_type=F32)
        total += jnp.dot(other[:, :rows], theirs, preferred_element_type=F32)
        total += jnp.dot(other[:, rows:], theirs, preferred_element_type=F32)
        return total

    def multiply(t):
        x_both(t).wait_recv()

        def of(h, b):
            return product(h, b, xm[h, bit[h], t], xin[t, h])

        for h in range(2):
            total = of(h, 1 - bit[1 - h]).astype(BF16)
            for k in range(2):
                rsend[t, k, h] = total[k * half * pr:(k + 1) * half * pr]
            r_copy(h, t, far).start()
        for h in range(2):
            total = of(h, bit[1 - h])
            for a in range(line):
                acc[t, a, h] = total[a * pr:(a + 1) * pr]

    def reduce(t, k):
        r_both(t, k).wait_recv()
        for h in range(2):
            for i in range(half):
                acc[t, k * half + i, h] += rrec[t, k, h, i * pr:(i + 1) * pr].astype(F32)

    def up(t, a):
        return remote(zsend.at[t, a], from_low.at[t, a], z_s.at[a], lo_r.at[t, a], row=(r + G) % n)

    def down(t, a):
        return remote(zsend.at[t, a], from_high.at[t, a], z_s.at[a], hi_r.at[t, a], row=(r + n - G) % n)

    def up_last(t):
        return remote(acc.at[t, line - 1], landed.at[t], z_s.at[line - 1], lo_r.at[t, line - 1], row=(r + G) % n)

    def down_last(t):
        return remote(acc.at[t, 0], landed.at[t], z_s.at[0], hi_r.at[t, 0], row=(r + n - G) % n)

    def either(pred, yes, no):
        pl.when(pred)(yes)
        pl.when(jnp.logical_not(pred))(no)

    def take_up(t, a):
        def last():
            up_last(t).wait_recv()
            acc[t, a] += landed[t]

        def other():
            up(t, a).wait_recv()
            acc[t, a] += from_low[t, a].astype(F32)

        @pl.when(z > 0)
        def _():
            either(z == line - 1, last, other)

    def take_down(t, a):
        def last():
            down_last(t).wait_recv()
            acc[t, a] += landed[t]

        def other():
            down(t, a).wait_recv()
            acc[t, a] += from_high[t, a].astype(F32)

        @pl.when(z < line - 1)
        def _():
            either(z == 0, last, other)

    def go_up(t, a):
        take_up(t, a)

        def other():
            zsend[t, a] = acc[t, a].astype(BF16)
            up(t, a).start()

        either(z == line - 2, lambda: up_last(t).start(), other)

    def go_down(t, a):
        take_down(t, a)

        def other():
            zsend[t, a] = acc[t, a].astype(BF16)
            down(t, a).start()

        either(z == 1, lambda: down_last(t).start(), other)

    def forward_far(t):
        @pl.loop(0, half)
        def _(i):
            either(z < half, lambda: go_up(t, line - 1 - i), lambda: go_down(t, i))

    def forward_near(t):
        last = (near + 1) * half - 1

        @pl.loop(0, last - z)
        def _(i):
            go_up(t, last - i)

        @pl.loop(near * half, z)
        def _(a):
            go_down(t, a)

    def cols_of(h, b, t):
        return pl.ds(pl.multiple_of(start_of(h, b) + t * tw, BLOCK), tw)

    def f_copy(h, t):
        return remote(fin.at[t, h, 1 - bit[h]], out.at[:, cols_of(h, bit[h], t)],
                      f_s.at[h], f_r.at[h], row=peer[h])

    def f_own(h, t):
        return pltpu.make_async_copy(fin.at[t, h, bit[h]], out.at[:, cols_of(h, bit[h], t)], g_s.at[h])

    def f_all(h, b):
        area = out.at[:, pl.ds(pl.multiple_of(start_of(h, b), BLOCK), quarter)]
        return remote(area, area, f_s.at[h], f_r.at[h], row=peer[h])

    def g_all(h):
        area = out.at[:, pl.ds(pl.multiple_of(start_of(h, bit[h]), BLOCK), quarter)]
        return pltpu.make_async_copy(area, area, g_s.at[h])

    def finish(t):
        take_up(t, z)
        take_down(t, z)
        for h in range(2):
            total = acc[t, z, h] * factor
            for o in range(2):
                fin[t, h, o] = total[o * pd:(o + 1) * pd]
            f_copy(h, t).start()
            f_own(h, t).start()

    def z1_copy(u, g):
        return remote(z1s.at[u, g], z1r.at[u, g], z1_s, z1_r.at[u], row=peer[g])

    def z2_copy(u, g):
        return remote(z2s.at[u, g], z2r.at[u, g], z2_s, z2_r.at[u], row=peer[1 - g])

    def z3_copy(u, k):
        to = (pair + k) % pairs
        return remote(z3s.at[u, to], z3r.at[u, pair], z3_s, z3_r.at[u], row=(2 * to + odd) * G + q)

    def z3_both(u):
        return remote(z3r.at[u, :pairs - 1], z3r.at[u, :pairs - 1], z3_s, z3_r.at[u], row=peer[0])

    def pair_cols(b, u):
        return pl.ds(pl.multiple_of(pair_start(b, u), BLOCK), 2 * tw)

    def fz_copy(u):
        return remote(fz.at[u, 1 - odd], out.at[:, pair_cols(odd, u)], fz_s, fz_r, row=peer[2])

    def fz_own(u):
        return pltpu.make_async_copy(fz.at[u, odd], out.at[:, pair_cols(odd, u)], gz_s)

    def pair_area(b):
        return out.at[:, pl.ds(pl.multiple_of(pair_start(b, 0), BLOCK), side)]

    def pair_multiply(u):
        zx_copy(u).wait_recv()
        for g in range(2):
            for b in range(2):
                total = product(2, b, xz[odd, u, g], zin[u, g])
                for k in range(pairs):
                    for i in range(2):
                        at = (2 * k + i) * pr
                        zfull[u, g, b, i, k] = total[at:at + pr]
            for i in range(2):
                z1s[u, g, i] = (zfull[u, 0, 1 - bit[0], i] if g == 0 else zfull[u, 1, i, 1 - bit[1]]).astype(BF16)
            z1_copy(u, g).start()

    def pair_first(u):
        remote(z1r.at[u], z1r.at[u], z1_s, z1_r.at[u], row=peer[0]).wait_recv()
        for i in range(2):
            zfull[u, 0, bit[0], i] += z1r[u, 0, i].astype(F32)
            zfull[u, 1, i, bit[1]] += z1r[u, 1, i].astype(F32)
        z2s[u, 0] = zfull[u, 0, bit[0], 1 - bit[1]].astype(BF16)
        z2s[u, 1] = zfull[u, 1, 1 - bit[0], bit[1]].astype(BF16)
        for g in range(2):
            z2_copy(u, g).start()

    def pair_second(u):
        remote(z2r.at[u], z2r.at[u], z2_s, z2_r.at[u], row=peer[0]).wait_recv()
        for g in range(2):
            total = zfull[u, g, bit[0], bit[1]] + z2r[u, g].astype(F32)
            zfull[u, g, bit[0], bit[1]] = total
            for k in range(pairs):
                z3s[u, k, g] = total[k].astype(BF16)

        @pl.loop(1, pairs)
        def _(k):
            z3_copy(u, k).start()

    def pair_finish(u):
        z3_both(u).wait_recv()
        for g in range(2):
            total = zfull[u, g, bit[0], bit[1], pair]
            for k in range(1, pairs):
                total += z3r[u, (pair + k) % pairs, g].astype(F32)
            total = total * factor
            for o in range(2):
                fz[u, o, :, g * tw:(g + 1) * tw] = total[o * pd:(o + 1) * pd]
        fz_copy(u).start()
        fz_own(u).start()

    edge = (z == 0) | (z == line - 1)

    def at(step, lag, act, also=True, count=tiles):
        t = step - lag

        @pl.when((t >= 0) & (t < count) & also)
        def _():
            act(t)

    def step(t, carry):
        at(t, 0, multiply)

        @pl.when(t + AHEAD[2] < tiles)
        def _():
            start_x(t + AHEAD[2])

        @pl.when(t + PAIR_AHEAD[2] < groups)
        def _():
            zx_copy(t + PAIR_AHEAD[2]).start()

        @pl.when((t >= DEFER) & (t < tiles))
        def _():
            start_r(t - DEFER, near)

        @pl.when(t == tiles - 1)
        def _():
            for k in range(tiles - DEFER, tiles):
                start_r(k, near)

        at(t, LAGS[0], lambda k: reduce(k, far))
        at(t, LAGS[0], forward_far, edge)
        at(t, LAGS[1], forward_far, jnp.logical_not(edge))
        at(t, LAGS[2], lambda k: reduce(k, near))
        at(t, LAGS[3], forward_near)
        at(t, LAGS[4], finish)
        for lag, act in zip(PAIR_LAGS, (pair_multiply, pair_first, pair_second, pair_finish)):
            at(t, lag, act, count=groups)
        return carry

    lax.fori_loop(0, tiles + LAGS[4], step, 0)

    for h in range(2):
        f_all(h, 1 - bit[h]).wait_recv()
        f_all(h, bit[h]).wait_send()
        g_all(h).wait()
        x_all(h).wait_send()
        p_copy(h).wait_send()
    p_copy(2).wait_send()
    r_all().wait_send()
    remote(xz.at[1 - odd], xz.at[1 - odd], zx_s, zx_r.at[0], row=peer[2]).wait_send()
    remote(z1s, z1r, z1_s, z1_r.at[0], row=peer[0]).wait_send()
    remote(z2s, z2r, z2_s, z2_r.at[0], row=peer[0]).wait_send()
    remote(z3s.at[:, :pairs - 1], z3r.at[:, :pairs - 1], z3_s, z3_r.at[0], row=peer[0]).wait_send()
    remote(pair_area(odd), pair_area(1 - odd), fz_s, fz_r, row=peer[2]).wait()
    pltpu.make_async_copy(pair_area(odd), pair_area(odd), gz_s).wait()

    @pl.loop(0, line)
    def _(a):
        last = ((z == line - 2) & (a == line - 1)) | ((z == 1) & (a == 0))

        @pl.when(last)
        def _():
            remote(acc.at[:, a], acc.at[:, a], z_s.at[a], lo_r.at[0, 0], row=peer[0]).wait_send()

        @pl.when(jnp.logical_not(last) & (a != z))
        def _():
            remote(zsend.at[:, a], zsend.at[:, a], z_s.at[a], lo_r.at[0, 0], row=peer[0]).wait_send()

    @pl.loop(1, ncol)
    def _(j):
        c_send(j).wait_send()
        for h in range(3):
            e_send(h, j).wait_send()

    all_a().wait_send()
    all_b().wait_send()


def body(descriptors, block_mask, config_of):
    n, ncol = lax.axis_size("row"), lax.axis_size("col")
    rows, width = descriptors.shape
    part = PW // ncol
    wide = -(-(part + 1) // BLOCK) * BLOCK
    bw = -(-2 * part // BLOCK) * BLOCK
    quarter_blocks = width // BLOCK // 5
    tiles = next(k for k in (TILES, 4, 2, 1) if quarter_blocks % k == 0)
    tw = quarter_blocks // tiles * BLOCK
    quarter = quarter_blocks * BLOCK
    groups = (width - 4 * quarter) // (4 * tw)
    line = n // G
    pd = PW // n
    pr = -(-2 * pd // 16) * 16
    zs = line // ncol

    cfg = (n, ncol, rows, width, part, wide, bw, tiles, tw, line, pd, pr, zs, quarter, groups, 1.0 / (rows * n))
    vm = pltpu.VMEM
    dma = pltpu.SemaphoreType.DMA
    hbm = pl.BlockSpec(memory_space=pl.ANY)
    return pl.pallas_call(
        functools.partial(kernel, cfg),
        out_shape=jax.ShapeDtypeStruct((pd, width), F32),
        in_specs=[hbm, hbm, hbm],
        out_specs=hbm,
        scratch_shapes=[
            vm((1, rows), jnp.int32),
            pltpu.SMEM(block_mask.shape, jnp.int32),
            vm((rows, wide), BF16),
            vm((n * SLOT, rows), BF16),
            vm((n * SLOT, wide), BF16),
            vm((n * SLOT, wide), BF16),
            vm((n * SLOT, bw), BF16),
            vm((n * SLOT, bw), BF16),
            vm((rows, width), BF16),
            vm((2, 2, tiles, rows, tw), BF16),
            vm((tiles, 2, rows, tw), BF16),
            vm((3, 2, ncol, zs * pr, 2 * rows), BF16),
            vm((3, 2, ncol, zs * pr, 2 * rows), BF16),
            vm((2, groups, 2, rows, tw), BF16),
            vm((groups, 2, rows, tw), BF16),
            vm((groups, 2, 2, 2, line // 2, pr, tw), F32),
            vm((groups, 2, 2, line // 2, pr, tw), BF16),
            vm((groups, 2, 2, line // 2, pr, tw), BF16),
            vm((groups, 2, line // 2, pr, tw), BF16),
            vm((groups, 2, line // 2, pr, tw), BF16),
            vm((groups, line // 2, 2, pr, tw), BF16),
            vm((groups, line // 2, 2, pr, tw), BF16),
            vm((groups, 2, pd, 2 * tw), F32),
            vm((tiles, line, 2, pr, tw), F32),
            vm((tiles, 2, 2, line // 2 * pr, tw), BF16),
            vm((tiles, 2, 2, line // 2 * pr, tw), BF16),
            vm((tiles, line, 2, pr, tw), BF16),
            vm((tiles, line, 2, pr, tw), BF16),
            vm((tiles, line, 2, pr, tw), BF16),
            vm((tiles, 2, pr, tw), F32),
            vm((tiles, 2, 2, pd, tw), F32),
            dma, dma, dma, dma,
            dma((3,)), dma((3,)), dma((ncol,)), dma((ncol,)), dma((3, ncol)), dma((3, ncol)), dma((9,)),
            dma((2,)), dma((tiles,)), dma, dma((tiles, 2)), dma((line,)), dma((tiles, line)), dma((tiles, line)),
            dma((2,)), dma((2,)), dma((2,)),
            dma, dma((groups,)), dma, dma((groups,)), dma, dma((groups,)), dma, dma((groups,)), dma, dma, dma,
        ],
        compiler_params=pltpu.CompilerParams(
            collective_id=0, has_side_effects=True, vmem_limit_bytes=56 * 1024 * 1024),
    )(config_of[None, :], block_mask, descriptors)


def solution(mesh):
    in_specs = (P("row", "col"), P("row", "col"), P("row"))
    out_specs = P("row", "col")
    return jax.shard_map(body, mesh=mesh, in_specs=in_specs, out_specs=out_specs, check_vma=False)
```

```python
import functools

import jax
import jax.numpy as jnp
from jax import lax
from jax.experimental import pallas as pl
from jax.experimental.pallas import tpu as pltpu
from jax.sharding import PartitionSpec as P

PW = 384
CONF_DEV = 64
BLOCK = 128
G = 4
SLOT = 16
AHEAD = (3, 4, 5)
DEFER = 3
LAGS = (1, 3, 4, 4, 6)
PAIR_AHEAD = (1, 1, 2)
PAIR_LAGS = (2, 3, 4, 6)
F32 = jnp.float32
BF16 = jnp.bfloat16


def remote(src, dst, send, recv, **where):
    return pltpu.make_async_remote_copy(
        src_ref=src, dst_ref=dst, send_sem=send, recv_sem=recv,
        device_id=where, device_id_type=pl.DeviceIdType.MESH,
    )


def kernel(cfg, config_of, block_mask, x, out,
           crow, marks, pext, perm, asend, arec, bsend, brec, xraw, xm, xin, own, mate,
           xz, zin, zfull, z1s, z1r, z2s, z2r, z3s, z3r, fz,
           acc, rsend, rrec, zsend, from_low, from_high, landed, fin,
           a_s, a_r, b_s, b_r, p_s, p_r, c_s, c_r, e_s, e_r, l_s,
           x_s, x_r, r_s, r_r, z_s, lo_r, hi_r, f_s, f_r, g_s,
           zx_s, zx_r, z1_s, z1_r, z2_s, z2_r, z3_s, z3_r, fz_s, fz_r, gz_s):
    n, ncol, rows, width, part, wide, bw, tiles, tw, line, pd, pr, zs, quarter, groups, factor = cfg
    side = (width - 4 * quarter) // 2
    pairs = line // 2
    half = line // 2
    r = lax.axis_index("row")
    c = lax.axis_index("col")
    z = r // G
    q = r % G
    near, far = z // half, 1 - z // half
    pair, odd = z // 2, z % 2
    bit = (q % 2, q // 2)
    peer = tuple(r + (1 - 2 * bit[h]) * (1 << h) for h in range(2)) + (r + (1 - 2 * odd) * G,)

    barrier = pltpu.get_barrier_semaphore()

    @pl.loop(1, n)
    def _(k):
        pl.semaphore_signal(barrier, inc=1, device_id={"row": (r + k) % n}, device_id_type=pl.DeviceIdType.MESH)

    @pl.loop(1, ncol)
    def _(k):
        pl.semaphore_signal(barrier, inc=1, device_id={"col": (c + k) % ncol}, device_id_type=pl.DeviceIdType.MESH)

    crow_copy = pltpu.make_async_copy(config_of, crow, l_s.at[6])
    marks_copy = pltpu.make_async_copy(block_mask, marks, l_s.at[7])
    crow_copy.start()
    marks_copy.start()
    panel_copy = pltpu.make_async_copy(x.at[:, :wide], pext, l_s.at[0])
    panel_copy.start()

    def start_of(h, b):
        return h * 2 * quarter + b * quarter

    def load(h, b, i):
        cols = pl.ds(pl.multiple_of(start_of(h, b), BLOCK), quarter)
        return pltpu.make_async_copy(x.at[:, cols], xraw.at[:, cols], l_s.at[i])

    away = [load(h, 1 - bit[h], 2 + h) for h in range(2)]
    kept = [load(h, bit[h], 4 + h) for h in range(2)]
    rest = pltpu.make_async_copy(x.at[:, 4 * quarter:], xraw.at[:, 4 * quarter:], l_s.at[8])
    for copy in away + [rest] + kept:
        copy.start()

    first = lax.broadcasted_iota(jnp.int32, (rows, rows), 0)
    second = lax.broadcasted_iota(jnp.int32, (rows, rows), 1)
    crow_copy.wait()
    ids_row = jnp.broadcast_to(crow[...], (rows, rows)).astype(F32)
    ids_col = jnp.sum(jnp.where(first == second, ids_row, 0.0), axis=1, keepdims=True).astype(jnp.int32)
    shift = CONF_DEV.bit_length() - 1
    owner = crow[...] >> shift
    before = ((ids_col >> shift) == owner) & (first < second)
    rank = jnp.sum(jnp.where(before, 1.0, 0.0), axis=0, keepdims=True)
    place = owner.astype(F32) * SLOT + rank
    slots = lax.broadcasted_iota(jnp.int32, (n * SLOT, rows), 0).astype(F32)
    perm[...] = jnp.where(slots == place, 1.0, 0.0).astype(BF16)
    label = ((ids_col & (CONF_DEV - 1)) + 1).astype(F32)
    lane = lax.broadcasted_iota(jnp.int32, (BLOCK, BLOCK), 1)
    panel_copy.wait()
    marks_copy.wait()
    for b in range(rows // BLOCK):
        span = slice(b * BLOCK, (b + 1) * BLOCK)
        for w in range(wide // BLOCK):
            cols = slice(w * BLOCK, (w + 1) * BLOCK)
            keep = marks[b, w].astype(F32) if w * BLOCK < part else 0.0
            block = pext[span, cols].astype(F32) * jnp.broadcast_to(keep, (BLOCK, BLOCK))
            if (w + 1) * BLOCK > part:
                block = jnp.where(lane + w * BLOCK < part, block, jnp.broadcast_to(label[span], (BLOCK, BLOCK)))
            pext[span, cols] = block.astype(BF16)
    asend[...] = jnp.dot(perm[...], pext[...], preferred_element_type=F32).astype(BF16)

    def mask_to(dst, base):
        for i in range(rows // BLOCK):
            span = slice(i * BLOCK, (i + 1) * BLOCK)
            for w in range(tw // BLOCK):
                keep = marks[i, base // BLOCK + w].astype(F32)
                cols = pl.ds(pl.multiple_of(base + w * BLOCK, BLOCK), BLOCK)
                dst[span, w * BLOCK:(w + 1) * BLOCK] = (
                    xraw[span, cols] * jnp.broadcast_to(keep, (BLOCK, BLOCK)).astype(BF16))

    def mask(h, b, t):
        mask_to(xm.at[h, b, t], start_of(h, b) + t * tw)

    def pair_start(b, u):
        return 4 * quarter + b * side + u * 2 * tw

    def mask_pair(b, u):
        for g in range(2):
            mask_to(xz.at[b, u, g], pair_start(b, u) + g * tw)

    def mask_away(low, high):
        @pl.loop(low, high)
        def _(t):
            for h in range(2):
                mask(h, 1 - bit[h], t)

    for copy in away:
        copy.wait()
    mask_away(0, AHEAD[0])
    pl.semaphore_wait(barrier, n - 1 + ncol - 1)

    def slot_rows(k):
        return pl.ds(pl.multiple_of(k * SLOT, SLOT), SLOT)

    def to_owner(k):
        to = (r + k) % n
        return remote(asend.at[slot_rows(to), :], arec.at[slot_rows(r), :], a_s, a_r, row=to)

    others = slice(0, (n - 1) * SLOT)

    def all_a():
        return remote(asend.at[others, :], arec.at[others, :], a_s, a_r, row=(r + 1) % n)

    def to_source(k):
        to = (r + k) % n
        return remote(bsend.at[slot_rows(to), :], brec.at[slot_rows(r), :], b_s, b_r, row=to)

    def all_b():
        return remote(bsend.at[others, :], brec.at[others, :], b_s, b_r, row=(r + 1) % n)

    def x_copy(h, t):
        return remote(xm.at[h, 1 - bit[h], t], xin.at[t, h], x_s.at[h], x_r.at[t], row=peer[h])

    def x_both(t):
        return remote(xin.at[t], xin.at[t], x_s.at[0], x_r.at[t], row=peer[0])

    def x_all(h):
        return remote(xm.at[h, 1 - bit[h]], xm.at[h, 1 - bit[h]], x_s.at[h], x_r.at[0], row=peer[h])

    def start_x(t):
        for h in range(2):
            x_copy(h, t).start()

    def zx_copy(u):
        return remote(xz.at[1 - odd, u], zin.at[u], zx_s, zx_r.at[u], row=peer[2])

    def p_copy(h):
        return remote(own.at[h, :, c], mate.at[h, :, c], p_s.at[h], p_r.at[h], row=peer[h])

    def c_send(j):
        to = (c + j) % ncol
        return remote(own.at[:, :, c], own.at[:, :, c], c_s.at[j], c_r.at[c], col=to)

    def c_from(j):
        to = (c + j) % ncol
        return remote(own.at[:, :, c], own.at[:, :, to], c_s.at[j], c_r.at[to], col=to)

    def e_send(h, j):
        to = (c + j) % ncol
        return remote(mate.at[h, :, c], mate.at[h, :, c], e_s.at[h, j], e_r.at[h, c], col=to)

    def e_from(h, j):
        to = (c + j) % ncol
        return remote(mate.at[h, :, c], mate.at[h, :, to], e_s.at[h, j], e_r.at[h, to], col=to)

    own_a = pltpu.make_async_copy(asend.at[slot_rows(r), :], arec.at[slot_rows(r), :], l_s.at[0])
    own_a.start()

    @pl.loop(1, n)
    def _(k):
        to_owner(k).start()

    for t in range(AHEAD[0]):
        start_x(t)
    rest.wait()
    for u in range(groups):
        mask_pair(1 - odd, u)
    for u in range(min(PAIR_AHEAD[0], groups)):
        zx_copy(u).start()
    mask_away(AHEAD[0], tiles)

    own_a.wait()
    all_a().wait_recv()

    arrived = arec[...]
    label = arrived[:, part:part + 1].astype(F32)
    ids = lax.broadcasted_iota(jnp.int32, (n * SLOT, BLOCK), 1).astype(F32) + 1.0
    member = jnp.where((label == ids) & (ids <= CONF_DEV), 1.0, 0.0).astype(BF16)
    same = lax.dot_general(member, member, (((1,), (1,)), ((), ())), preferred_element_type=F32)
    counts = jnp.maximum(jnp.sum(same, axis=1, keepdims=True), 1.0)
    same = same.astype(BF16)
    means = jnp.dot(same, arrived, preferred_element_type=F32) / counts
    high = (arrived.astype(F32) - means).astype(BF16)
    low = -(jnp.dot(same, high, preferred_element_type=F32) / counts)
    both = [high.astype(F32)[:, :part], low[:, :part]]
    if bw > 2 * part:
        both.append(jnp.zeros((n * SLOT, bw - 2 * part), F32))
    bsend[...] = jnp.concatenate(both, axis=1).astype(BF16)

    own_b = pltpu.make_async_copy(bsend.at[slot_rows(r), :], brec.at[slot_rows(r), :], l_s.at[1])
    own_b.start()

    @pl.loop(1, n)
    def _(k):
        to_source(k).start()

    for t in range(AHEAD[0], AHEAD[1]):
        start_x(t)
    for u in range(min(PAIR_AHEAD[0], groups), min(PAIR_AHEAD[1], groups)):
        zx_copy(u).start()
    for u in range(groups):
        mask_pair(odd, u)
    for copy in kept:
        copy.wait()

    @pl.loop(0, tiles)
    def _(t):
        for h in range(2):
            mask(h, bit[h], t)

    own_b.wait()
    all_b().wait_recv()

    back = lax.dot_general(brec[...], perm[...], (((0,), (0,)), ((), ())), preferred_element_type=F32)
    for h in range(3):
        for b in range(2):
            for s in range(zs):
                for i in range(2):
                    pieces = []
                    for o in range(2):
                        if h == 2:
                            at = i * part + ((s // 2 * 2 + o) * G + 2 * (s % 2) + b) * pd
                        else:
                            at = i * part + (s * G + (2 * b + o if h == 0 else 2 * o + b)) * pd
                        pieces.append(back[at:at + pd])
                    if pr > 2 * pd:
                        pieces.append(jnp.zeros((pr - 2 * pd, rows), F32))
                    own[h, b, c, s * pr:(s + 1) * pr, i * rows:(i + 1) * rows] = (
                        jnp.concatenate(pieces, axis=0).astype(BF16))
    for h in range(3):
        p_copy(h).start()

    @pl.loop(1, ncol)
    def _(j):
        c_send(j).start()

    for t in range(AHEAD[1], AHEAD[2]):
        start_x(t)
    for u in range(min(PAIR_AHEAD[1], groups), min(PAIR_AHEAD[2], groups)):
        zx_copy(u).start()

    def relay(h):
        p_copy(h).wait_recv()

        @pl.loop(1, ncol)
        def _(j):
            e_send(h, j).start()

    def relayed(h):
        @pl.loop(1, ncol)
        def _(j):
            e_from(h, j).wait_recv()

    for h in range(2):
        relay(h)

    @pl.loop(1, ncol)
    def _(j):
        c_from(j).wait_recv()

    for h in range(2):
        relayed(h)

    def r_copy(h, t, k):
        return remote(rsend.at[t, k, h], rrec.at[t, k, h], r_s, r_r.at[t, k], row=peer[1 - h])

    def r_both(t, k):
        return remote(rrec.at[t, k], rrec.at[t, k], r_s, r_r.at[t, k], row=peer[0])

    def r_all():
        return remote(rsend, rrec, r_s, r_r.at[0, 0], row=peer[0])

    def start_r(t, k):
        for h in range(2):
            r_copy(h, t, k).start()

    def product(h, b, mine, theirs):
        ours = own[h, b].reshape(line * pr, 2 * rows)
        other = mate[h, b].reshape(line * pr, 2 * rows)
        total = jnp.dot(ours[:, :rows], mine, preferred_element_type=F32)
        total += jnp.dot(ours[:, rows:], mine, preferred_element_type=F32)
        total += jnp.dot(other[:, :rows], theirs, preferred_element_type=F32)
        total += jnp.dot(other[:, rows:], theirs, preferred_element_type=F32)
        return total

    def multiply(t):
        x_both(t).wait_recv()

        def of(h, b):
            return product(h, b, xm[h, bit[h], t], xin[t, h])

        for h in range(2):
            total = of(h, 1 - bit[1 - h]).astype(BF16)
            for k in range(2):
                rsend[t, k, h] = total[k * half * pr:(k + 1) * half * pr]
            r_copy(h, t, far).start()
        for h in range(2):
            total = of(h, bit[1 - h])
            for a in range(line):
                acc[t, a, h] = total[a * pr:(a + 1) * pr]

    def reduce(t, k):
        r_both(t, k).wait_recv()
        for h in range(2):
            for i in range(half):
                acc[t, k * half + i, h] += rrec[t, k, h, i * pr:(i + 1) * pr].astype(F32)

    def up(t, a):
        return remote(zsend.at[t, a], from_low.at[t, a], z_s.at[a], lo_r.at[t, a], row=(r + G) % n)

    def down(t, a):
        return remote(zsend.at[t, a], from_high.at[t, a], z_s.at[a], hi_r.at[t, a], row=(r + n - G) % n)

    def up_last(t):
        return remote(acc.at[t, line - 1], landed.at[t], z_s.at[line - 1], lo_r.at[t, line - 1], row=(r + G) % n)

    def down_last(t):
        return remote(acc.at[t, 0], landed.at[t], z_s.at[0], hi_r.at[t, 0], row=(r + n - G) % n)

    def either(pred, yes, no):
        pl.when(pred)(yes)
        pl.when(jnp.logical_not(pred))(no)

    def take_up(t, a):
        def last():
            up_last(t).wait_recv()
            acc[t, a] += landed[t]

        def other():
            up(t, a).wait_recv()
            acc[t, a] += from_low[t, a].astype(F32)

        @pl.when(z > 0)
        def _():
            either(z == line - 1, last, other)

    def take_down(t, a):
        def last():
            down_last(t).wait_recv()
            acc[t, a] += landed[t]

        def other():
            down(t, a).wait_recv()
            acc[t, a] += from_high[t, a].astype(F32)

        @pl.when(z < line - 1)
        def _():
            either(z == 0, last, other)

    def go_up(t, a):
        take_up(t, a)

        def other():
            zsend[t, a] = acc[t, a].astype(BF16)
            up(t, a).start()

        either(z == line - 2, lambda: up_last(t).start(), other)

    def go_down(t, a):
        take_down(t, a)

        def other():
            zsend[t, a] = acc[t, a].astype(BF16)
            down(t, a).start()

        either(z == 1, lambda: down_last(t).start(), other)

    def forward_far(t):
        @pl.loop(0, half)
        def _(i):
            either(z < half, lambda: go_up(t, line - 1 - i), lambda: go_down(t, i))

    def forward_near(t):
        last = (near + 1) * half - 1

        @pl.loop(0, last - z)
        def _(i):
            go_up(t, last - i)

        @pl.loop(near * half, z)
        def _(a):
            go_down(t, a)

    def cols_of(h, b, t):
        return pl.ds(pl.multiple_of(start_of(h, b) + t * tw, BLOCK), tw)

    def f_copy(h, t):
        return remote(fin.at[t, h, 1 - bit[h]], out.at[:, cols_of(h, bit[h], t)],
                      f_s.at[h], f_r.at[h], row=peer[h])

    def f_own(h, t):
        return pltpu.make_async_copy(fin.at[t, h, bit[h]], out.at[:, cols_of(h, bit[h], t)], g_s.at[h])

    def f_all(h, b):
        area = out.at[:, pl.ds(pl.multiple_of(start_of(h, b), BLOCK), quarter)]
        return remote(area, area, f_s.at[h], f_r.at[h], row=peer[h])

    def g_all(h):
        area = out.at[:, pl.ds(pl.multiple_of(start_of(h, bit[h]), BLOCK), quarter)]
        return pltpu.make_async_copy(area, area, g_s.at[h])

    def finish(t):
        take_up(t, z)
        take_down(t, z)
        for h in range(2):
            total = acc[t, z, h] * factor
            for o in range(2):
                fin[t, h, o] = total[o * pd:(o + 1) * pd]
            f_copy(h, t).start()
            f_own(h, t).start()

    def z1_copy(u, g):
        return remote(z1s.at[u, g], z1r.at[u, g], z1_s, z1_r.at[u], row=peer[g])

    def z2_copy(u, g):
        return remote(z2s.at[u, g], z2r.at[u, g], z2_s, z2_r.at[u], row=peer[1 - g])

    def z3_copy(u, k):
        to = (pair + k) % pairs
        return remote(z3s.at[u, to], z3r.at[u, pair], z3_s, z3_r.at[u], row=(2 * to + odd) * G + q)

    def z3_both(u):
        return remote(z3r.at[u, :pairs - 1], z3r.at[u, :pairs - 1], z3_s, z3_r.at[u], row=peer[0])

    def pair_cols(b, u):
        return pl.ds(pl.multiple_of(pair_start(b, u), BLOCK), 2 * tw)

    def fz_copy(u):
        return remote(fz.at[u, 1 - odd], out.at[:, pair_cols(odd, u)], fz_s, fz_r, row=peer[2])

    def fz_own(u):
        return pltpu.make_async_copy(fz.at[u, odd], out.at[:, pair_cols(odd, u)], gz_s)

    def pair_area(b):
        return out.at[:, pl.ds(pl.multiple_of(pair_start(b, 0), BLOCK), side)]

    def pair_multiply(u):
        zx_copy(u).wait_recv()
        for g in range(2):
            for b in range(2):
                total = product(2, b, xz[odd, u, g], zin[u, g])
                for k in range(pairs):
                    for i in range(2):
                        at = (2 * k + i) * pr
                        zfull[u, g, b, i, k] = total[at:at + pr]
            for i in range(2):
                z1s[u, g, i] = (zfull[u, 0, 1 - bit[0], i] if g == 0 else zfull[u, 1, i, 1 - bit[1]]).astype(BF16)
            z1_copy(u, g).start()

    def pair_first(u):
        remote(z1r.at[u], z1r.at[u], z1_s, z1_r.at[u], row=peer[0]).wait_recv()
        for i in range(2):
            zfull[u, 0, bit[0], i] += z1r[u, 0, i].astype(F32)
            zfull[u, 1, i, bit[1]] += z1r[u, 1, i].astype(F32)
        z2s[u, 0] = zfull[u, 0, bit[0], 1 - bit[1]].astype(BF16)
        z2s[u, 1] = zfull[u, 1, 1 - bit[0], bit[1]].astype(BF16)
        for g in range(2):
            z2_copy(u, g).start()

    def pair_second(u):
        remote(z2r.at[u], z2r.at[u], z2_s, z2_r.at[u], row=peer[0]).wait_recv()
        for g in range(2):
            total = zfull[u, g, bit[0], bit[1]] + z2r[u, g].astype(F32)
            zfull[u, g, bit[0], bit[1]] = total
            for k in range(pairs):
                z3s[u, k, g] = total[k].astype(BF16)

        @pl.loop(1, pairs)
        def _(k):
            z3_copy(u, k).start()

    def pair_finish(u):
        z3_both(u).wait_recv()
        for g in range(2):
            total = zfull[u, g, bit[0], bit[1], pair]
            for k in range(1, pairs):
                total += z3r[u, (pair + k) % pairs, g].astype(F32)
            total = total * factor
            for o in range(2):
                fz[u, o, :, g * tw:(g + 1) * tw] = total[o * pd:(o + 1) * pd]
        fz_copy(u).start()
        fz_own(u).start()

    edge = (z == 0) | (z == line - 1)

    def at(step, lag, act, also=True, count=tiles):
        t = step - lag

        @pl.when((t >= 0) & (t < count) & also)
        def _():
            act(t)

    def step(t, carry):
        at(t, 0, multiply)

        @pl.when(t + AHEAD[2] < tiles)
        def _():
            start_x(t + AHEAD[2])

        @pl.when(t + PAIR_AHEAD[2] < groups)
        def _():
            zx_copy(t + PAIR_AHEAD[2]).start()

        @pl.when((t >= DEFER) & (t < tiles))
        def _():
            start_r(t - DEFER, near)

        @pl.when(t == tiles - 1)
        def _():
            for k in range(tiles - DEFER, tiles):
                start_r(k, near)

        at(t, LAGS[0], lambda k: reduce(k, far))
        at(t, LAGS[0], forward_far, edge)
        at(t, LAGS[1], forward_far, jnp.logical_not(edge))
        at(t, LAGS[2], lambda k: reduce(k, near))
        at(t, LAGS[3], forward_near)
        at(t, LAGS[4], finish)
        at(t, PAIR_LAGS[0] - 1, lambda k: relay(2), count=1)
        at(t, PAIR_LAGS[0], lambda k: relayed(2), count=1)
        for lag, act in zip(PAIR_LAGS, (pair_multiply, pair_first, pair_second, pair_finish)):
            at(t, lag, act, count=groups)
        return carry

    lax.fori_loop(0, tiles + LAGS[4], step, 0)

    for h in range(2):
        f_all(h, 1 - bit[h]).wait_recv()
        f_all(h, bit[h]).wait_send()
        g_all(h).wait()
        x_all(h).wait_send()
        p_copy(h).wait_send()
    p_copy(2).wait_send()
    r_all().wait_send()
    remote(xz.at[1 - odd], xz.at[1 - odd], zx_s, zx_r.at[0], row=peer[2]).wait_send()
    remote(z1s, z1r, z1_s, z1_r.at[0], row=peer[0]).wait_send()
    remote(z2s, z2r, z2_s, z2_r.at[0], row=peer[0]).wait_send()
    remote(z3s.at[:, :pairs - 1], z3r.at[:, :pairs - 1], z3_s, z3_r.at[0], row=peer[0]).wait_send()
    remote(pair_area(odd), pair_area(1 - odd), fz_s, fz_r, row=peer[2]).wait()
    pltpu.make_async_copy(pair_area(odd), pair_area(odd), gz_s).wait()

    @pl.loop(0, line)
    def _(a):
        last = ((z == line - 2) & (a == line - 1)) | ((z == 1) & (a == 0))

        @pl.when(last)
        def _():
            remote(acc.at[:, a], acc.at[:, a], z_s.at[a], lo_r.at[0, 0], row=peer[0]).wait_send()

        @pl.when(jnp.logical_not(last) & (a != z))
        def _():
            remote(zsend.at[:, a], zsend.at[:, a], z_s.at[a], lo_r.at[0, 0], row=peer[0]).wait_send()

    @pl.loop(1, ncol)
    def _(j):
        c_send(j).wait_send()
        for h in range(3):
            e_send(h, j).wait_send()

    all_a().wait_send()
    all_b().wait_send()


def body(descriptors, block_mask, config_of):
    n, ncol = lax.axis_size("row"), lax.axis_size("col")
    rows, width = descriptors.shape
    part = PW // ncol
    wide = -(-(part + 1) // BLOCK) * BLOCK
    bw = -(-2 * part // BLOCK) * BLOCK
    blocks = width // BLOCK
    quarter_blocks = blocks * 7 // 40
    per = next(k for k in (2, 1) if quarter_blocks % k == 0 and (blocks - 4 * quarter_blocks) % (4 * k) == 0)
    tiles = quarter_blocks // per
    tw = quarter_blocks // tiles * BLOCK
    quarter = quarter_blocks * BLOCK
    groups = (width - 4 * quarter) // (4 * tw)
    line = n // G
    pd = PW // n
    pr = -(-2 * pd // 16) * 16
    zs = line // ncol

    cfg = (n, ncol, rows, width, part, wide, bw, tiles, tw, line, pd, pr, zs, quarter, groups, 1.0 / (rows * n))
    vm = pltpu.VMEM
    dma = pltpu.SemaphoreType.DMA
    hbm = pl.BlockSpec(memory_space=pl.ANY)
    return pl.pallas_call(
        functools.partial(kernel, cfg),
        out_shape=jax.ShapeDtypeStruct((pd, width), F32),
        in_specs=[hbm, hbm, hbm],
        out_specs=hbm,
        scratch_shapes=[
            vm((1, rows), jnp.int32),
            pltpu.SMEM(block_mask.shape, jnp.int32),
            vm((rows, wide), BF16),
            vm((n * SLOT, rows), BF16),
            vm((n * SLOT, wide), BF16),
            vm((n * SLOT, wide), BF16),
            vm((n * SLOT, bw), BF16),
            vm((n * SLOT, bw), BF16),
            vm((rows, width), BF16),
            vm((2, 2, tiles, rows, tw), BF16),
            vm((tiles, 2, rows, tw), BF16),
            vm((3, 2, ncol, zs * pr, 2 * rows), BF16),
            vm((3, 2, ncol, zs * pr, 2 * rows), BF16),
            vm((2, groups, 2, rows, tw), BF16),
            vm((groups, 2, rows, tw), BF16),
            vm((groups, 2, 2, 2, line // 2, pr, tw), F32),
            vm((groups, 2, 2, line // 2, pr, tw), BF16),
            vm((groups, 2, 2, line // 2, pr, tw), BF16),
            vm((groups, 2, line // 2, pr, tw), BF16),
            vm((groups, 2, line // 2, pr, tw), BF16),
            vm((groups, line // 2, 2, pr, tw), BF16),
            vm((groups, line // 2, 2, pr, tw), BF16),
            vm((groups, 2, pd, 2 * tw), F32),
            vm((tiles, line, 2, pr, tw), F32),
            vm((tiles, 2, 2, line // 2 * pr, tw), BF16),
            vm((tiles, 2, 2, line // 2 * pr, tw), BF16),
            vm((tiles, line, 2, pr, tw), BF16),
            vm((tiles, line, 2, pr, tw), BF16),
            vm((tiles, line, 2, pr, tw), BF16),
            vm((tiles, 2, pr, tw), F32),
            vm((tiles, 2, 2, pd, tw), F32),
            dma, dma, dma, dma,
            dma((3,)), dma((3,)), dma((ncol,)), dma((ncol,)), dma((3, ncol)), dma((3, ncol)), dma((9,)),
            dma((2,)), dma((tiles,)), dma, dma((tiles, 2)), dma((line,)), dma((tiles, line)), dma((tiles, line)),
            dma((2,)), dma((2,)), dma((2,)),
            dma, dma((groups,)), dma, dma((groups,)), dma, dma((groups,)), dma, dma((groups,)), dma, dma, dma,
        ],
        compiler_params=pltpu.CompilerParams(
            collective_id=0, has_side_effects=True, vmem_limit_bytes=56 * 1024 * 1024),
    )(config_of[None, :], block_mask, descriptors)


def solution(mesh):
    in_specs = (P("row", "col"), P("row", "col"), P("row"))
    out_specs = P("row", "col")
    return jax.shard_map(body, mesh=mesh, in_specs=in_specs, out_specs=out_specs, check_vma=False)
```

```python
import functools

import jax
import jax.numpy as jnp
from jax import lax
from jax.experimental import pallas as pl
from jax.experimental.pallas import tpu as pltpu
from jax.sharding import PartitionSpec as P

PW = 384
CONF_DEV = 64
BLOCK = 128
G = 4
SLOT = 16
AHEAD = (3, 4, 5)
DEFER = 2
LAGS = (1, 2, 3, 3, 5)
PAIR_AHEAD = (1, 1, 2)
PAIR_LAGS = (2, 3, 4, 6)
F32 = jnp.float32
BF16 = jnp.bfloat16


def remote(src, dst, send, recv, **where):
    return pltpu.make_async_remote_copy(
        src_ref=src, dst_ref=dst, send_sem=send, recv_sem=recv,
        device_id=where, device_id_type=pl.DeviceIdType.MESH,
    )


def kernel(cfg, config_of, block_mask, x, out,
           crow, marks, pext, perm, asend, arec, bsend, brec, xraw, xm, xin, own, mate,
           xz, zin, zfull, z1s, z1r, z2s, z2r, z3s, z3r, fz,
           acc, rsend, rrec, zsend, from_low, from_high, landed, fin,
           a_s, a_r, b_s, b_r, p_s, p_r, c_s, c_r, e_s, e_r, l_s,
           x_s, x_r, r_s, r_r, z_s, lo_r, hi_r, f_s, f_r, g_s,
           zx_s, zx_r, z1_s, z1_r, z2_s, z2_r, z3_s, z3_r, fz_s, fz_r, gz_s):
    n, ncol, rows, width, part, wide, bw, tiles, tw, line, pd, pr, zs, quarter, groups, factor = cfg
    side = (width - 4 * quarter) // 2
    pairs = line // 2
    half = line // 2
    r = lax.axis_index("row")
    c = lax.axis_index("col")
    z = r // G
    q = r % G
    near, far = z // half, 1 - z // half
    pair, odd = z // 2, z % 2
    bit = (q % 2, q // 2)
    peer = tuple(r + (1 - 2 * bit[h]) * (1 << h) for h in range(2)) + (r + (1 - 2 * odd) * G,)

    barrier = pltpu.get_barrier_semaphore()

    @pl.loop(1, n)
    def _(k):
        pl.semaphore_signal(barrier, inc=1, device_id={"row": (r + k) % n}, device_id_type=pl.DeviceIdType.MESH)

    @pl.loop(1, ncol)
    def _(k):
        pl.semaphore_signal(barrier, inc=1, device_id={"col": (c + k) % ncol}, device_id_type=pl.DeviceIdType.MESH)

    crow_copy = pltpu.make_async_copy(config_of, crow, l_s.at[6])
    marks_copy = pltpu.make_async_copy(block_mask, marks, l_s.at[7])
    crow_copy.start()
    marks_copy.start()
    panel_copy = pltpu.make_async_copy(x.at[:, :wide], pext, l_s.at[0])
    panel_copy.start()

    def start_of(h, b):
        return h * 2 * quarter + b * quarter

    def load(h, b, i):
        cols = pl.ds(pl.multiple_of(start_of(h, b), BLOCK), quarter)
        return pltpu.make_async_copy(x.at[:, cols], xraw.at[:, cols], l_s.at[i])

    away = [load(h, 1 - bit[h], 2 + h) for h in range(2)]
    kept = [load(h, bit[h], 4 + h) for h in range(2)]
    rest = pltpu.make_async_copy(x.at[:, 4 * quarter:], xraw.at[:, 4 * quarter:], l_s.at[8])
    for copy in away + [rest] + kept:
        copy.start()

    first = lax.broadcasted_iota(jnp.int32, (rows, rows), 0)
    second = lax.broadcasted_iota(jnp.int32, (rows, rows), 1)
    crow_copy.wait()
    ids_row = jnp.broadcast_to(crow[...], (rows, rows)).astype(F32)
    ids_col = jnp.sum(jnp.where(first == second, ids_row, 0.0), axis=1, keepdims=True).astype(jnp.int32)
    shift = CONF_DEV.bit_length() - 1
    owner = crow[...] >> shift
    before = ((ids_col >> shift) == owner) & (first < second)
    rank = jnp.sum(jnp.where(before, 1.0, 0.0), axis=0, keepdims=True)
    place = owner.astype(F32) * SLOT + rank
    slots = lax.broadcasted_iota(jnp.int32, (n * SLOT, rows), 0).astype(F32)
    perm[...] = jnp.where(slots == place, 1.0, 0.0).astype(BF16)
    label = ((ids_col & (CONF_DEV - 1)) + 1).astype(F32)
    lane = lax.broadcasted_iota(jnp.int32, (BLOCK, BLOCK), 1)
    panel_copy.wait()
    marks_copy.wait()
    for b in range(rows // BLOCK):
        span = slice(b * BLOCK, (b + 1) * BLOCK)
        for w in range(wide // BLOCK):
            cols = slice(w * BLOCK, (w + 1) * BLOCK)
            keep = marks[b, w].astype(F32) if w * BLOCK < part else 0.0
            block = pext[span, cols].astype(F32) * jnp.broadcast_to(keep, (BLOCK, BLOCK))
            if (w + 1) * BLOCK > part:
                block = jnp.where(lane + w * BLOCK < part, block, jnp.broadcast_to(label[span], (BLOCK, BLOCK)))
            pext[span, cols] = block.astype(BF16)
    asend[...] = jnp.dot(perm[...], pext[...], preferred_element_type=F32).astype(BF16)

    def mask_to(dst, base):
        for i in range(rows // BLOCK):
            span = slice(i * BLOCK, (i + 1) * BLOCK)
            for w in range(tw // BLOCK):
                keep = marks[i, base // BLOCK + w].astype(F32)
                cols = pl.ds(pl.multiple_of(base + w * BLOCK, BLOCK), BLOCK)
                dst[span, w * BLOCK:(w + 1) * BLOCK] = (
                    xraw[span, cols] * jnp.broadcast_to(keep, (BLOCK, BLOCK)).astype(BF16))

    def mask(h, b, t):
        mask_to(xm.at[h, b, t], start_of(h, b) + t * tw)

    def pair_start(b, u):
        return 4 * quarter + b * side + u * 2 * tw

    def mask_pair(b, u):
        for g in range(2):
            mask_to(xz.at[b, u, g], pair_start(b, u) + g * tw)

    def mask_away(low, high):
        @pl.loop(low, high)
        def _(t):
            for h in range(2):
                mask(h, 1 - bit[h], t)

    for copy in away:
        copy.wait()
    mask_away(0, AHEAD[0])
    pl.semaphore_wait(barrier, n - 1 + ncol - 1)

    def slot_rows(k):
        return pl.ds(pl.multiple_of(k * SLOT, SLOT), SLOT)

    def to_owner(k):
        to = (r + k) % n
        return remote(asend.at[slot_rows(to), :], arec.at[slot_rows(r), :], a_s, a_r, row=to)

    others = slice(0, (n - 1) * SLOT)

    def all_a():
        return remote(asend.at[others, :], arec.at[others, :], a_s, a_r, row=(r + 1) % n)

    def to_source(k):
        to = (r + k) % n
        return remote(bsend.at[slot_rows(to), :], brec.at[slot_rows(r), :], b_s, b_r, row=to)

    def all_b():
        return remote(bsend.at[others, :], brec.at[others, :], b_s, b_r, row=(r + 1) % n)

    def x_copy(h, t):
        return remote(xm.at[h, 1 - bit[h], t], xin.at[t, h], x_s.at[h], x_r.at[t], row=peer[h])

    def x_both(t):
        return remote(xin.at[t], xin.at[t], x_s.at[0], x_r.at[t], row=peer[0])

    def x_all(h):
        return remote(xm.at[h, 1 - bit[h]], xm.at[h, 1 - bit[h]], x_s.at[h], x_r.at[0], row=peer[h])

    def start_x(t):
        for h in range(2):
            x_copy(h, t).start()

    def zx_copy(u):
        return remote(xz.at[1 - odd, u], zin.at[u], zx_s, zx_r.at[u], row=peer[2])

    def p_copy(h):
        return remote(own.at[h, :, c], mate.at[h, :, c], p_s.at[h], p_r.at[h], row=peer[h])

    def c_send(j):
        to = (c + j) % ncol
        return remote(own.at[:, :, c], own.at[:, :, c], c_s.at[j], c_r.at[c], col=to)

    def c_from(j):
        to = (c + j) % ncol
        return remote(own.at[:, :, c], own.at[:, :, to], c_s.at[j], c_r.at[to], col=to)

    def e_send(h, j):
        to = (c + j) % ncol
        return remote(mate.at[h, :, c], mate.at[h, :, c], e_s.at[h, j], e_r.at[h, c], col=to)

    def e_from(h, j):
        to = (c + j) % ncol
        return remote(mate.at[h, :, c], mate.at[h, :, to], e_s.at[h, j], e_r.at[h, to], col=to)

    own_a = pltpu.make_async_copy(asend.at[slot_rows(r), :], arec.at[slot_rows(r), :], l_s.at[0])
    own_a.start()

    @pl.loop(1, n)
    def _(k):
        to_owner(k).start()

    for t in range(AHEAD[0]):
        start_x(t)
    rest.wait()
    for u in range(groups):
        mask_pair(1 - odd, u)
    for u in range(min(PAIR_AHEAD[0], groups)):
        zx_copy(u).start()
    mask_away(AHEAD[0], tiles)

    own_a.wait()
    all_a().wait_recv()

    arrived = arec[...]
    label = arrived[:, part:part + 1].astype(F32)
    ids = lax.broadcasted_iota(jnp.int32, (n * SLOT, BLOCK), 1).astype(F32) + 1.0
    member = jnp.where((label == ids) & (ids <= CONF_DEV), 1.0, 0.0).astype(BF16)
    same = lax.dot_general(member, member, (((1,), (1,)), ((), ())), preferred_element_type=F32)
    counts = jnp.maximum(jnp.sum(same, axis=1, keepdims=True), 1.0)
    same = same.astype(BF16)
    means = jnp.dot(same, arrived, preferred_element_type=F32) / counts
    high = (arrived.astype(F32) - means).astype(BF16)
    low = -(jnp.dot(same, high, preferred_element_type=F32) / counts)
    both = [high.astype(F32)[:, :part], low[:, :part]]
    if bw > 2 * part:
        both.append(jnp.zeros((n * SLOT, bw - 2 * part), F32))
    bsend[...] = jnp.concatenate(both, axis=1).astype(BF16)

    own_b = pltpu.make_async_copy(bsend.at[slot_rows(r), :], brec.at[slot_rows(r), :], l_s.at[1])
    own_b.start()

    @pl.loop(1, n)
    def _(k):
        to_source(k).start()

    for t in range(AHEAD[0], AHEAD[1]):
        start_x(t)
    for u in range(min(PAIR_AHEAD[0], groups), min(PAIR_AHEAD[1], groups)):
        zx_copy(u).start()
    for u in range(groups):
        mask_pair(odd, u)
    for copy in kept:
        copy.wait()

    @pl.loop(0, tiles)
    def _(t):
        for h in range(2):
            mask(h, bit[h], t)

    own_b.wait()
    all_b().wait_recv()

    back = lax.dot_general(brec[...], perm[...], (((0,), (0,)), ((), ())), preferred_element_type=F32)
    for h in range(3):
        for b in range(2):
            for s in range(zs):
                for i in range(2):
                    pieces = []
                    for o in range(2):
                        if h == 2:
                            at = i * part + ((s // 2 * 2 + o) * G + 2 * (s % 2) + b) * pd
                        else:
                            at = i * part + (s * G + (2 * b + o if h == 0 else 2 * o + b)) * pd
                        pieces.append(back[at:at + pd])
                    if pr > 2 * pd:
                        pieces.append(jnp.zeros((pr - 2 * pd, rows), F32))
                    own[h, b, c, s * pr:(s + 1) * pr, i * rows:(i + 1) * rows] = (
                        jnp.concatenate(pieces, axis=0).astype(BF16))
    for h in range(3):
        p_copy(h).start()

    @pl.loop(1, ncol)
    def _(j):
        c_send(j).start()

    for t in range(AHEAD[1], AHEAD[2]):
        start_x(t)
    for u in range(min(PAIR_AHEAD[1], groups), min(PAIR_AHEAD[2], groups)):
        zx_copy(u).start()

    def relay(h):
        p_copy(h).wait_recv()

        @pl.loop(1, ncol)
        def _(j):
            e_send(h, j).start()

    def relayed(h):
        @pl.loop(1, ncol)
        def _(j):
            e_from(h, j).wait_recv()

    for h in range(2):
        relay(h)

    @pl.loop(1, ncol)
    def _(j):
        c_from(j).wait_recv()

    for h in range(2):
        relayed(h)

    def r_copy(h, t, k):
        return remote(rsend.at[t, k, h], rrec.at[t, k, h], r_s, r_r.at[t, k], row=peer[1 - h])

    def r_both(t, k):
        return remote(rrec.at[t, k], rrec.at[t, k], r_s, r_r.at[t, k], row=peer[0])

    def r_all():
        return remote(rsend, rrec, r_s, r_r.at[0, 0], row=peer[0])

    def start_r(t, k):
        for h in range(2):
            r_copy(h, t, k).start()

    def product(h, b, mine, theirs):
        ours = own[h, b].reshape(line * pr, 2 * rows)
        other = mate[h, b].reshape(line * pr, 2 * rows)
        left = jnp.concatenate([ours, other], axis=1)
        right = jnp.concatenate([mine, mine, theirs, theirs], axis=0)
        return jnp.dot(left, right, preferred_element_type=F32)

    def multiply(t):
        x_both(t).wait_recv()

        def of(h, b):
            return product(h, b, xm[h, bit[h], t], xin[t, h])

        for h in range(2):
            total = of(h, 1 - bit[1 - h]).astype(BF16)
            for k in range(2):
                rsend[t, k, h] = total[k * half * pr:(k + 1) * half * pr]
            r_copy(h, t, far).start()
        for h in range(2):
            total = of(h, bit[1 - h])
            for a in range(line):
                acc[t, a, h] = total[a * pr:(a + 1) * pr]

    def reduce(t, k):
        r_both(t, k).wait_recv()
        for h in range(2):
            for i in range(half):
                acc[t, k * half + i, h] += rrec[t, k, h, i * pr:(i + 1) * pr].astype(F32)

    def up(t, a):
        return remote(zsend.at[t, a], from_low.at[t, a], z_s.at[a], lo_r.at[t, a], row=(r + G) % n)

    def down(t, a):
        return remote(zsend.at[t, a], from_high.at[t, a], z_s.at[a], hi_r.at[t, a], row=(r + n - G) % n)

    def up_last(t):
        return remote(acc.at[t, line - 1], landed.at[t], z_s.at[line - 1], lo_r.at[t, line - 1], row=(r + G) % n)

    def down_last(t):
        return remote(acc.at[t, 0], landed.at[t], z_s.at[0], hi_r.at[t, 0], row=(r + n - G) % n)

    def either(pred, yes, no):
        pl.when(pred)(yes)
        pl.when(jnp.logical_not(pred))(no)

    def take_up(t, a):
        def last():
            up_last(t).wait_recv()
            acc[t, a] += landed[t]

        def other():
            up(t, a).wait_recv()
            acc[t, a] += from_low[t, a].astype(F32)

        @pl.when(z > 0)
        def _():
            either(z == line - 1, last, other)

    def take_down(t, a):
        def last():
            down_last(t).wait_recv()
            acc[t, a] += landed[t]

        def other():
            down(t, a).wait_recv()
            acc[t, a] += from_high[t, a].astype(F32)

        @pl.when(z < line - 1)
        def _():
            either(z == 0, last, other)

    def go_up(t, a):
        take_up(t, a)

        def other():
            zsend[t, a] = acc[t, a].astype(BF16)
            up(t, a).start()

        either(z == line - 2, lambda: up_last(t).start(), other)

    def go_down(t, a):
        take_down(t, a)

        def other():
            zsend[t, a] = acc[t, a].astype(BF16)
            down(t, a).start()

        either(z == 1, lambda: down_last(t).start(), other)

    def forward_far(t):
        @pl.loop(0, half)
        def _(i):
            either(z < half, lambda: go_up(t, line - 1 - i), lambda: go_down(t, i))

    def forward_near(t):
        last = (near + 1) * half - 1

        @pl.loop(0, last - z)
        def _(i):
            go_up(t, last - i)

        @pl.loop(near * half, z)
        def _(a):
            go_down(t, a)

    def cols_of(h, b, t):
        return pl.ds(pl.multiple_of(start_of(h, b) + t * tw, BLOCK), tw)

    def f_copy(h, t):
        return remote(fin.at[t, h, 1 - bit[h]], out.at[:, cols_of(h, bit[h], t)],
                      f_s.at[h], f_r.at[h], row=peer[h])

    def f_own(h, t):
        return pltpu.make_async_copy(fin.at[t, h, bit[h]], out.at[:, cols_of(h, bit[h], t)], g_s.at[h])

    def f_all(h, b):
        area = out.at[:, pl.ds(pl.multiple_of(start_of(h, b), BLOCK), quarter)]
        return remote(area, area, f_s.at[h], f_r.at[h], row=peer[h])

    def g_all(h):
        area = out.at[:, pl.ds(pl.multiple_of(start_of(h, bit[h]), BLOCK), quarter)]
        return pltpu.make_async_copy(area, area, g_s.at[h])

    def finish(t):
        take_up(t, z)
        take_down(t, z)
        for h in range(2):
            total = acc[t, z, h] * factor
            for o in range(2):
                fin[t, h, o] = total[o * pd:(o + 1) * pd]
            f_copy(h, t).start()
            f_own(h, t).start()

    def z1_copy(u, g):
        return remote(z1s.at[u, g], z1r.at[u, g], z1_s, z1_r.at[u], row=peer[g])

    def z2_copy(u, g):
        return remote(z2s.at[u, g], z2r.at[u, g], z2_s, z2_r.at[u], row=peer[1 - g])

    def z3_copy(u, k):
        to = (pair + k) % pairs
        return remote(z3s.at[u, to], z3r.at[u, pair], z3_s, z3_r.at[u], row=(2 * to + odd) * G + q)

    def z3_both(u):
        return remote(z3r.at[u, :pairs - 1], z3r.at[u, :pairs - 1], z3_s, z3_r.at[u], row=peer[0])

    def pair_cols(b, u):
        return pl.ds(pl.multiple_of(pair_start(b, u), BLOCK), 2 * tw)

    def fz_copy(u):
        return remote(fz.at[u, 1 - odd], out.at[:, pair_cols(odd, u)], fz_s, fz_r, row=peer[2])

    def fz_own(u):
        return pltpu.make_async_copy(fz.at[u, odd], out.at[:, pair_cols(odd, u)], gz_s)

    def pair_area(b):
        return out.at[:, pl.ds(pl.multiple_of(pair_start(b, 0), BLOCK), side)]

    def pair_multiply(u):
        zx_copy(u).wait_recv()
        for g in range(2):
            for b in range(2):
                total = product(2, b, xz[odd, u, g], zin[u, g])
                for k in range(pairs):
                    for i in range(2):
                        at = (2 * k + i) * pr
                        zfull[u, g, b, i, k] = total[at:at + pr]
            for i in range(2):
                z1s[u, g, i] = (zfull[u, 0, 1 - bit[0], i] if g == 0 else zfull[u, 1, i, 1 - bit[1]]).astype(BF16)
            z1_copy(u, g).start()

    def pair_first(u):
        remote(z1r.at[u], z1r.at[u], z1_s, z1_r.at[u], row=peer[0]).wait_recv()
        for i in range(2):
            zfull[u, 0, bit[0], i] += z1r[u, 0, i].astype(F32)
            zfull[u, 1, i, bit[1]] += z1r[u, 1, i].astype(F32)
        z2s[u, 0] = zfull[u, 0, bit[0], 1 - bit[1]].astype(BF16)
        z2s[u, 1] = zfull[u, 1, 1 - bit[0], bit[1]].astype(BF16)
        for g in range(2):
            z2_copy(u, g).start()

    def pair_second(u):
        remote(z2r.at[u], z2r.at[u], z2_s, z2_r.at[u], row=peer[0]).wait_recv()
        for g in range(2):
            total = zfull[u, g, bit[0], bit[1]] + z2r[u, g].astype(F32)
            zfull[u, g, bit[0], bit[1]] = total
            for k in range(pairs):
                z3s[u, k, g] = total[k].astype(BF16)

        @pl.loop(1, pairs)
        def _(k):
            z3_copy(u, k).start()

    def pair_finish(u):
        z3_both(u).wait_recv()
        for g in range(2):
            total = zfull[u, g, bit[0], bit[1], pair]
            for k in range(1, pairs):
                total += z3r[u, (pair + k) % pairs, g].astype(F32)
            total = total * factor
            for o in range(2):
                fz[u, o, :, g * tw:(g + 1) * tw] = total[o * pd:(o + 1) * pd]
        fz_copy(u).start()
        fz_own(u).start()

    edge = (z == 0) | (z == line - 1)

    def at(step, lag, act, also=True, count=tiles):
        t = step - lag

        @pl.when((t >= 0) & (t < count) & also)
        def _():
            act(t)

    def step(t, carry):
        at(t, 0, multiply)

        @pl.when(t + AHEAD[2] < tiles)
        def _():
            start_x(t + AHEAD[2])

        @pl.when(t + PAIR_AHEAD[2] < groups)
        def _():
            zx_copy(t + PAIR_AHEAD[2]).start()

        @pl.when((t >= DEFER) & (t < tiles))
        def _():
            start_r(t - DEFER, near)

        @pl.when(t == tiles - 1)
        def _():
            for k in range(tiles - DEFER, tiles):
                start_r(k, near)

        at(t, LAGS[0], lambda k: reduce(k, far))
        at(t, LAGS[0], forward_far, edge)
        at(t, LAGS[1], forward_far, jnp.logical_not(edge))
        at(t, LAGS[2], lambda k: reduce(k, near))
        at(t, LAGS[3], forward_near)
        at(t, LAGS[4], finish)
        at(t, PAIR_LAGS[0] - 1, lambda k: relay(2), count=1)
        at(t, PAIR_LAGS[0], lambda k: relayed(2), count=1)
        for lag, act in zip(PAIR_LAGS, (pair_multiply, pair_first, pair_second, pair_finish)):
            at(t, lag, act, count=groups)
        return carry

    lax.fori_loop(0, tiles + LAGS[4], step, 0)

    for h in range(2):
        f_all(h, 1 - bit[h]).wait_recv()
        f_all(h, bit[h]).wait_send()
        g_all(h).wait()
        x_all(h).wait_send()
        p_copy(h).wait_send()
    p_copy(2).wait_send()
    r_all().wait_send()
    remote(xz.at[1 - odd], xz.at[1 - odd], zx_s, zx_r.at[0], row=peer[2]).wait_send()
    remote(z1s, z1r, z1_s, z1_r.at[0], row=peer[0]).wait_send()
    remote(z2s, z2r, z2_s, z2_r.at[0], row=peer[0]).wait_send()
    remote(z3s.at[:, :pairs - 1], z3r.at[:, :pairs - 1], z3_s, z3_r.at[0], row=peer[0]).wait_send()
    remote(pair_area(odd), pair_area(1 - odd), fz_s, fz_r, row=peer[2]).wait()
    pltpu.make_async_copy(pair_area(odd), pair_area(odd), gz_s).wait()

    @pl.loop(0, line)
    def _(a):
        last = ((z == line - 2) & (a == line - 1)) | ((z == 1) & (a == 0))

        @pl.when(last)
        def _():
            remote(acc.at[:, a], acc.at[:, a], z_s.at[a], lo_r.at[0, 0], row=peer[0]).wait_send()

        @pl.when(jnp.logical_not(last) & (a != z))
        def _():
            remote(zsend.at[:, a], zsend.at[:, a], z_s.at[a], lo_r.at[0, 0], row=peer[0]).wait_send()

    @pl.loop(1, ncol)
    def _(j):
        c_send(j).wait_send()
        for h in range(3):
            e_send(h, j).wait_send()

    all_a().wait_send()
    all_b().wait_send()


def body(descriptors, block_mask, config_of):
    n, ncol = lax.axis_size("row"), lax.axis_size("col")
    rows, width = descriptors.shape
    part = PW // ncol
    wide = -(-(part + 1) // BLOCK) * BLOCK
    bw = -(-2 * part // BLOCK) * BLOCK
    blocks = width // BLOCK
    quarter_blocks = blocks * 7 // 40
    per = next(k for k in (2, 1) if quarter_blocks % k == 0 and (blocks - 4 * quarter_blocks) % (4 * k) == 0)
    tiles = quarter_blocks // per
    tw = quarter_blocks // tiles * BLOCK
    quarter = quarter_blocks * BLOCK
    groups = (width - 4 * quarter) // (4 * tw)
    line = n // G
    pd = PW // n
    pr = -(-2 * pd // 16) * 16
    zs = line // ncol

    cfg = (n, ncol, rows, width, part, wide, bw, tiles, tw, line, pd, pr, zs, quarter, groups, 1.0 / (rows * n))
    vm = pltpu.VMEM
    dma = pltpu.SemaphoreType.DMA
    hbm = pl.BlockSpec(memory_space=pl.ANY)
    return pl.pallas_call(
        functools.partial(kernel, cfg),
        out_shape=pltpu.VMEM((pd, width), F32),
        in_specs=[hbm, hbm, hbm],
        out_specs=pl.BlockSpec(memory_space=pltpu.VMEM),
        scratch_shapes=[
            vm((1, rows), jnp.int32),
            pltpu.SMEM(block_mask.shape, jnp.int32),
            vm((rows, wide), BF16),
            vm((n * SLOT, rows), BF16),
            vm((n * SLOT, wide), BF16),
            vm((n * SLOT, wide), BF16),
            vm((n * SLOT, bw), BF16),
            vm((n * SLOT, bw), BF16),
            vm((rows, width), BF16),
            vm((2, 2, tiles, rows, tw), BF16),
            vm((tiles, 2, rows, tw), BF16),
            vm((3, 2, ncol, zs * pr, 2 * rows), BF16),
            vm((3, 2, ncol, zs * pr, 2 * rows), BF16),
            vm((2, groups, 2, rows, tw), BF16),
            vm((groups, 2, rows, tw), BF16),
            vm((groups, 2, 2, 2, line // 2, pr, tw), F32),
            vm((groups, 2, 2, line // 2, pr, tw), BF16),
            vm((groups, 2, 2, line // 2, pr, tw), BF16),
            vm((groups, 2, line // 2, pr, tw), BF16),
            vm((groups, 2, line // 2, pr, tw), BF16),
            vm((groups, line // 2, 2, pr, tw), BF16),
            vm((groups, line // 2, 2, pr, tw), BF16),
            vm((groups, 2, pd, 2 * tw), F32),
            vm((tiles, line, 2, pr, tw), F32),
            vm((tiles, 2, 2, line // 2 * pr, tw), BF16),
            vm((tiles, 2, 2, line // 2 * pr, tw), BF16),
            vm((tiles, line, 2, pr, tw), BF16),
            vm((tiles, line, 2, pr, tw), BF16),
            vm((tiles, line, 2, pr, tw), BF16),
            vm((tiles, 2, pr, tw), F32),
            vm((tiles, 2, 2, pd, tw), F32),
            dma, dma, dma, dma,
            dma((3,)), dma((3,)), dma((ncol,)), dma((ncol,)), dma((3, ncol)), dma((3, ncol)), dma((9,)),
            dma((2,)), dma((tiles,)), dma, dma((tiles, 2)), dma((line,)), dma((tiles, line)), dma((tiles, line)),
            dma((2,)), dma((2,)), dma((2,)),
            dma, dma((groups,)), dma, dma((groups,)), dma, dma((groups,)), dma, dma((groups,)), dma, dma, dma,
        ],
        compiler_params=pltpu.CompilerParams(
            collective_id=0, has_side_effects=True, vmem_limit_bytes=56 * 1024 * 1024),
    )(config_of[None, :], block_mask, descriptors)


def solution(mesh):
    in_specs = (P("row", "col"), P("row", "col"), P("row"))
    out_specs = P("row", "col")
    return jax.shard_map(body, mesh=mesh, in_specs=in_specs, out_specs=out_specs, check_vma=False)
```

```python
import functools

import jax
import jax.numpy as jnp
from jax import lax
from jax.experimental import pallas as pl
from jax.experimental.pallas import tpu as pltpu
from jax.sharding import PartitionSpec as P

PW = 384
CONF_DEV = 64
BLOCK = 128
G = 4
SLOT = 16
AHEAD = (3, 4, 5)
DEFER = 2
LAGS = (1, 2, 3, 3, 5)
PAIR_AHEAD = (1, 1, 2)
PAIR_LAGS = (2, 3, 4, 6)
F32 = jnp.float32
BF16 = jnp.bfloat16


def remote(src, dst, send, recv, **where):
    return pltpu.make_async_remote_copy(
        src_ref=src, dst_ref=dst, send_sem=send, recv_sem=recv,
        device_id=where, device_id_type=pl.DeviceIdType.MESH,
    )


def kernel(cfg, config_of, block_mask, x, out,
           crow, marks, pext, perm, asend, arec, bsend, brec, xraw, xm, xin, own, mate,
           xz, zin, zfull, z1s, z1r, z2s, z2r, z3s, z3r, fz,
           acc, rsend, rrec, zsend, from_low, from_high, landed, fin,
           a_s, a_r, b_s, b_r, p_s, p_r, c_s, c_r, e_s, e_r, l_s,
           x_s, x_r, r_s, r_r, z_s, lo_r, hi_r, f_s, f_r, g_s,
           zx_s, zx_r, z1_s, z1_r, z2_s, z2_r, z3_s, z3_r, fz_s, fz_r, gz_s):
    n, ncol, rows, width, part, wide, bw, tiles, tw, line, pd, pr, zs, quarter, groups, factor = cfg
    side = (width - 4 * quarter) // 2
    pairs = line // 2
    half = line // 2
    r = lax.axis_index("row")
    c = lax.axis_index("col")
    z = r // G
    q = r % G
    near, far = z // half, 1 - z // half
    pair, odd = z // 2, z % 2
    bit = (q % 2, q // 2)
    peer = tuple(r + (1 - 2 * bit[h]) * (1 << h) for h in range(2)) + (r + (1 - 2 * odd) * G,)

    barrier = pltpu.get_barrier_semaphore()

    @pl.loop(1, n)
    def _(k):
        pl.semaphore_signal(barrier, inc=1, device_id={"row": (r + k) % n}, device_id_type=pl.DeviceIdType.MESH)

    @pl.loop(1, ncol)
    def _(k):
        pl.semaphore_signal(barrier, inc=1, device_id={"col": (c + k) % ncol}, device_id_type=pl.DeviceIdType.MESH)

    crow_copy = pltpu.make_async_copy(config_of, crow, l_s.at[6])
    marks_copy = pltpu.make_async_copy(block_mask, marks, l_s.at[7])
    crow_copy.start()
    marks_copy.start()
    panel_copy = pltpu.make_async_copy(x.at[:, :wide], pext, l_s.at[0])
    panel_copy.start()

    def start_of(h, b):
        return h * 2 * quarter + b * quarter

    def load(h, b, i):
        cols = pl.ds(pl.multiple_of(start_of(h, b), BLOCK), quarter)
        return pltpu.make_async_copy(x.at[:, cols], xraw.at[:, cols], l_s.at[i])

    away = [load(h, 1 - bit[h], 2 + h) for h in range(2)]
    kept = [load(h, bit[h], 4 + h) for h in range(2)]
    rest = pltpu.make_async_copy(x.at[:, 4 * quarter:], xraw.at[:, 4 * quarter:], l_s.at[8])
    for copy in away + [rest] + kept:
        copy.start()

    first = lax.broadcasted_iota(jnp.int32, (rows, rows), 0)
    second = lax.broadcasted_iota(jnp.int32, (rows, rows), 1)
    crow_copy.wait()
    ids_row = jnp.broadcast_to(crow[...], (rows, rows)).astype(F32)
    ids_col = jnp.sum(jnp.where(first == second, ids_row, 0.0), axis=1, keepdims=True).astype(jnp.int32)
    shift = CONF_DEV.bit_length() - 1
    owner = crow[...] >> shift
    before = ((ids_col >> shift) == owner) & (first < second)
    rank = jnp.sum(jnp.where(before, 1.0, 0.0), axis=0, keepdims=True)
    place = owner.astype(F32) * SLOT + rank
    slots = lax.broadcasted_iota(jnp.int32, (n * SLOT, rows), 0).astype(F32)
    perm[...] = jnp.where(slots == place, 1.0, 0.0).astype(BF16)
    label = ((ids_col & (CONF_DEV - 1)) + 1).astype(F32)
    lane = lax.broadcasted_iota(jnp.int32, (BLOCK, BLOCK), 1)
    panel_copy.wait()
    marks_copy.wait()
    for b in range(rows // BLOCK):
        span = slice(b * BLOCK, (b + 1) * BLOCK)
        for w in range(wide // BLOCK):
            cols = slice(w * BLOCK, (w + 1) * BLOCK)
            keep = marks[b, w].astype(F32) if w * BLOCK < part else 0.0
            block = pext[span, cols].astype(F32) * jnp.broadcast_to(keep, (BLOCK, BLOCK))
            if (w + 1) * BLOCK > part:
                block = jnp.where(lane + w * BLOCK < part, block, jnp.broadcast_to(label[span], (BLOCK, BLOCK)))
            pext[span, cols] = block.astype(BF16)
    asend[...] = jnp.dot(perm[...], pext[...], preferred_element_type=F32).astype(BF16)

    def mask_to(dst, base):
        for i in range(rows // BLOCK):
            span = slice(i * BLOCK, (i + 1) * BLOCK)
            for w in range(tw // BLOCK):
                keep = marks[i, base // BLOCK + w].astype(F32)
                cols = pl.ds(pl.multiple_of(base + w * BLOCK, BLOCK), BLOCK)
                dst[span, w * BLOCK:(w + 1) * BLOCK] = (
                    xraw[span, cols] * jnp.broadcast_to(keep, (BLOCK, BLOCK)).astype(BF16))

    def mask(h, b, t):
        mask_to(xm.at[h, b, t], start_of(h, b) + t * tw)

    def pair_start(b, u):
        return 4 * quarter + b * side + u * 2 * tw

    def mask_pair(b, u):
        for g in range(2):
            mask_to(xz.at[b, u, g], pair_start(b, u) + g * tw)

    def mask_away(low, high):
        @pl.loop(low, high)
        def _(t):
            for h in range(2):
                mask(h, 1 - bit[h], t)

    for copy in away:
        copy.wait()
    mask_away(0, AHEAD[0])
    pl.semaphore_wait(barrier, n - 1 + ncol - 1)

    def slot_rows(k):
        return pl.ds(pl.multiple_of(k * SLOT, SLOT), SLOT)

    def to_owner(k):
        to = (r + k) % n
        return remote(asend.at[slot_rows(to), :], arec.at[slot_rows(r), :], a_s, a_r, row=to)

    others = slice(0, (n - 1) * SLOT)

    def all_a():
        return remote(asend.at[others, :], arec.at[others, :], a_s, a_r, row=(r + 1) % n)

    def to_source(k):
        to = (r + k) % n
        return remote(bsend.at[slot_rows(to), :], brec.at[slot_rows(r), :], b_s, b_r, row=to)

    def all_b():
        return remote(bsend.at[others, :], brec.at[others, :], b_s, b_r, row=(r + 1) % n)

    def x_copy(h, t):
        return remote(xm.at[h, 1 - bit[h], t], xin.at[t, h], x_s.at[h], x_r.at[t], row=peer[h])

    def x_both(t):
        return remote(xin.at[t], xin.at[t], x_s.at[0], x_r.at[t], row=peer[0])

    def x_all(h):
        return remote(xm.at[h, 1 - bit[h]], xm.at[h, 1 - bit[h]], x_s.at[h], x_r.at[0], row=peer[h])

    def start_x(t):
        for h in range(2):
            x_copy(h, t).start()

    def zx_copy(u):
        return remote(xz.at[1 - odd, u], zin.at[u], zx_s, zx_r.at[u], row=peer[2])

    def p_copy(h):
        return remote(own.at[h, :, c], mate.at[h, :, c], p_s.at[h], p_r.at[h], row=peer[h])

    def c_send(j):
        to = (c + j) % ncol
        return remote(own.at[:, :, c], own.at[:, :, c], c_s.at[j], c_r.at[c], col=to)

    def c_from(j):
        to = (c + j) % ncol
        return remote(own.at[:, :, c], own.at[:, :, to], c_s.at[j], c_r.at[to], col=to)

    def e_send(h, j):
        to = (c + j) % ncol
        return remote(mate.at[h, :, c], mate.at[h, :, c], e_s.at[h, j], e_r.at[h, c], col=to)

    def e_from(h, j):
        to = (c + j) % ncol
        return remote(mate.at[h, :, c], mate.at[h, :, to], e_s.at[h, j], e_r.at[h, to], col=to)

    own_a = pltpu.make_async_copy(asend.at[slot_rows(r), :], arec.at[slot_rows(r), :], l_s.at[0])
    own_a.start()

    @pl.loop(1, n)
    def _(k):
        to_owner(k).start()

    for t in range(AHEAD[0]):
        start_x(t)
    rest.wait()
    for u in range(groups):
        mask_pair(1 - odd, u)
    for u in range(min(PAIR_AHEAD[0], groups)):
        zx_copy(u).start()
    mask_away(AHEAD[0], tiles)

    own_a.wait()
    all_a().wait_recv()

    arrived = arec[...]
    label = arrived[:, part:part + 1].astype(F32)
    ids = lax.broadcasted_iota(jnp.int32, (n * SLOT, BLOCK), 1).astype(F32) + 1.0
    member = jnp.where((label == ids) & (ids <= CONF_DEV), 1.0, 0.0).astype(BF16)
    same = lax.dot_general(member, member, (((1,), (1,)), ((), ())), preferred_element_type=F32)
    counts = jnp.maximum(jnp.sum(same, axis=1, keepdims=True), 1.0)
    same = same.astype(BF16)
    means = jnp.dot(same, arrived, preferred_element_type=F32) / counts
    high = (arrived.astype(F32) - means).astype(BF16)
    low = -(jnp.dot(same, high, preferred_element_type=F32) / counts)
    both = [high.astype(F32)[:, :part], low[:, :part]]
    if bw > 2 * part:
        both.append(jnp.zeros((n * SLOT, bw - 2 * part), F32))
    bsend[...] = jnp.concatenate(both, axis=1).astype(BF16)

    own_b = pltpu.make_async_copy(bsend.at[slot_rows(r), :], brec.at[slot_rows(r), :], l_s.at[1])
    own_b.start()

    @pl.loop(1, n)
    def _(k):
        to_source(k).start()

    for t in range(AHEAD[0], AHEAD[1]):
        start_x(t)
    for u in range(min(PAIR_AHEAD[0], groups), min(PAIR_AHEAD[1], groups)):
        zx_copy(u).start()
    for u in range(groups):
        mask_pair(odd, u)
    for copy in kept:
        copy.wait()

    @pl.loop(0, tiles)
    def _(t):
        for h in range(2):
            mask(h, bit[h], t)

    own_b.wait()
    all_b().wait_recv()

    back = lax.dot_general(brec[...], perm[...], (((0,), (0,)), ((), ())), preferred_element_type=F32)
    for h in range(3):
        for b in range(2):
            for s in range(zs):
                for i in range(2):
                    pieces = []
                    for o in range(2):
                        if h == 2:
                            at = i * part + ((s // 2 * 2 + o) * G + 2 * (s % 2) + b) * pd
                        else:
                            at = i * part + (s * G + (2 * b + o if h == 0 else 2 * o + b)) * pd
                        pieces.append(back[at:at + pd])
                    if pr > 2 * pd:
                        pieces.append(jnp.zeros((pr - 2 * pd, rows), F32))
                    own[h, b, c, s * pr:(s + 1) * pr, i * rows:(i + 1) * rows] = (
                        jnp.concatenate(pieces, axis=0).astype(BF16))
    for h in range(3):
        p_copy(h).start()

    @pl.loop(1, ncol)
    def _(j):
        c_send(j).start()

    for t in range(AHEAD[1], AHEAD[2]):
        start_x(t)
    for u in range(min(PAIR_AHEAD[1], groups), min(PAIR_AHEAD[2], groups)):
        zx_copy(u).start()

    def relay(h):
        p_copy(h).wait_recv()

        @pl.loop(1, ncol)
        def _(j):
            e_send(h, j).start()

    def relayed(h):
        @pl.loop(1, ncol)
        def _(j):
            e_from(h, j).wait_recv()

    for h in range(2):
        relay(h)

    @pl.loop(1, ncol)
    def _(j):
        c_from(j).wait_recv()

    for h in range(2):
        relayed(h)

    def r_copy(h, t, k):
        return remote(rsend.at[t, k, h], rrec.at[t, k, h], r_s, r_r.at[t, k], row=peer[1 - h])

    def r_both(t, k):
        return remote(rrec.at[t, k], rrec.at[t, k], r_s, r_r.at[t, k], row=peer[0])

    def r_all():
        return remote(rsend, rrec, r_s, r_r.at[0, 0], row=peer[0])

    def start_r(t, k):
        for h in range(2):
            r_copy(h, t, k).start()

    def product(h, b, mine, theirs):
        ours = own[h, b].reshape(line * pr, 2 * rows)
        other = mate[h, b].reshape(line * pr, 2 * rows)
        left = jnp.concatenate([ours, other], axis=1)
        right = jnp.concatenate([mine, mine, theirs, theirs], axis=0)
        return jnp.dot(left, right, preferred_element_type=F32)

    def multiply(t):
        x_both(t).wait_recv()

        def of(h, b):
            return product(h, b, xm[h, bit[h], t], xin[t, h])

        for h in range(2):
            total = of(h, 1 - bit[1 - h]).astype(BF16)
            for k in range(2):
                rsend[t, k, h] = total[k * half * pr:(k + 1) * half * pr]
            r_copy(h, t, far).start()
        for h in range(2):
            total = of(h, bit[1 - h])
            for a in range(line):
                acc[t, a, h] = total[a * pr:(a + 1) * pr]

    def reduce(t, k):
        r_both(t, k).wait_recv()
        for h in range(2):
            for i in range(half):
                acc[t, k * half + i, h] += rrec[t, k, h, i * pr:(i + 1) * pr].astype(F32)

    def up(t, a):
        return remote(zsend.at[t, a], from_low.at[t, a], z_s.at[a], lo_r.at[t, a], row=(r + G) % n)

    def down(t, a):
        return remote(zsend.at[t, a], from_high.at[t, a], z_s.at[a], hi_r.at[t, a], row=(r + n - G) % n)

    def up_last(t):
        return remote(acc.at[t, line - 1], landed.at[t], z_s.at[line - 1], lo_r.at[t, line - 1], row=(r + G) % n)

    def down_last(t):
        return remote(acc.at[t, 0], landed.at[t], z_s.at[0], hi_r.at[t, 0], row=(r + n - G) % n)

    def either(pred, yes, no):
        pl.when(pred)(yes)
        pl.when(jnp.logical_not(pred))(no)

    def take_up(t, a):
        def last():
            up_last(t).wait_recv()
            acc[t, a] += landed[t]

        def other():
            up(t, a).wait_recv()
            acc[t, a] += from_low[t, a].astype(F32)

        @pl.when(z > 0)
        def _():
            either(z == line - 1, last, other)

    def take_down(t, a):
        def last():
            down_last(t).wait_recv()
            acc[t, a] += landed[t]

        def other():
            down(t, a).wait_recv()
            acc[t, a] += from_high[t, a].astype(F32)

        @pl.when(z < line - 1)
        def _():
            either(z == 0, last, other)

    def go_up(t, a):
        take_up(t, a)

        def other():
            zsend[t, a] = acc[t, a].astype(BF16)
            up(t, a).start()

        either(z == line - 2, lambda: up_last(t).start(), other)

    def go_down(t, a):
        take_down(t, a)

        def other():
            zsend[t, a] = acc[t, a].astype(BF16)
            down(t, a).start()

        either(z == 1, lambda: down_last(t).start(), other)

    def forward_far(t):
        @pl.loop(0, half)
        def _(i):
            either(z < half, lambda: go_up(t, line - 1 - i), lambda: go_down(t, i))

    def forward_near(t):
        last = (near + 1) * half - 1

        @pl.loop(0, last - z)
        def _(i):
            go_up(t, last - i)

        @pl.loop(near * half, z)
        def _(a):
            go_down(t, a)

    def cols_of(h, b, t):
        return pl.ds(pl.multiple_of(start_of(h, b) + t * tw, BLOCK), tw)

    def f_copy(h, t):
        return remote(fin.at[t, h, 1 - bit[h]], out.at[:, cols_of(h, bit[h], t)],
                      f_s.at[h], f_r.at[h], row=peer[h])

    def f_own(h, t):
        return pltpu.make_async_copy(fin.at[t, h, bit[h]], out.at[:, cols_of(h, bit[h], t)], g_s.at[h])

    def f_all(h, b):
        area = out.at[:, pl.ds(pl.multiple_of(start_of(h, b), BLOCK), quarter)]
        return remote(area, area, f_s.at[h], f_r.at[h], row=peer[h])

    def g_all(h):
        area = out.at[:, pl.ds(pl.multiple_of(start_of(h, bit[h]), BLOCK), quarter)]
        return pltpu.make_async_copy(area, area, g_s.at[h])

    def finish(t):
        take_up(t, z)
        take_down(t, z)
        for h in range(2):
            total = acc[t, z, h] * factor
            for o in range(2):
                fin[t, h, o] = total[o * pd:(o + 1) * pd]
            f_copy(h, t).start()
            f_own(h, t).start()

    def z1_copy(u, g):
        return remote(z1s.at[u, g], z1r.at[u, g], z1_s, z1_r.at[u], row=peer[g])

    def z2_copy(u, g):
        return remote(z2s.at[u, g], z2r.at[u, g], z2_s, z2_r.at[u], row=peer[1 - g])

    def z3_copy(u, k):
        to = (pair + k) % pairs
        return remote(z3s.at[u, to], z3r.at[u, pair], z3_s, z3_r.at[u], row=(2 * to + odd) * G + q)

    def z3_both(u):
        return remote(z3r.at[u, :pairs - 1], z3r.at[u, :pairs - 1], z3_s, z3_r.at[u], row=peer[0])

    def pair_cols(b, u):
        return pl.ds(pl.multiple_of(pair_start(b, u), BLOCK), 2 * tw)

    def fz_copy(u):
        return remote(fz.at[u, 1 - odd], out.at[:, pair_cols(odd, u)], fz_s, fz_r, row=peer[2])

    def fz_own(u):
        return pltpu.make_async_copy(fz.at[u, odd], out.at[:, pair_cols(odd, u)], gz_s)

    def pair_area(b):
        return out.at[:, pl.ds(pl.multiple_of(pair_start(b, 0), BLOCK), side)]

    def pair_multiply(u):
        zx_copy(u).wait_recv()
        for g in range(2):
            for b in range(2):
                total = product(2, b, xz[odd, u, g], zin[u, g])
                for k in range(pairs):
                    for i in range(2):
                        at = (2 * k + i) * pr
                        zfull[u, g, b, i, k] = total[at:at + pr]
            for i in range(2):
                z1s[u, g, i] = (zfull[u, 0, 1 - bit[0], i] if g == 0 else zfull[u, 1, i, 1 - bit[1]]).astype(BF16)
            z1_copy(u, g).start()

    def pair_first(u):
        remote(z1r.at[u], z1r.at[u], z1_s, z1_r.at[u], row=peer[0]).wait_recv()
        for i in range(2):
            zfull[u, 0, bit[0], i] += z1r[u, 0, i].astype(F32)
            zfull[u, 1, i, bit[1]] += z1r[u, 1, i].astype(F32)
        z2s[u, 0] = zfull[u, 0, bit[0], 1 - bit[1]].astype(BF16)
        z2s[u, 1] = zfull[u, 1, 1 - bit[0], bit[1]].astype(BF16)
        for g in range(2):
            z2_copy(u, g).start()

    def pair_second(u):
        remote(z2r.at[u], z2r.at[u], z2_s, z2_r.at[u], row=peer[0]).wait_recv()
        for g in range(2):
            total = zfull[u, g, bit[0], bit[1]] + z2r[u, g].astype(F32)
            zfull[u, g, bit[0], bit[1]] = total
            for k in range(pairs):
                z3s[u, k, g] = total[k].astype(BF16)

        @pl.loop(1, pairs)
        def _(k):
            z3_copy(u, k).start()

    def pair_finish(u):
        z3_both(u).wait_recv()
        for g in range(2):
            total = zfull[u, g, bit[0], bit[1], pair]
            for k in range(1, pairs):
                total += z3r[u, (pair + k) % pairs, g].astype(F32)
            total = total * factor
            for o in range(2):
                fz[u, o, :, g * tw:(g + 1) * tw] = total[o * pd:(o + 1) * pd]
        fz_copy(u).start()
        fz_own(u).start()

    edge = (z == 0) | (z == line - 1)

    def at(step, lag, act, also=True, count=tiles):
        t = step - lag

        @pl.when((t >= 0) & (t < count) & also)
        def _():
            act(t)

    def step(t, carry):
        at(t, LAGS[4], finish)
        at(t, 0, multiply)

        @pl.when(t + AHEAD[2] < tiles)
        def _():
            start_x(t + AHEAD[2])

        @pl.when(t + PAIR_AHEAD[2] < groups)
        def _():
            zx_copy(t + PAIR_AHEAD[2]).start()

        @pl.when((t >= DEFER) & (t < tiles))
        def _():
            start_r(t - DEFER, near)

        @pl.when(t == tiles - 1)
        def _():
            for k in range(tiles - DEFER, tiles):
                start_r(k, near)

        at(t, LAGS[0], lambda k: reduce(k, far))
        at(t, LAGS[0], forward_far, edge)
        at(t, LAGS[1], forward_far, jnp.logical_not(edge))
        at(t, LAGS[2], lambda k: reduce(k, near))
        at(t, LAGS[3], forward_near)
        at(t, PAIR_LAGS[0] - 1, lambda k: relay(2), count=1)
        at(t, PAIR_LAGS[0], lambda k: relayed(2), count=1)
        for lag, act in zip(PAIR_LAGS, (pair_multiply, pair_first, pair_second, pair_finish)):
            at(t, lag, act, count=groups)
        return carry

    lax.fori_loop(0, tiles + LAGS[4], step, 0)

    for h in range(2):
        f_all(h, 1 - bit[h]).wait_recv()
        f_all(h, bit[h]).wait_send()
        g_all(h).wait()
        x_all(h).wait_send()
        p_copy(h).wait_send()
    p_copy(2).wait_send()
    r_all().wait_send()
    remote(xz.at[1 - odd], xz.at[1 - odd], zx_s, zx_r.at[0], row=peer[2]).wait_send()
    remote(z1s, z1r, z1_s, z1_r.at[0], row=peer[0]).wait_send()
    remote(z2s, z2r, z2_s, z2_r.at[0], row=peer[0]).wait_send()
    remote(z3s.at[:, :pairs - 1], z3r.at[:, :pairs - 1], z3_s, z3_r.at[0], row=peer[0]).wait_send()
    remote(pair_area(odd), pair_area(1 - odd), fz_s, fz_r, row=peer[2]).wait()
    pltpu.make_async_copy(pair_area(odd), pair_area(odd), gz_s).wait()

    @pl.loop(0, line)
    def _(a):
        last = ((z == line - 2) & (a == line - 1)) | ((z == 1) & (a == 0))

        @pl.when(last)
        def _():
            remote(acc.at[:, a], acc.at[:, a], z_s.at[a], lo_r.at[0, 0], row=peer[0]).wait_send()

        @pl.when(jnp.logical_not(last) & (a != z))
        def _():
            remote(zsend.at[:, a], zsend.at[:, a], z_s.at[a], lo_r.at[0, 0], row=peer[0]).wait_send()

    @pl.loop(1, ncol)
    def _(j):
        c_send(j).wait_send()
        for h in range(3):
            e_send(h, j).wait_send()

    all_a().wait_send()
    all_b().wait_send()


def body(descriptors, block_mask, config_of):
    n, ncol = lax.axis_size("row"), lax.axis_size("col")
    rows, width = descriptors.shape
    part = PW // ncol
    wide = -(-(part + 1) // BLOCK) * BLOCK
    bw = -(-2 * part // BLOCK) * BLOCK
    blocks = width // BLOCK
    quarter_blocks = blocks * 7 // 40
    per = next(k for k in (2, 1) if quarter_blocks % k == 0 and (blocks - 4 * quarter_blocks) % (4 * k) == 0)
    tiles = quarter_blocks // per
    tw = quarter_blocks // tiles * BLOCK
    quarter = quarter_blocks * BLOCK
    groups = (width - 4 * quarter) // (4 * tw)
    line = n // G
    pd = PW // n
    pr = -(-2 * pd // 16) * 16
    zs = line // ncol

    cfg = (n, ncol, rows, width, part, wide, bw, tiles, tw, line, pd, pr, zs, quarter, groups, 1.0 / (rows * n))
    vm = pltpu.VMEM
    dma = pltpu.SemaphoreType.DMA
    hbm = pl.BlockSpec(memory_space=pl.ANY)
    return pl.pallas_call(
        functools.partial(kernel, cfg),
        out_shape=pltpu.VMEM((pd, width), F32),
        in_specs=[hbm, hbm, hbm],
        out_specs=pl.BlockSpec(memory_space=pltpu.VMEM),
        scratch_shapes=[
            vm((1, rows), jnp.int32),
            pltpu.SMEM(block_mask.shape, jnp.int32),
            vm((rows, wide), BF16),
            vm((n * SLOT, rows), BF16),
            vm((n * SLOT, wide), BF16),
            vm((n * SLOT, wide), BF16),
            vm((n * SLOT, bw), BF16),
            vm((n * SLOT, bw), BF16),
            vm((rows, width), BF16),
            vm((2, 2, tiles, rows, tw), BF16),
            vm((tiles, 2, rows, tw), BF16),
            vm((3, 2, ncol, zs * pr, 2 * rows), BF16),
            vm((3, 2, ncol, zs * pr, 2 * rows), BF16),
            vm((2, groups, 2, rows, tw), BF16),
            vm((groups, 2, rows, tw), BF16),
            vm((groups, 2, 2, 2, line // 2, pr, tw), F32),
            vm((groups, 2, 2, line // 2, pr, tw), BF16),
            vm((groups, 2, 2, line // 2, pr, tw), BF16),
            vm((groups, 2, line // 2, pr, tw), BF16),
            vm((groups, 2, line // 2, pr, tw), BF16),
            vm((groups, line // 2, 2, pr, tw), BF16),
            vm((groups, line // 2, 2, pr, tw), BF16),
            vm((groups, 2, pd, 2 * tw), F32),
            vm((tiles, line, 2, pr, tw), F32),
            vm((tiles, 2, 2, line // 2 * pr, tw), BF16),
            vm((tiles, 2, 2, line // 2 * pr, tw), BF16),
            vm((tiles, line, 2, pr, tw), BF16),
            vm((tiles, line, 2, pr, tw), BF16),
            vm((tiles, line, 2, pr, tw), BF16),
            vm((tiles, 2, pr, tw), F32),
            vm((tiles, 2, 2, pd, tw), F32),
            dma, dma, dma, dma,
            dma((3,)), dma((3,)), dma((ncol,)), dma((ncol,)), dma((3, ncol)), dma((3, ncol)), dma((9,)),
            dma((2,)), dma((tiles,)), dma, dma((tiles, 2)), dma((line,)), dma((tiles, line)), dma((tiles, line)),
            dma((2,)), dma((2,)), dma((2,)),
            dma, dma((groups,)), dma, dma((groups,)), dma, dma((groups,)), dma, dma((groups,)), dma, dma, dma,
        ],
        compiler_params=pltpu.CompilerParams(
            collective_id=0, has_side_effects=True, vmem_limit_bytes=56 * 1024 * 1024),
    )(config_of[None, :], block_mask, descriptors)


def solution(mesh):
    in_specs = (P("row", "col"), P("row", "col"), P("row"))
    out_specs = P("row", "col")
    return jax.shard_map(body, mesh=mesh, in_specs=in_specs, out_specs=out_specs, check_vma=False)
```

```python
import functools

import jax
import jax.numpy as jnp
from jax import lax
from jax.experimental import pallas as pl
from jax.experimental.pallas import tpu as pltpu
from jax.sharding import PartitionSpec as P

PW = 384
CONF_DEV = 64
BLOCK = 128
G = 4
SLOT = 16
AHEAD = (2, 4, 5)
DEFER = 2
LAGS = (1, 2, 3, 3, 5)
PAIR_AHEAD = (1, 1, 2)
PAIR_LAGS = (2, 3, 4, 6)
F32 = jnp.float32
BF16 = jnp.bfloat16


def remote(src, dst, send, recv, **where):
    return pltpu.make_async_remote_copy(
        src_ref=src, dst_ref=dst, send_sem=send, recv_sem=recv,
        device_id=where, device_id_type=pl.DeviceIdType.MESH,
    )


def kernel(cfg, config_of, block_mask, x, out,
           crow, marks, pext, perm, asend, arec, bsend, brec, xraw, xm, xin, own, mate,
           xz, zin, zfull, z1s, z1r, z2s, z2r, z3s, z3r, fz,
           acc, rsend, rrec, zsend, from_low, from_high, landed, fin,
           a_s, a_r, b_s, b_r, p_s, p_r, c_s, c_r, e_s, e_r, l_s,
           x_s, x_r, r_s, r_r, z_s, lo_r, hi_r, f_s, f_r,
           zx_s, zx_r, z1_s, z1_r, z2_s, z2_r, z3_s, z3_r, fz_s, fz_r):
    n, ncol, rows, width, part, wide, bw, tiles, tw, line, pd, pr, zs, quarter, groups, factor = cfg
    side = (width - 4 * quarter) // 2
    pairs = line // 2
    half = line // 2
    r = lax.axis_index("row")
    c = lax.axis_index("col")
    z = r // G
    q = r % G
    near, far = z // half, 1 - z // half
    pair, odd = z // 2, z % 2
    bit = (q % 2, q // 2)
    peer = tuple(r + (1 - 2 * bit[h]) * (1 << h) for h in range(2)) + (r + (1 - 2 * odd) * G,)

    barrier = pltpu.get_barrier_semaphore()

    @pl.loop(1, n)
    def _(k):
        pl.semaphore_signal(barrier, inc=1, device_id={"row": (r + k) % n}, device_id_type=pl.DeviceIdType.MESH)

    @pl.loop(1, ncol)
    def _(k):
        pl.semaphore_signal(barrier, inc=1, device_id={"col": (c + k) % ncol}, device_id_type=pl.DeviceIdType.MESH)

    crow_copy = pltpu.make_async_copy(config_of, crow, l_s.at[6])
    marks_copy = pltpu.make_async_copy(block_mask, marks, l_s.at[7])
    crow_copy.start()
    marks_copy.start()
    panel_copy = pltpu.make_async_copy(x.at[:, :wide], pext, l_s.at[0])
    panel_copy.start()

    def start_of(h, b):
        return h * 2 * quarter + b * quarter

    def load(h, b, i):
        cols = pl.ds(pl.multiple_of(start_of(h, b), BLOCK), quarter)
        return pltpu.make_async_copy(x.at[:, cols], xraw.at[:, cols], l_s.at[i])

    away = [load(h, 1 - bit[h], 2 + h) for h in range(2)]
    kept = [load(h, bit[h], 4 + h) for h in range(2)]
    rest = pltpu.make_async_copy(x.at[:, 4 * quarter:], xraw.at[:, 4 * quarter:], l_s.at[8])
    for copy in away + [rest] + kept:
        copy.start()

    first = lax.broadcasted_iota(jnp.int32, (rows, rows), 0)
    second = lax.broadcasted_iota(jnp.int32, (rows, rows), 1)
    crow_copy.wait()
    ids_row = jnp.broadcast_to(crow[...], (rows, rows)).astype(F32)
    ids_col = jnp.sum(jnp.where(first == second, ids_row, 0.0), axis=1, keepdims=True).astype(jnp.int32)
    shift = CONF_DEV.bit_length() - 1
    owner = crow[...] >> shift
    before = ((ids_col >> shift) == owner) & (first < second)
    rank = jnp.sum(jnp.where(before, 1.0, 0.0), axis=0, keepdims=True)
    place = owner.astype(F32) * SLOT + rank
    slots = lax.broadcasted_iota(jnp.int32, (n * SLOT, rows), 0).astype(F32)
    perm[...] = jnp.where(slots == place, 1.0, 0.0).astype(BF16)
    label = ((ids_col & (CONF_DEV - 1)) + 1).astype(F32)
    lane = lax.broadcasted_iota(jnp.int32, (BLOCK, BLOCK), 1)
    panel_copy.wait()
    marks_copy.wait()
    for b in range(rows // BLOCK):
        span = slice(b * BLOCK, (b + 1) * BLOCK)
        for w in range(wide // BLOCK):
            cols = slice(w * BLOCK, (w + 1) * BLOCK)
            keep = marks[b, w].astype(F32) if w * BLOCK < part else 0.0
            block = pext[span, cols].astype(F32) * jnp.broadcast_to(keep, (BLOCK, BLOCK))
            if (w + 1) * BLOCK > part:
                block = jnp.where(lane + w * BLOCK < part, block, jnp.broadcast_to(label[span], (BLOCK, BLOCK)))
            pext[span, cols] = block.astype(BF16)
    asend[...] = jnp.dot(perm[...], pext[...], preferred_element_type=F32).astype(BF16)

    def mask_to(dst, base):
        for i in range(rows // BLOCK):
            span = slice(i * BLOCK, (i + 1) * BLOCK)
            for w in range(tw // BLOCK):
                keep = marks[i, base // BLOCK + w].astype(F32)
                cols = pl.ds(pl.multiple_of(base + w * BLOCK, BLOCK), BLOCK)
                dst[span, w * BLOCK:(w + 1) * BLOCK] = (
                    xraw[span, cols] * jnp.broadcast_to(keep, (BLOCK, BLOCK)).astype(BF16))

    def mask(h, b, t):
        mask_to(xm.at[h, b, t], start_of(h, b) + t * tw)

    def pair_start(b, u):
        return 4 * quarter + b * side + u * 2 * tw

    def mask_pair(b, u):
        for g in range(2):
            mask_to(xz.at[b, u, g], pair_start(b, u) + g * tw)

    def mask_away(low, high):
        @pl.loop(low, high)
        def _(t):
            for h in range(2):
                mask(h, 1 - bit[h], t)

    for copy in away:
        copy.wait()
    mask_away(0, AHEAD[0])
    pl.semaphore_wait(barrier, n - 1 + ncol - 1)

    def slot_rows(k):
        return pl.ds(pl.multiple_of(k * SLOT, SLOT), SLOT)

    def to_owner(k):
        to = (r + k) % n
        return remote(asend.at[slot_rows(to), :], arec.at[slot_rows(r), :], a_s, a_r, row=to)

    others = slice(0, (n - 1) * SLOT)

    def all_a():
        return remote(asend.at[others, :], arec.at[others, :], a_s, a_r, row=(r + 1) % n)

    def to_source(k):
        to = (r + k) % n
        return remote(bsend.at[slot_rows(to), :], brec.at[slot_rows(r), :], b_s, b_r, row=to)

    def all_b():
        return remote(bsend.at[others, :], brec.at[others, :], b_s, b_r, row=(r + 1) % n)

    def x_copy(h, t):
        return remote(xm.at[h, 1 - bit[h], t], xin.at[t, h], x_s.at[h], x_r.at[t], row=peer[h])

    def x_both(t):
        return remote(xin.at[t], xin.at[t], x_s.at[0], x_r.at[t], row=peer[0])

    def x_all(h):
        return remote(xm.at[h, 1 - bit[h]], xm.at[h, 1 - bit[h]], x_s.at[h], x_r.at[0], row=peer[h])

    def start_x(t):
        for h in range(2):
            x_copy(h, t).start()

    def zx_copy(u):
        return remote(xz.at[1 - odd, u], zin.at[u], zx_s, zx_r.at[u], row=peer[2])

    def p_copy(h):
        return remote(own.at[h, :, c], mate.at[h, :, c], p_s.at[h], p_r.at[h], row=peer[h])

    def c_send(j):
        to = (c + j) % ncol
        return remote(own.at[:, :, c], own.at[:, :, c], c_s.at[j], c_r.at[c], col=to)

    def c_from(j):
        to = (c + j) % ncol
        return remote(own.at[:, :, c], own.at[:, :, to], c_s.at[j], c_r.at[to], col=to)

    def e_send(h, j):
        to = (c + j) % ncol
        return remote(mate.at[h, :, c], mate.at[h, :, c], e_s.at[h, j], e_r.at[h, c], col=to)

    def e_from(h, j):
        to = (c + j) % ncol
        return remote(mate.at[h, :, c], mate.at[h, :, to], e_s.at[h, j], e_r.at[h, to], col=to)

    own_a = pltpu.make_async_copy(asend.at[slot_rows(r), :], arec.at[slot_rows(r), :], l_s.at[0])
    own_a.start()

    @pl.loop(1, n)
    def _(k):
        to_owner(k).start()

    for t in range(AHEAD[0]):
        start_x(t)
    rest.wait()
    for u in range(groups):
        mask_pair(1 - odd, u)
    for u in range(min(PAIR_AHEAD[0], groups)):
        zx_copy(u).start()
    mask_away(AHEAD[0], tiles)

    own_a.wait()
    all_a().wait_recv()

    arrived = arec[...]
    label = arrived[:, part:part + 1].astype(F32)
    ids = lax.broadcasted_iota(jnp.int32, (n * SLOT, BLOCK), 1).astype(F32) + 1.0
    member = jnp.where((label == ids) & (ids <= CONF_DEV), 1.0, 0.0).astype(BF16)
    same = lax.dot_general(member, member, (((1,), (1,)), ((), ())), preferred_element_type=F32)
    counts = jnp.maximum(jnp.sum(same, axis=1, keepdims=True), 1.0)
    same = same.astype(BF16)
    means = jnp.dot(same, arrived, preferred_element_type=F32) / counts
    high = (arrived.astype(F32) - means).astype(BF16)
    low = -(jnp.dot(same, high, preferred_element_type=F32) / counts)
    both = [high.astype(F32)[:, :part], low[:, :part]]
    if bw > 2 * part:
        both.append(jnp.zeros((n * SLOT, bw - 2 * part), F32))
    bsend[...] = jnp.concatenate(both, axis=1).astype(BF16)

    own_b = pltpu.make_async_copy(bsend.at[slot_rows(r), :], brec.at[slot_rows(r), :], l_s.at[1])
    own_b.start()

    @pl.loop(1, n)
    def _(k):
        to_source(k).start()

    for t in range(AHEAD[0], AHEAD[1]):
        start_x(t)
    for u in range(min(PAIR_AHEAD[0], groups), min(PAIR_AHEAD[1], groups)):
        zx_copy(u).start()
    for u in range(groups):
        mask_pair(odd, u)
    for copy in kept:
        copy.wait()

    @pl.loop(0, tiles)
    def _(t):
        for h in range(2):
            mask(h, bit[h], t)

    own_b.wait()
    all_b().wait_recv()

    back = lax.dot_general(brec[...], perm[...], (((0,), (0,)), ((), ())), preferred_element_type=F32)
    for h in range(3):
        for b in range(2):
            for s in range(zs):
                for i in range(2):
                    pieces = []
                    for o in range(2):
                        if h == 2:
                            at = i * part + ((s // 2 * 2 + o) * G + 2 * (s % 2) + b) * pd
                        else:
                            at = i * part + (s * G + (2 * b + o if h == 0 else 2 * o + b)) * pd
                        pieces.append(back[at:at + pd])
                    if pr > 2 * pd:
                        pieces.append(jnp.zeros((pr - 2 * pd, rows), F32))
                    own[h, b, c, s * pr:(s + 1) * pr, i * rows:(i + 1) * rows] = (
                        jnp.concatenate(pieces, axis=0).astype(BF16))
    for h in range(3):
        p_copy(h).start()

    @pl.loop(1, ncol)
    def _(j):
        c_send(j).start()

    for t in range(AHEAD[1], AHEAD[2]):
        start_x(t)
    for u in range(min(PAIR_AHEAD[1], groups), min(PAIR_AHEAD[2], groups)):
        zx_copy(u).start()

    def relay(h):
        p_copy(h).wait_recv()

        @pl.loop(1, ncol)
        def _(j):
            e_send(h, j).start()

    def relayed(h):
        @pl.loop(1, ncol)
        def _(j):
            e_from(h, j).wait_recv()

    for h in range(2):
        relay(h)

    @pl.loop(1, ncol)
    def _(j):
        c_from(j).wait_recv()

    for h in range(2):
        relayed(h)

    def r_copy(h, t, k):
        return remote(rsend.at[t, k, h], rrec.at[t, k, h], r_s, r_r.at[t, k], row=peer[1 - h])

    def r_both(t, k):
        return remote(rrec.at[t, k], rrec.at[t, k], r_s, r_r.at[t, k], row=peer[0])

    def r_all():
        return remote(rsend, rrec, r_s, r_r.at[0, 0], row=peer[0])

    def start_r(t, k):
        for h in range(2):
            r_copy(h, t, k).start()

    def product(h, b, mine, theirs):
        ours = own[h, b].reshape(line * pr, 2 * rows)
        other = mate[h, b].reshape(line * pr, 2 * rows)
        left = jnp.concatenate([ours, other], axis=1)
        right = jnp.concatenate([mine, mine, theirs, theirs], axis=0)
        return jnp.dot(left, right, preferred_element_type=F32)

    def multiply(t):
        x_both(t).wait_recv()

        def of(h, b):
            return product(h, b, xm[h, bit[h], t], xin[t, h])

        for h in range(2):
            total = of(h, 1 - bit[1 - h]).astype(BF16)
            for k in range(2):
                rsend[t, k, h] = total[k * half * pr:(k + 1) * half * pr]
            r_copy(h, t, far).start()
        for h in range(2):
            total = of(h, bit[1 - h])
            for a in range(line):
                acc[t, a, h] = total[a * pr:(a + 1) * pr]

    def reduce(t, k):
        r_both(t, k).wait_recv()
        for h in range(2):
            for i in range(half):
                acc[t, k * half + i, h] += rrec[t, k, h, i * pr:(i + 1) * pr].astype(F32)

    def up(t, a):
        return remote(zsend.at[t, a], from_low.at[t, a], z_s.at[a], lo_r.at[t, a], row=(r + G) % n)

    def down(t, a):
        return remote(zsend.at[t, a], from_high.at[t, a], z_s.at[a], hi_r.at[t, a], row=(r + n - G) % n)

    def up_last(t):
        return remote(acc.at[t, line - 1], landed.at[t], z_s.at[line - 1], lo_r.at[t, line - 1], row=(r + G) % n)

    def down_last(t):
        return remote(acc.at[t, 0], landed.at[t], z_s.at[0], hi_r.at[t, 0], row=(r + n - G) % n)

    def either(pred, yes, no):
        pl.when(pred)(yes)
        pl.when(jnp.logical_not(pred))(no)

    def take_up(t, a):
        def last():
            up_last(t).wait_recv()
            acc[t, a] += landed[t]

        def other():
            up(t, a).wait_recv()
            acc[t, a] += from_low[t, a].astype(F32)

        @pl.when(z > 0)
        def _():
            either(z == line - 1, last, other)

    def take_down(t, a):
        def last():
            down_last(t).wait_recv()
            acc[t, a] += landed[t]

        def other():
            down(t, a).wait_recv()
            acc[t, a] += from_high[t, a].astype(F32)

        @pl.when(z < line - 1)
        def _():
            either(z == 0, last, other)

    def go_up(t, a):
        take_up(t, a)

        def other():
            zsend[t, a] = acc[t, a].astype(BF16)
            up(t, a).start()

        either(z == line - 2, lambda: up_last(t).start(), other)

    def go_down(t, a):
        take_down(t, a)

        def other():
            zsend[t, a] = acc[t, a].astype(BF16)
            down(t, a).start()

        either(z == 1, lambda: down_last(t).start(), other)

    def forward_far(t):
        @pl.loop(0, half)
        def _(i):
            either(z < half, lambda: go_up(t, line - 1 - i), lambda: go_down(t, i))

    def forward_near(t):
        last = (near + 1) * half - 1

        @pl.loop(0, last - z)
        def _(i):
            go_up(t, last - i)

        @pl.loop(near * half, z)
        def _(a):
            go_down(t, a)

    def cols_of(h, b, t):
        return pl.ds(pl.multiple_of(start_of(h, b) + t * tw, BLOCK), tw)

    def f_copy(h, t):
        return remote(fin.at[t, h, 1 - bit[h]], out.at[:, cols_of(h, bit[h], t)],
                      f_s.at[h], f_r.at[h], row=peer[h])

    def f_all(h, b):
        area = out.at[:, pl.ds(pl.multiple_of(start_of(h, b), BLOCK), quarter)]
        return remote(area, area, f_s.at[h], f_r.at[h], row=peer[h])

    def finish(t):
        take_up(t, z)
        take_down(t, z)
        for h in range(2):
            total = acc[t, z, h] * factor
            for o in range(2):
                fin[t, h, o] = total[o * pd:(o + 1) * pd]
            f_copy(h, t).start()
            out[:, cols_of(h, bit[h], t)] = fin[t, h, bit[h]]

    def z1_copy(u, g):
        return remote(z1s.at[u, g], z1r.at[u, g], z1_s, z1_r.at[u], row=peer[g])

    def z2_copy(u, g):
        return remote(z2s.at[u, g], z2r.at[u, g], z2_s, z2_r.at[u], row=peer[1 - g])

    def z3_copy(u, k):
        to = (pair + k) % pairs
        return remote(z3s.at[u, to], z3r.at[u, pair], z3_s, z3_r.at[u], row=(2 * to + odd) * G + q)

    def z3_both(u):
        return remote(z3r.at[u, :pairs - 1], z3r.at[u, :pairs - 1], z3_s, z3_r.at[u], row=peer[0])

    def pair_cols(b, u):
        return pl.ds(pl.multiple_of(pair_start(b, u), BLOCK), 2 * tw)

    def fz_copy(u):
        return remote(fz.at[u, 1 - odd], out.at[:, pair_cols(odd, u)], fz_s, fz_r, row=peer[2])

    def pair_area(b):
        return out.at[:, pl.ds(pl.multiple_of(pair_start(b, 0), BLOCK), side)]

    def pair_multiply(u):
        zx_copy(u).wait_recv()
        for g in range(2):
            for b in range(2):
                total = product(2, b, xz[odd, u, g], zin[u, g])
                for k in range(pairs):
                    for i in range(2):
                        at = (2 * k + i) * pr
                        zfull[u, g, b, i, k] = total[at:at + pr]
            for i in range(2):
                z1s[u, g, i] = (zfull[u, 0, 1 - bit[0], i] if g == 0 else zfull[u, 1, i, 1 - bit[1]]).astype(BF16)
            z1_copy(u, g).start()

    def pair_first(u):
        remote(z1r.at[u], z1r.at[u], z1_s, z1_r.at[u], row=peer[0]).wait_recv()
        for i in range(2):
            zfull[u, 0, bit[0], i] += z1r[u, 0, i].astype(F32)
            zfull[u, 1, i, bit[1]] += z1r[u, 1, i].astype(F32)
        z2s[u, 0] = zfull[u, 0, bit[0], 1 - bit[1]].astype(BF16)
        z2s[u, 1] = zfull[u, 1, 1 - bit[0], bit[1]].astype(BF16)
        for g in range(2):
            z2_copy(u, g).start()

    def pair_second(u):
        remote(z2r.at[u], z2r.at[u], z2_s, z2_r.at[u], row=peer[0]).wait_recv()
        for g in range(2):
            total = zfull[u, g, bit[0], bit[1]] + z2r[u, g].astype(F32)
            zfull[u, g, bit[0], bit[1]] = total
            for k in range(pairs):
                z3s[u, k, g] = total[k].astype(BF16)

        @pl.loop(1, pairs)
        def _(k):
            z3_copy(u, k).start()

    def pair_finish(u):
        z3_both(u).wait_recv()
        for g in range(2):
            total = zfull[u, g, bit[0], bit[1], pair]
            for k in range(1, pairs):
                total += z3r[u, (pair + k) % pairs, g].astype(F32)
            total = total * factor
            for o in range(2):
                fz[u, o, :, g * tw:(g + 1) * tw] = total[o * pd:(o + 1) * pd]
        fz_copy(u).start()
        out[:, pair_cols(odd, u)] = fz[u, odd]

    edge = (z == 0) | (z == line - 1)

    def at(step, lag, act, also=True, count=tiles):
        t = step - lag

        @pl.when((t >= 0) & (t < count) & also)
        def _():
            act(t)

    def step(t, carry):
        at(t, LAGS[4], finish)
        at(t, 0, multiply)

        @pl.when(t + AHEAD[2] < tiles)
        def _():
            start_x(t + AHEAD[2])

        @pl.when(t + PAIR_AHEAD[2] < groups)
        def _():
            zx_copy(t + PAIR_AHEAD[2]).start()

        @pl.when((t >= DEFER) & (t < tiles))
        def _():
            start_r(t - DEFER, near)

        @pl.when(t == tiles - 1)
        def _():
            for k in range(tiles - DEFER, tiles):
                start_r(k, near)

        at(t, LAGS[0], lambda k: reduce(k, far))
        at(t, LAGS[0], forward_far, edge)
        at(t, LAGS[1], forward_far, jnp.logical_not(edge))
        at(t, LAGS[2], lambda k: reduce(k, near))
        at(t, LAGS[3], forward_near)
        at(t, PAIR_LAGS[0] - 1, lambda k: relay(2), count=1)
        at(t, PAIR_LAGS[0], lambda k: relayed(2), count=1)
        for lag, act in zip(PAIR_LAGS, (pair_multiply, pair_first, pair_second, pair_finish)):
            at(t, lag, act, count=groups)
        return carry

    lax.fori_loop(0, tiles + LAGS[4], step, 0)

    for h in range(2):
        f_all(h, 1 - bit[h]).wait_recv()
        f_all(h, bit[h]).wait_send()
        x_all(h).wait_send()
        p_copy(h).wait_send()
    p_copy(2).wait_send()
    r_all().wait_send()
    remote(xz.at[1 - odd], xz.at[1 - odd], zx_s, zx_r.at[0], row=peer[2]).wait_send()
    remote(z1s, z1r, z1_s, z1_r.at[0], row=peer[0]).wait_send()
    remote(z2s, z2r, z2_s, z2_r.at[0], row=peer[0]).wait_send()
    remote(z3s.at[:, :pairs - 1], z3r.at[:, :pairs - 1], z3_s, z3_r.at[0], row=peer[0]).wait_send()
    remote(pair_area(odd), pair_area(1 - odd), fz_s, fz_r, row=peer[2]).wait()

    @pl.loop(0, line)
    def _(a):
        last = ((z == line - 2) & (a == line - 1)) | ((z == 1) & (a == 0))

        @pl.when(last)
        def _():
            remote(acc.at[:, a], acc.at[:, a], z_s.at[a], lo_r.at[0, 0], row=peer[0]).wait_send()

        @pl.when(jnp.logical_not(last) & (a != z))
        def _():
            remote(zsend.at[:, a], zsend.at[:, a], z_s.at[a], lo_r.at[0, 0], row=peer[0]).wait_send()

    @pl.loop(1, ncol)
    def _(j):
        c_send(j).wait_send()
        for h in range(3):
            e_send(h, j).wait_send()

    all_a().wait_send()
    all_b().wait_send()


def body(descriptors, block_mask, config_of):
    n, ncol = lax.axis_size("row"), lax.axis_size("col")
    rows, width = descriptors.shape
    part = PW // ncol
    wide = -(-(part + 1) // BLOCK) * BLOCK
    bw = -(-2 * part // BLOCK) * BLOCK
    blocks = width // BLOCK
    quarter_blocks = blocks * 7 // 40
    per = next(k for k in (2, 1) if quarter_blocks % k == 0 and (blocks - 4 * quarter_blocks) % (4 * k) == 0)
    tiles = quarter_blocks // per
    tw = quarter_blocks // tiles * BLOCK
    quarter = quarter_blocks * BLOCK
    groups = (width - 4 * quarter) // (4 * tw)
    line = n // G
    pd = PW // n
    pr = -(-2 * pd // 16) * 16
    zs = line // ncol

    cfg = (n, ncol, rows, width, part, wide, bw, tiles, tw, line, pd, pr, zs, quarter, groups, 1.0 / (rows * n))
    vm = pltpu.VMEM
    dma = pltpu.SemaphoreType.DMA
    hbm = pl.BlockSpec(memory_space=pl.ANY)
    return pl.pallas_call(
        functools.partial(kernel, cfg),
        out_shape=pltpu.VMEM((pd, width), F32),
        in_specs=[hbm, hbm, hbm],
        out_specs=pl.BlockSpec(memory_space=pltpu.VMEM),
        scratch_shapes=[
            vm((1, rows), jnp.int32),
            pltpu.SMEM(block_mask.shape, jnp.int32),
            vm((rows, wide), BF16),
            vm((n * SLOT, rows), BF16),
            vm((n * SLOT, wide), BF16),
            vm((n * SLOT, wide), BF16),
            vm((n * SLOT, bw), BF16),
            vm((n * SLOT, bw), BF16),
            vm((rows, width), BF16),
            vm((2, 2, tiles, rows, tw), BF16),
            vm((tiles, 2, rows, tw), BF16),
            vm((3, 2, ncol, zs * pr, 2 * rows), BF16),
            vm((3, 2, ncol, zs * pr, 2 * rows), BF16),
            vm((2, groups, 2, rows, tw), BF16),
            vm((groups, 2, rows, tw), BF16),
            vm((groups, 2, 2, 2, line // 2, pr, tw), F32),
            vm((groups, 2, 2, line // 2, pr, tw), BF16),
            vm((groups, 2, 2, line // 2, pr, tw), BF16),
            vm((groups, 2, line // 2, pr, tw), BF16),
            vm((groups, 2, line // 2, pr, tw), BF16),
            vm((groups, line // 2, 2, pr, tw), BF16),
            vm((groups, line // 2, 2, pr, tw), BF16),
            vm((groups, 2, pd, 2 * tw), F32),
            vm((tiles, line, 2, pr, tw), F32),
            vm((tiles, 2, 2, line // 2 * pr, tw), BF16),
            vm((tiles, 2, 2, line // 2 * pr, tw), BF16),
            vm((tiles, line, 2, pr, tw), BF16),
            vm((tiles, line, 2, pr, tw), BF16),
            vm((tiles, line, 2, pr, tw), BF16),
            vm((tiles, 2, pr, tw), F32),
            vm((tiles, 2, 2, pd, tw), F32),
            dma, dma, dma, dma,
            dma((3,)), dma((3,)), dma((ncol,)), dma((ncol,)), dma((3, ncol)), dma((3, ncol)), dma((9,)),
            dma((2,)), dma((tiles,)), dma, dma((tiles, 2)), dma((line,)), dma((tiles, line)), dma((tiles, line)),
            dma((2,)), dma((2,)),
            dma, dma((groups,)), dma, dma((groups,)), dma, dma((groups,)), dma, dma((groups,)), dma, dma,
        ],
        compiler_params=pltpu.CompilerParams(
            collective_id=0, has_side_effects=True, vmem_limit_bytes=56 * 1024 * 1024),
    )(config_of[None, :], block_mask, descriptors)


def solution(mesh):
    in_specs = (P("row", "col"), P("row", "col"), P("row"))
    out_specs = P("row", "col")
    return jax.shard_map(body, mesh=mesh, in_specs=in_specs, out_specs=out_specs, check_vma=False)
```

```python
import functools

import jax
import jax.numpy as jnp
from jax import lax
from jax.experimental import pallas as pl
from jax.experimental.pallas import tpu as pltpu
from jax.sharding import PartitionSpec as P

PW = 384
CONF_DEV = 64
BLOCK = 128
G = 4
SLOT = 16
AHEAD = (2, 4, 5)
DEFER = 2
LAGS = (1, 2, 3, 3, 5)
PAIR_AHEAD = (1, 1, 2)
PAIR_LAGS = (2, 3, 4, 5)
F32 = jnp.float32
BF16 = jnp.bfloat16


def remote(src, dst, send, recv, **where):
    return pltpu.make_async_remote_copy(
        src_ref=src, dst_ref=dst, send_sem=send, recv_sem=recv,
        device_id=where, device_id_type=pl.DeviceIdType.MESH,
    )


def kernel(cfg, config_of, block_mask, x, out,
           crow, marks, pext, perm, asend, arec, bsend, brec, xraw, xm, xin, own, mate,
           xz, zin, zfull, z1s, z1r, z2s, z2r, z3s, z3r, fz,
           acc, rsend, rrec, zsend, from_low, from_high, landed, fin,
           a_s, a_r, b_s, b_r, p_s, p_r, c_s, c_r, e_s, e_r, l_s,
           x_s, x_r, r_s, r_r, z_s, lo_r, hi_r, f_s, f_r,
           zx_s, zx_r, z1_s, z1_r, z2_s, z2_r, z3_s, z3_r, fz_s, fz_r):
    n, ncol, rows, width, part, wide, bw, tiles, tw, line, pd, pr, zs, quarter, groups, factor = cfg
    side = (width - 4 * quarter) // 2
    pairs = line // 2
    half = line // 2
    r = lax.axis_index("row")
    c = lax.axis_index("col")
    z = r // G
    q = r % G
    near, far = z // half, 1 - z // half
    pair, odd = z // 2, z % 2
    bit = (q % 2, q // 2)
    peer = tuple(r + (1 - 2 * bit[h]) * (1 << h) for h in range(2)) + (r + (1 - 2 * odd) * G,)

    barrier = pltpu.get_barrier_semaphore()

    @pl.loop(1, n)
    def _(k):
        pl.semaphore_signal(barrier, inc=1, device_id={"row": (r + k) % n}, device_id_type=pl.DeviceIdType.MESH)

    @pl.loop(1, ncol)
    def _(k):
        pl.semaphore_signal(barrier, inc=1, device_id={"col": (c + k) % ncol}, device_id_type=pl.DeviceIdType.MESH)

    crow_copy = pltpu.make_async_copy(config_of, crow, l_s.at[6])
    marks_copy = pltpu.make_async_copy(block_mask, marks, l_s.at[7])
    crow_copy.start()
    marks_copy.start()
    panel_copy = pltpu.make_async_copy(x.at[:, :wide], pext, l_s.at[0])
    panel_copy.start()

    def start_of(h, b):
        return h * 2 * quarter + b * quarter

    def load(h, b, i):
        cols = pl.ds(pl.multiple_of(start_of(h, b), BLOCK), quarter)
        return pltpu.make_async_copy(x.at[:, cols], xraw.at[:, cols], l_s.at[i])

    away = [load(h, 1 - bit[h], 2 + h) for h in range(2)]
    kept = [load(h, bit[h], 4 + h) for h in range(2)]
    rest = pltpu.make_async_copy(x.at[:, 4 * quarter:], xraw.at[:, 4 * quarter:], l_s.at[8])
    for copy in away + [rest] + kept:
        copy.start()

    first = lax.broadcasted_iota(jnp.int32, (rows, rows), 0)
    second = lax.broadcasted_iota(jnp.int32, (rows, rows), 1)
    crow_copy.wait()
    ids_row = jnp.broadcast_to(crow[...], (rows, rows)).astype(F32)
    ids_col = jnp.sum(jnp.where(first == second, ids_row, 0.0), axis=1, keepdims=True).astype(jnp.int32)
    shift = CONF_DEV.bit_length() - 1
    owner = crow[...] >> shift
    before = ((ids_col >> shift) == owner) & (first < second)
    rank = jnp.sum(jnp.where(before, 1.0, 0.0), axis=0, keepdims=True)
    place = owner.astype(F32) * SLOT + rank
    slots = lax.broadcasted_iota(jnp.int32, (n * SLOT, rows), 0).astype(F32)
    perm[...] = jnp.where(slots == place, 1.0, 0.0).astype(BF16)
    label = ((ids_col & (CONF_DEV - 1)) + 1).astype(F32)
    lane = lax.broadcasted_iota(jnp.int32, (BLOCK, BLOCK), 1)
    panel_copy.wait()
    marks_copy.wait()
    for b in range(rows // BLOCK):
        span = slice(b * BLOCK, (b + 1) * BLOCK)
        for w in range(wide // BLOCK):
            cols = slice(w * BLOCK, (w + 1) * BLOCK)
            keep = marks[b, w].astype(F32) if w * BLOCK < part else 0.0
            block = pext[span, cols].astype(F32) * jnp.broadcast_to(keep, (BLOCK, BLOCK))
            if (w + 1) * BLOCK > part:
                block = jnp.where(lane + w * BLOCK < part, block, jnp.broadcast_to(label[span], (BLOCK, BLOCK)))
            pext[span, cols] = block.astype(BF16)
    asend[...] = jnp.dot(perm[...], pext[...], preferred_element_type=F32).astype(BF16)

    def mask_to(dst, base):
        for i in range(rows // BLOCK):
            span = slice(i * BLOCK, (i + 1) * BLOCK)
            for w in range(tw // BLOCK):
                keep = marks[i, base // BLOCK + w].astype(F32)
                cols = pl.ds(pl.multiple_of(base + w * BLOCK, BLOCK), BLOCK)
                dst[span, w * BLOCK:(w + 1) * BLOCK] = (
                    xraw[span, cols] * jnp.broadcast_to(keep, (BLOCK, BLOCK)).astype(BF16))

    def mask(h, b, t):
        mask_to(xm.at[h, b, t], start_of(h, b) + t * tw)

    def pair_start(b, u):
        return 4 * quarter + b * side + u * 2 * tw

    def mask_pair(b, u):
        for g in range(2):
            mask_to(xz.at[b, u, g], pair_start(b, u) + g * tw)

    def mask_away(low, high):
        @pl.loop(low, high)
        def _(t):
            for h in range(2):
                mask(h, 1 - bit[h], t)

    for copy in away:
        copy.wait()
    mask_away(0, AHEAD[0])
    pl.semaphore_wait(barrier, n - 1 + ncol - 1)

    def slot_rows(k):
        return pl.ds(pl.multiple_of(k * SLOT, SLOT), SLOT)

    def to_owner(k):
        to = (r + k) % n
        return remote(asend.at[slot_rows(to), :], arec.at[slot_rows(r), :], a_s, a_r, row=to)

    others = slice(0, (n - 1) * SLOT)

    def all_a():
        return remote(asend.at[others, :], arec.at[others, :], a_s, a_r, row=(r + 1) % n)

    def to_source(k):
        to = (r + k) % n
        return remote(bsend.at[slot_rows(to), :], brec.at[slot_rows(r), :], b_s, b_r, row=to)

    def all_b():
        return remote(bsend.at[others, :], brec.at[others, :], b_s, b_r, row=(r + 1) % n)

    def x_copy(h, t):
        return remote(xm.at[h, 1 - bit[h], t], xin.at[t, h], x_s.at[h], x_r.at[t], row=peer[h])

    def x_both(t):
        return remote(xin.at[t], xin.at[t], x_s.at[0], x_r.at[t], row=peer[0])

    def x_all(h):
        return remote(xm.at[h, 1 - bit[h]], xm.at[h, 1 - bit[h]], x_s.at[h], x_r.at[0], row=peer[h])

    def start_x(t):
        for h in range(2):
            x_copy(h, t).start()

    def zx_copy(u):
        return remote(xz.at[1 - odd, u], zin.at[u], zx_s, zx_r.at[u], row=peer[2])

    def p_copy(h):
        return remote(own.at[h, :, c], mate.at[h, :, c], p_s.at[h], p_r.at[h], row=peer[h])

    def c_send(j):
        to = (c + j) % ncol
        return remote(own.at[:, :, c], own.at[:, :, c], c_s.at[j], c_r.at[c], col=to)

    def c_from(j):
        to = (c + j) % ncol
        return remote(own.at[:, :, c], own.at[:, :, to], c_s.at[j], c_r.at[to], col=to)

    def e_send(h, j):
        to = (c + j) % ncol
        return remote(mate.at[h, :, c], mate.at[h, :, c], e_s.at[h, j], e_r.at[h, c], col=to)

    def e_from(h, j):
        to = (c + j) % ncol
        return remote(mate.at[h, :, c], mate.at[h, :, to], e_s.at[h, j], e_r.at[h, to], col=to)

    own_a = pltpu.make_async_copy(asend.at[slot_rows(r), :], arec.at[slot_rows(r), :], l_s.at[0])
    own_a.start()

    @pl.loop(1, n)
    def _(k):
        to_owner(k).start()

    for t in range(AHEAD[0]):
        start_x(t)
    rest.wait()
    for u in range(groups):
        mask_pair(1 - odd, u)
    for u in range(min(PAIR_AHEAD[0], groups)):
        zx_copy(u).start()
    mask_away(AHEAD[0], tiles)

    own_a.wait()
    all_a().wait_recv()

    arrived = arec[...]
    label = arrived[:, part:part + 1].astype(F32)
    ids = lax.broadcasted_iota(jnp.int32, (n * SLOT, BLOCK), 1).astype(F32) + 1.0
    member = jnp.where((label == ids) & (ids <= CONF_DEV), 1.0, 0.0).astype(BF16)
    same = lax.dot_general(member, member, (((1,), (1,)), ((), ())), preferred_element_type=F32)
    counts = jnp.maximum(jnp.sum(same, axis=1, keepdims=True), 1.0)
    same = same.astype(BF16)
    means = jnp.dot(same, arrived, preferred_element_type=F32) / counts
    high = (arrived.astype(F32) - means).astype(BF16)
    low = -(jnp.dot(same, high, preferred_element_type=F32) / counts)
    both = [high.astype(F32)[:, :part], low[:, :part]]
    if bw > 2 * part:
        both.append(jnp.zeros((n * SLOT, bw - 2 * part), F32))
    bsend[...] = jnp.concatenate(both, axis=1).astype(BF16)

    own_b = pltpu.make_async_copy(bsend.at[slot_rows(r), :], brec.at[slot_rows(r), :], l_s.at[1])
    own_b.start()

    @pl.loop(1, n)
    def _(k):
        to_source(k).start()

    for t in range(AHEAD[0], AHEAD[1]):
        start_x(t)
    for u in range(min(PAIR_AHEAD[0], groups), min(PAIR_AHEAD[1], groups)):
        zx_copy(u).start()
    for u in range(groups):
        mask_pair(odd, u)
    for copy in kept:
        copy.wait()

    @pl.loop(0, tiles)
    def _(t):
        for h in range(2):
            mask(h, bit[h], t)

    own_b.wait()
    all_b().wait_recv()

    back = lax.dot_general(brec[...], perm[...], (((0,), (0,)), ((), ())), preferred_element_type=F32)
    for h in range(3):
        for b in range(2):
            for s in range(zs):
                for i in range(2):
                    pieces = []
                    for o in range(2):
                        if h == 2:
                            at = i * part + ((s // 2 * 2 + o) * G + 2 * (s % 2) + b) * pd
                        else:
                            at = i * part + (s * G + (2 * b + o if h == 0 else 2 * o + b)) * pd
                        pieces.append(back[at:at + pd])
                    if pr > 2 * pd:
                        pieces.append(jnp.zeros((pr - 2 * pd, rows), F32))
                    own[h, b, c, s * pr:(s + 1) * pr, i * rows:(i + 1) * rows] = (
                        jnp.concatenate(pieces, axis=0).astype(BF16))
    for h in range(3):
        p_copy(h).start()

    @pl.loop(1, ncol)
    def _(j):
        c_send(j).start()

    for t in range(AHEAD[1], AHEAD[2]):
        start_x(t)
    for u in range(min(PAIR_AHEAD[1], groups), min(PAIR_AHEAD[2], groups)):
        zx_copy(u).start()

    def relay(h):
        p_copy(h).wait_recv()

        @pl.loop(1, ncol)
        def _(j):
            e_send(h, j).start()

    def relayed(h):
        @pl.loop(1, ncol)
        def _(j):
            e_from(h, j).wait_recv()

    for h in range(2):
        relay(h)

    @pl.loop(1, ncol)
    def _(j):
        c_from(j).wait_recv()

    for h in range(2):
        relayed(h)

    def r_copy(h, t, k):
        return remote(rsend.at[t, k, h], rrec.at[t, k, h], r_s, r_r.at[t, k], row=peer[1 - h])

    def r_both(t, k):
        return remote(rrec.at[t, k], rrec.at[t, k], r_s, r_r.at[t, k], row=peer[0])

    def r_all():
        return remote(rsend, rrec, r_s, r_r.at[0, 0], row=peer[0])

    def start_r(t, k):
        for h in range(2):
            r_copy(h, t, k).start()

    def product(h, b, mine, theirs):
        ours = own[h, b].reshape(line * pr, 2 * rows)
        other = mate[h, b].reshape(line * pr, 2 * rows)
        left = jnp.concatenate([ours, other], axis=1)
        right = jnp.concatenate([mine, mine, theirs, theirs], axis=0)
        return jnp.dot(left, right, preferred_element_type=F32)

    def multiply(t):
        x_both(t).wait_recv()

        def of(h, b):
            return product(h, b, xm[h, bit[h], t], xin[t, h])

        for h in range(2):
            total = of(h, 1 - bit[1 - h]).astype(BF16)
            for k in range(2):
                rsend[t, k, h] = total[k * half * pr:(k + 1) * half * pr]
            r_copy(h, t, far).start()
        for h in range(2):
            total = of(h, bit[1 - h])
            for a in range(line):
                acc[t, a, h] = total[a * pr:(a + 1) * pr]

    def reduce(t, k):
        r_both(t, k).wait_recv()
        for h in range(2):
            for i in range(half):
                acc[t, k * half + i, h] += rrec[t, k, h, i * pr:(i + 1) * pr].astype(F32)

    def up(t, a):
        return remote(zsend.at[t, a], from_low.at[t, a], z_s.at[a], lo_r.at[t, a], row=(r + G) % n)

    def down(t, a):
        return remote(zsend.at[t, a], from_high.at[t, a], z_s.at[a], hi_r.at[t, a], row=(r + n - G) % n)

    def up_last(t):
        return remote(acc.at[t, line - 1], landed.at[t], z_s.at[line - 1], lo_r.at[t, line - 1], row=(r + G) % n)

    def down_last(t):
        return remote(acc.at[t, 0], landed.at[t], z_s.at[0], hi_r.at[t, 0], row=(r + n - G) % n)

    def either(pred, yes, no):
        pl.when(pred)(yes)
        pl.when(jnp.logical_not(pred))(no)

    def take_up(t, a):
        def last():
            up_last(t).wait_recv()
            acc[t, a] += landed[t]

        def other():
            up(t, a).wait_recv()
            acc[t, a] += from_low[t, a].astype(F32)

        @pl.when(z > 0)
        def _():
            either(z == line - 1, last, other)

    def take_down(t, a):
        def last():
            down_last(t).wait_recv()
            acc[t, a] += landed[t]

        def other():
            down(t, a).wait_recv()
            acc[t, a] += from_high[t, a].astype(F32)

        @pl.when(z < line - 1)
        def _():
            either(z == 0, last, other)

    def go_up(t, a):
        take_up(t, a)

        def other():
            zsend[t, a] = acc[t, a].astype(BF16)
            up(t, a).start()

        either(z == line - 2, lambda: up_last(t).start(), other)

    def go_down(t, a):
        take_down(t, a)

        def other():
            zsend[t, a] = acc[t, a].astype(BF16)
            down(t, a).start()

        either(z == 1, lambda: down_last(t).start(), other)

    def forward_far(t):
        @pl.loop(0, half)
        def _(i):
            either(z < half, lambda: go_up(t, line - 1 - i), lambda: go_down(t, i))

    def forward_near(t):
        last = (near + 1) * half - 1

        @pl.loop(0, last - z)
        def _(i):
            go_up(t, last - i)

        @pl.loop(near * half, z)
        def _(a):
            go_down(t, a)

    def cols_of(h, b, t):
        return pl.ds(pl.multiple_of(start_of(h, b) + t * tw, BLOCK), tw)

    def f_copy(h, t):
        return remote(fin.at[t, h, 1 - bit[h]], out.at[:, cols_of(h, bit[h], t)],
                      f_s.at[h], f_r.at[h], row=peer[h])

    def f_all(h, b):
        area = out.at[:, pl.ds(pl.multiple_of(start_of(h, b), BLOCK), quarter)]
        return remote(area, area, f_s.at[h], f_r.at[h], row=peer[h])

    def finish(t):
        take_up(t, z)
        take_down(t, z)
        for h in range(2):
            total = acc[t, z, h] * factor
            for o in range(2):
                fin[t, h, o] = total[o * pd:(o + 1) * pd]
            f_copy(h, t).start()
            out[:, cols_of(h, bit[h], t)] = fin[t, h, bit[h]]

    def z1_copy(u, g):
        return remote(z1s.at[u, g], z1r.at[u, g], z1_s, z1_r.at[u], row=peer[g])

    def z2_copy(u, g):
        return remote(z2s.at[u, g], z2r.at[u, g], z2_s, z2_r.at[u], row=peer[1 - g])

    def z3_copy(u, k):
        to = (pair + k) % pairs
        return remote(z3s.at[u, to], z3r.at[u, pair], z3_s, z3_r.at[u], row=(2 * to + odd) * G + q)

    def z3_both(u):
        return remote(z3r.at[u, :pairs - 1], z3r.at[u, :pairs - 1], z3_s, z3_r.at[u], row=peer[0])

    def pair_cols(b, u):
        return pl.ds(pl.multiple_of(pair_start(b, u), BLOCK), 2 * tw)

    def fz_copy(u):
        return remote(fz.at[u, 1 - odd], out.at[:, pair_cols(odd, u)], fz_s, fz_r, row=peer[2])

    def pair_area(b):
        return out.at[:, pl.ds(pl.multiple_of(pair_start(b, 0), BLOCK), side)]

    def pair_multiply(u):
        zx_copy(u).wait_recv()
        for g in range(2):
            for b in range(2):
                total = product(2, b, xz[odd, u, g], zin[u, g])
                for k in range(pairs):
                    for i in range(2):
                        at = (2 * k + i) * pr
                        zfull[u, g, b, i, k] = total[at:at + pr]
            for i in range(2):
                z1s[u, g, i] = (zfull[u, 0, 1 - bit[0], i] if g == 0 else zfull[u, 1, i, 1 - bit[1]]).astype(BF16)
            z1_copy(u, g).start()

    def pair_first(u):
        remote(z1r.at[u], z1r.at[u], z1_s, z1_r.at[u], row=peer[0]).wait_recv()
        for i in range(2):
            zfull[u, 0, bit[0], i] += z1r[u, 0, i].astype(F32)
            zfull[u, 1, i, bit[1]] += z1r[u, 1, i].astype(F32)
        z2s[u, 0] = zfull[u, 0, bit[0], 1 - bit[1]].astype(BF16)
        z2s[u, 1] = zfull[u, 1, 1 - bit[0], bit[1]].astype(BF16)
        for g in range(2):
            z2_copy(u, g).start()

    def pair_second(u):
        remote(z2r.at[u], z2r.at[u], z2_s, z2_r.at[u], row=peer[0]).wait_recv()
        for g in range(2):
            total = zfull[u, g, bit[0], bit[1]] + z2r[u, g].astype(F32)
            zfull[u, g, bit[0], bit[1]] = total
            for k in range(pairs):
                z3s[u, k, g] = total[k].astype(BF16)

        @pl.loop(1, pairs)
        def _(k):
            z3_copy(u, k).start()

    def pair_finish(u):
        z3_both(u).wait_recv()
        for g in range(2):
            total = zfull[u, g, bit[0], bit[1], pair]
            for k in range(1, pairs):
                total += z3r[u, (pair + k) % pairs, g].astype(F32)
            total = total * factor
            for o in range(2):
                fz[u, o, :, g * tw:(g + 1) * tw] = total[o * pd:(o + 1) * pd]
        fz_copy(u).start()
        out[:, pair_cols(odd, u)] = fz[u, odd]

    edge = (z == 0) | (z == line - 1)

    def at(step, lag, act, also=True, count=tiles):
        t = step - lag

        @pl.when((t >= 0) & (t < count) & also)
        def _():
            act(t)

    def step(t, carry):
        at(t, LAGS[4], finish)
        at(t, 0, multiply)

        @pl.when(t + AHEAD[2] < tiles)
        def _():
            start_x(t + AHEAD[2])

        @pl.when(t + PAIR_AHEAD[2] < groups)
        def _():
            zx_copy(t + PAIR_AHEAD[2]).start()

        @pl.when((t >= DEFER) & (t < tiles))
        def _():
            start_r(t - DEFER, near)

        @pl.when(t == tiles - 1)
        def _():
            for k in range(tiles - DEFER, tiles):
                start_r(k, near)

        at(t, LAGS[0], lambda k: reduce(k, far))
        at(t, LAGS[0], forward_far, edge)
        at(t, LAGS[1], forward_far, jnp.logical_not(edge))
        at(t, LAGS[2], lambda k: reduce(k, near))
        at(t, LAGS[3], forward_near)
        at(t, PAIR_LAGS[0] - 1, lambda k: relay(2), count=1)
        at(t, PAIR_LAGS[0], lambda k: relayed(2), count=1)
        for lag, act in zip(PAIR_LAGS, (pair_multiply, pair_first, pair_second, pair_finish)):
            at(t, lag, act, count=groups)
        return carry

    lax.fori_loop(0, tiles + LAGS[4], step, 0)

    for h in range(2):
        f_all(h, 1 - bit[h]).wait_recv()
        f_all(h, bit[h]).wait_send()
        x_all(h).wait_send()
        p_copy(h).wait_send()
    p_copy(2).wait_send()
    r_all().wait_send()
    remote(xz.at[1 - odd], xz.at[1 - odd], zx_s, zx_r.at[0], row=peer[2]).wait_send()
    remote(z1s, z1r, z1_s, z1_r.at[0], row=peer[0]).wait_send()
    remote(z2s, z2r, z2_s, z2_r.at[0], row=peer[0]).wait_send()
    remote(z3s.at[:, :pairs - 1], z3r.at[:, :pairs - 1], z3_s, z3_r.at[0], row=peer[0]).wait_send()
    remote(pair_area(odd), pair_area(1 - odd), fz_s, fz_r, row=peer[2]).wait()

    @pl.loop(0, line)
    def _(a):
        last = ((z == line - 2) & (a == line - 1)) | ((z == 1) & (a == 0))

        @pl.when(last)
        def _():
            remote(acc.at[:, a], acc.at[:, a], z_s.at[a], lo_r.at[0, 0], row=peer[0]).wait_send()

        @pl.when(jnp.logical_not(last) & (a != z))
        def _():
            remote(zsend.at[:, a], zsend.at[:, a], z_s.at[a], lo_r.at[0, 0], row=peer[0]).wait_send()

    @pl.loop(1, ncol)
    def _(j):
        c_send(j).wait_send()
        for h in range(3):
            e_send(h, j).wait_send()

    all_a().wait_send()
    all_b().wait_send()


def body(descriptors, block_mask, config_of):
    n, ncol = lax.axis_size("row"), lax.axis_size("col")
    rows, width = descriptors.shape
    part = PW // ncol
    wide = -(-(part + 1) // BLOCK) * BLOCK
    bw = -(-2 * part // BLOCK) * BLOCK
    blocks = width // BLOCK
    quarter_blocks = blocks * 7 // 40
    per = next(k for k in (2, 1) if quarter_blocks % k == 0 and (blocks - 4 * quarter_blocks) % (4 * k) == 0)
    tiles = quarter_blocks // per
    tw = quarter_blocks // tiles * BLOCK
    quarter = quarter_blocks * BLOCK
    groups = (width - 4 * quarter) // (4 * tw)
    line = n // G
    pd = PW // n
    pr = -(-2 * pd // 16) * 16
    zs = line // ncol

    cfg = (n, ncol, rows, width, part, wide, bw, tiles, tw, line, pd, pr, zs, quarter, groups, 1.0 / (rows * n))
    vm = pltpu.VMEM
    dma = pltpu.SemaphoreType.DMA
    hbm = pl.BlockSpec(memory_space=pl.ANY)
    return pl.pallas_call(
        functools.partial(kernel, cfg),
        out_shape=pltpu.VMEM((pd, width), F32),
        in_specs=[hbm, hbm, hbm],
        out_specs=pl.BlockSpec(memory_space=pltpu.VMEM),
        scratch_shapes=[
            vm((1, rows), jnp.int32),
            pltpu.SMEM(block_mask.shape, jnp.int32),
            vm((rows, wide), BF16),
            vm((n * SLOT, rows), BF16),
            vm((n * SLOT, wide), BF16),
            vm((n * SLOT, wide), BF16),
            vm((n * SLOT, bw), BF16),
            vm((n * SLOT, bw), BF16),
            vm((rows, width), BF16),
            vm((2, 2, tiles, rows, tw), BF16),
            vm((tiles, 2, rows, tw), BF16),
            vm((3, 2, ncol, zs * pr, 2 * rows), BF16),
            vm((3, 2, ncol, zs * pr, 2 * rows), BF16),
            vm((2, groups, 2, rows, tw), BF16),
            vm((groups, 2, rows, tw), BF16),
            vm((groups, 2, 2, 2, line // 2, pr, tw), F32),
            vm((groups, 2, 2, line // 2, pr, tw), BF16),
            vm((groups, 2, 2, line // 2, pr, tw), BF16),
            vm((groups, 2, line // 2, pr, tw), BF16),
            vm((groups, 2, line // 2, pr, tw), BF16),
            vm((groups, line // 2, 2, pr, tw), BF16),
            vm((groups, line // 2, 2, pr, tw), BF16),
            vm((groups, 2, pd, 2 * tw), F32),
            vm((tiles, line, 2, pr, tw), F32),
            vm((tiles, 2, 2, line // 2 * pr, tw), BF16),
            vm((tiles, 2, 2, line // 2 * pr, tw), BF16),
            vm((tiles, line, 2, pr, tw), BF16),
            vm((tiles, line, 2, pr, tw), BF16),
            vm((tiles, line, 2, pr, tw), BF16),
            vm((tiles, 2, pr, tw), F32),
            vm((tiles, 2, 2, pd, tw), F32),
            dma, dma, dma, dma,
            dma((3,)), dma((3,)), dma((ncol,)), dma((ncol,)), dma((3, ncol)), dma((3, ncol)), dma((9,)),
            dma((2,)), dma((tiles,)), dma, dma((tiles, 2)), dma((line,)), dma((tiles, line)), dma((tiles, line)),
            dma((2,)), dma((2,)),
            dma, dma((groups,)), dma, dma((groups,)), dma, dma((groups,)), dma, dma((groups,)), dma, dma,
        ],
        compiler_params=pltpu.CompilerParams(
            collective_id=0, has_side_effects=True, vmem_limit_bytes=56 * 1024 * 1024),
    )(config_of[None, :], block_mask, descriptors)


def solution(mesh):
    in_specs = (P("row", "col"), P("row", "col"), P("row"))
    out_specs = P("row", "col")
    return jax.shard_map(body, mesh=mesh, in_specs=in_specs, out_specs=out_specs, check_vma=False)
```
